256 devices in a mesh: row: 32 (over x_lo, z, core), feat: 8 (over x_hi, y).
Axes of the slice: x: 4 (x_hi: 2, x_lo: 2; x = x_hi * 2 + x_lo), y: 4, z: 8, core: 2. Of those that a mesh axis runs over, the one named last changes fastest.
Arguments:
- features: bfloat16 [8192, 1024], P('row', 'feat'), may hold values from -6 to 6
- weight: bfloat16 [1024, 1024], P('feat'), may hold values from -0.1875 to 0.1875
- bias_vector: bfloat16 [1024], P('feat'), may hold values from -3 to 3
- adj_tiles: bfloat16 [2048, 128, 128], P('row'), may hold values from -0.09375 to 0.09375
- col_blocks: int32 [2048], P('row'), may hold values from 0 to 63, as said below
- dest_blocks: int32 [2048], P('row'), may hold values from 0 to 1
- out_grad: bfloat16 [8192, 1024], P('row', 'feat'), may hold values from -6 to 6
Outputs:
- hidden: float32 [8192, 1024], P('row', 'feat')
- input_grad: float32 [8192, 1024], P('row', 'feat')
- weight_grad: float32 [1024, 1024], P('feat')
- bias_grad: float32 [1024], P('feat')
The draws below stay inside these ranges and needn't reach their ends.
Inputs may be any that keep to these rules, and one draw needn't show every extreme that they name: Within the 64 entries of one index r of row, col_blocks // 2 never falls from one entry to the next and is never r; at most 4 of them lie in any one index's range of 2 blocks, and exactly 4 lie in the range of index (r + 1) mod 32.
All inputs are finite; a program needn't handle non-finite values.
Results may differ from the reference program's by a relative error of at most 0.0055.
Values may be sent and summed in bfloat16 or wider, within the bound.
No kernel may reach another device: no remote copies, remote signals or barrier semaphores. Data moves between devices by JAX's collectives and lax.ppermute only.
A program may use at most 64 MiB of HBM per device.

```python
import jax
import jax.numpy as jnp
from jax import lax

D = 1024
BLOCK = 128
NB = 2
TPB = 32
TILE_DEV = 64
CAP = 4
NBLK = 64
NODES = 8192
TILES = 2048


def draw_col_blocks(key, part):
    shards = TILES // TILE_DEV

    def one_device(device):
        device_key = jax.random.fold_in(key, device)
        first_key = jax.random.fold_in(device_key, 11)
        second_key = jax.random.fold_in(device_key, 23)
        slots = jnp.arange(shards * CAP, dtype=jnp.int32)
        slot_shard = slots // CAP
        priority = jax.random.permutation(first_key, shards * CAP).astype(jnp.int32)
        priority = jnp.where(slot_shard == device, shards * CAP + 1, priority)
        priority = jnp.where(slot_shard == (device + 1) % shards, -1, priority)
        ranked = jnp.argsort(priority, stable=True)[:TILE_DEV]
        chosen = jnp.sort(ranked // CAP)
        within = jax.random.randint(second_key, (TILE_DEV,), 0, NB)
        return (chosen * NB + within).astype(jnp.int32)
    return jax.vmap(one_device)(jnp.arange(shards, dtype=jnp.int32)).reshape(-1).astype(jnp.int32)


def place_ends(entries, own_key, low, top_value):
    spot = [jax.random.randint(jax.random.fold_in(own_key, axis), (), 0, length) for axis, length in enumerate(entries.shape)]
    main_axis = entries.shape.index(max(entries.shape))
    next_to = spot[:main_axis] + [(spot[main_axis] + 1) % entries.shape[main_axis]] + spot[main_axis + 1:]
    return entries.at[tuple(spot)].set(low).at[tuple(next_to)].set(top_value)


def block_scale(key, shape, cuts, smallest, high):
    def one(position, shards_of):
        draws = jax.random.uniform(jax.random.fold_in(jax.random.fold_in(key, 6), position), (shards_of,), jnp.float32, smallest / len(cuts), high / len(cuts))
        return jnp.repeat(jnp.exp(draws), shape[position] // shards_of).reshape((-1,) + (1,) * (len(shape) - position - 1))

    level = one(*cuts[0])
    for cut in cuts[1:]:
        level = level * one(*cut)
    return level


def noise(own_key, shape, deviation, limit, cuts=(), kind=jnp.bfloat16):
    loudness = block_scale(own_key, shape, cuts, -0.22, 0.18) if cuts else 1.0
    result = jax.random.normal(own_key, shape, jnp.float32) * deviation * loudness
    return jnp.minimum(jnp.maximum(result, -limit), limit).astype(kind)


def setup_inputs(seed: int = 0) -> dict:
    arg_keys = jax.random.split(jax.random.key(seed), 8)
    features = noise(arg_keys[0], (NODES, D), 1.0, 6.0, ((0, 32), (1, 8)))
    weight = noise(arg_keys[1], (D, D), D ** -0.5, 0.1875, ((0, 8),))
    bias_vector = noise(arg_keys[2], (D,), 0.5, 3.0, ((0, 8),))
    adj_tiles = noise(arg_keys[3], (TILES, BLOCK, BLOCK), (TPB * BLOCK) ** -0.5, 0.09375, ((0, 32),))
    col_blocks = draw_col_blocks(jax.random.fold_in(arg_keys[7], 71), 0)
    dest_blocks = place_ends(jax.random.randint(arg_keys[5], (TILES,), 0, NB), jax.random.fold_in(arg_keys[5], 1), 0, NB - 1).astype(jnp.int32)
    out_grad = noise(arg_keys[6], (NODES, D), 1.0, 6.0, ((0, 32), (1, 8)))
    return {"features": features, "weight": weight, "bias_vector": bias_vector, "adj_tiles": adj_tiles, "col_blocks": col_blocks, "dest_blocks": dest_blocks, "out_grad": out_grad}


def reference(features, weight, bias_vector, adj_tiles, col_blocks, dest_blocks, out_grad):
    device_count = TILES // TILE_DEV
    source_blocks = features.reshape(NBLK, BLOCK, D)
    tile_sets = adj_tiles.reshape(device_count, TILE_DEV, BLOCK, BLOCK)
    col_sets = col_blocks.reshape(device_count, TILE_DEV)
    dest_sets = dest_blocks.reshape(device_count, TILE_DEV)

    def aggregate(inputs):
        tile_set, col_set, dest_set = inputs
        gathered = source_blocks[col_set].astype(jnp.float32)
        contrib = jnp.einsum("tij,tjd->tid", tile_set.astype(jnp.float32), gathered)
        return jax.ops.segment_sum(contrib, dest_set, num_segments=NB)

    aggregated = lax.map(aggregate, (tile_sets, col_sets, dest_sets)).reshape(NODES, D).astype(jnp.bfloat16)
    preact = jnp.dot(aggregated, weight, preferred_element_type=jnp.float32) + bias_vector.astype(jnp.float32)
    hidden = jax.nn.silu(preact)
    sigmoid_z = jax.nn.sigmoid(preact)
    grad_pre = (out_grad.astype(jnp.float32) * sigmoid_z * (1.0 + preact * (1.0 - sigmoid_z))).astype(jnp.bfloat16)
    grad_scale = float(NODES) ** -0.5
    weight_grad = jnp.dot(aggregated.T, grad_pre, preferred_element_type=jnp.float32) * grad_scale
    bias_grad = jnp.sum(grad_pre.astype(jnp.float32), axis=0) * grad_scale
    prop_grad = jnp.dot(grad_pre, weight.T, preferred_element_type=jnp.float32).astype(jnp.bfloat16)
    prop_blocks = prop_grad.reshape(device_count, NB, BLOCK, D)

    def spread(running, inputs):
        tile_set, col_set, dest_set, local_prop = inputs
        gathered = local_prop[dest_set].astype(jnp.float32)
        contrib = jnp.einsum("tij,tid->tjd", tile_set.astype(jnp.float32), gathered)
        return running + jax.ops.segment_sum(contrib, col_set, num_segments=NBLK), None

    start_sum = jnp.zeros((NBLK, BLOCK, D), jnp.float32)
    spread_sum, unused = lax.scan(spread, start_sum, (tile_sets, col_sets, dest_sets, prop_blocks))
    input_grad = spread_sum.reshape(NODES, D)
    return (hidden, input_grad, weight_grad, bias_grad)
```

```python
import functools

import jax
import jax.numpy as jnp
from jax import lax
from jax.experimental import pallas as pl
from jax.experimental.pallas import tpu as pltpu
from jax.sharding import PartitionSpec as P

bf16 = jnp.bfloat16
f32 = jnp.float32
B = 128
NZ = 8
VM = pl.BlockSpec(memory_space=pltpu.VMEM)
SM = pl.BlockSpec(memory_space=pltpu.SMEM)


def row_send(v, dx=0, dz=0, dc=0):
    perm = []
    for i in range(32):
        x, z, c = i >> 4, (i >> 1) & 7, i & 1
        perm.append((i, ((x ^ dx) << 4) | (((z + dz) % NZ) << 1) | (c ^ dc)))
    return lax.ppermute(v, "row", perm)


def feat_send(v, dx=0, dy=0):
    return lax.ppermute(v, "feat", [(i, (((i >> 2) ^ dx) << 2) | ((i + dy) & 3)) for i in range(8)])


def params(mib=48):
    return pltpu.CompilerParams(vmem_limit_bytes=mib << 20)


def cost(flops, nbytes):
    return pl.CostEstimate(flops=flops, bytes_accessed=nbytes, transcendentals=0)


def agg_body(idx, dest, tiles, near, far, out):
    group = 4

    def step(g, acc):
        lhs, rhs = [], []
        for u in range(group):
            t = g * group + u
            a = tiles[t]
            zero = jnp.zeros_like(a)
            d = dest[t]
            lhs.append(jnp.concatenate([jnp.where(d == 0, a, zero), jnp.where(d == 1, a, zero)], axis=0))
            i = idx[t]
            j = i & 31
            rhs.append(jnp.where(i < 32, near[j], far[j]))
        return acc + jnp.dot(
            jnp.concatenate(lhs, axis=1), jnp.concatenate(rhs, axis=0), preferred_element_type=f32
        )

    acc = lax.fori_loop(0, 64 // group, step, jnp.zeros((2 * B, B), f32))
    out[...] = acc.astype(bf16)


def aggregate(idx, dest, tiles, near, far):
    return pl.pallas_call(
        agg_body,
        out_shape=jax.ShapeDtypeStruct((2 * B, B), bf16),
        in_specs=[SM, SM, VM, VM, VM],
        out_specs=VM,
        compiler_params=params(),
        cost_estimate=cost(2 * 64 * B**3, 4 << 20),
        name="aggregate",
    )(idx, dest, tiles, near, far)


def lay_body(who, *refs):
    own, other = refs[0:4], refs[4:8]
    w_out, og_out, bias_out = refs[8:11]
    core = who[0]
    for j in range(4):
        for i in range(2):
            k = j * 2 + i
            base = i * 784
            col = pl.multiple_of(who[1 + k] * B, B)
            for src, c in ((own[j], core), (other[j], 1 - core)):
                for m in range(4):
                    at = pl.multiple_of(c * 512 + m * B, B)
                    w_out[pl.ds(k * B, B), pl.ds(at, B)] = src[pl.ds(base + m * B, B), :]
            og_out[:, pl.ds(col, B)] = own[j][pl.ds(base + 512, 256), :]
            bias_out[:, pl.ds(col, B)] = own[j][pl.ds(base + 768, 16), :].astype(f32)[0:8]


def lay_out(who, own, other):
    return pl.pallas_call(
        lay_body,
        out_shape=(
            jax.ShapeDtypeStruct((1024, 1024), bf16),
            jax.ShapeDtypeStruct((256, 1024), bf16),
            jax.ShapeDtypeStruct((8, 1024), f32),
        ),
        in_specs=[SM] + [VM] * 8,
        out_specs=(VM, VM, VM),
        compiler_params=params(),
        cost_estimate=cost(0, 5 << 20),
        name="lay_out",
    )(who, *own, *other)


def mid_body(who, p0, p1, p2, p3, w_full, og, bias, w_own, hidden, prop, wpart, agg, pre, gp):
    for j, p in enumerate((p0, p1, p2, p3)):
        for i in range(2):
            agg[:, (j * 2 + i) * B : (j * 2 + i + 1) * B] = p[i * 256 : (i + 1) * 256, :]
    for n in range(4):
        cols = slice(n * 256, (n + 1) * 256)
        v = jnp.dot(agg[...], w_full[:, cols], preferred_element_type=f32) + bias[0:1, cols]
        pre[:, cols] = v
        s = jax.nn.sigmoid(v)
        gp[:, cols] = (og[:, cols].astype(f32) * s * (1.0 + v * (1.0 - s))).astype(bf16)
    mine = pl.ds(pl.multiple_of(who[0] * B, B), B)
    v = pre[:, mine]
    hidden[...] = v * jax.nn.sigmoid(v)
    prop[...] = lax.dot_general(
        gp[...], w_own[...], (((1,), (1,)), ((), ())), preferred_element_type=f32
    ).astype(bf16)
    wpart[:, 0:1024] = lax.dot_general(
        agg[:, 0:B], gp[...], (((0,), (0,)), ((), ())), preferred_element_type=f32
    )
    total = jnp.sum(gp[:, mine].astype(f32), axis=0, keepdims=True)
    wpart[:, 1024:1152] = jnp.broadcast_to(total, (B, B))


def middle(feat, pieces, w_full, og, bias, w_own):
    return pl.pallas_call(
        mid_body,
        out_shape=(
            jax.ShapeDtypeStruct((256, B), f32),
            jax.ShapeDtypeStruct((256, B), bf16),
            jax.ShapeDtypeStruct((B, 1152), f32),
        ),
        in_specs=[SM] + [VM] * 8,
        out_specs=(VM, VM, VM),
        scratch_shapes=[
            pltpu.VMEM((256, 1024), bf16),
            pltpu.VMEM((256, 1024), f32),
            pltpu.VMEM((256, 1024), bf16),
        ],
        compiler_params=params(),
        cost_estimate=cost(2 * 256 * 1024 * 1280, 5 << 20),
        name="middle",
    )(feat, *pieces, w_full, og, bias, w_own)


def spread_body(idx, dest, tiles, prop, mine, other, acc):
    acc[...] = jnp.zeros_like(acc)

    def step(g, carry):
        for u in range(4):
            t = g * 4 + u
            i = idx[t]
            acc[i] += lax.dot_general(
                tiles[t], prop[dest[t]], (((0,), (0,)), ((), ())), preferred_element_type=f32
            )
        return carry

    lax.fori_loop(0, 16, step, 0)
    mine[...] = acc[0:32]
    other[...] = acc[32:64].astype(bf16)


def spread(idx, dest, tiles, prop):
    return pl.pallas_call(
        spread_body,
        out_shape=(
            jax.ShapeDtypeStruct((32, B, B), f32),
            jax.ShapeDtypeStruct((32, B, B), bf16),
        ),
        in_specs=[SM, SM, VM, VM],
        out_specs=(VM, VM),
        scratch_shapes=[pltpu.VMEM((64, B, B), f32)],
        compiler_params=params(),
        cost_estimate=cost(2 * 64 * B**3, 6 << 20),
        name="spread",
    )(idx, dest, tiles, prop)


def body(features, weight, bias_vector, adj_tiles, col_blocks, dest_blocks, out_grad):
    me = lax.axis_index("row")
    my_x, my_z, my_c = me >> 4, (me >> 1) & 7, me & 1
    ft = lax.axis_index("feat")
    owner = col_blocks >> 1
    ox, oz, oc = owner >> 4, (owner >> 1) & 7, owner & 1
    idx = ((((oc ^ my_c) * NZ + ((oz - my_z) & 7)) * 2 + (ox ^ my_x)) * 2) + (col_blocks & 1)

    half = lax.dynamic_slice(weight, (0, my_c * 512), (B, 512))
    pack = jnp.concatenate(
        [half[:, m * B : (m + 1) * B] for m in range(4)]
        + [out_grad, jnp.broadcast_to(bias_vector[None, :], (16, B))],
        axis=0,
    )
    pair = jnp.concatenate([pack, feat_send(pack, dx=1)], axis=0)
    own = (pair, feat_send(pair, dy=1), feat_send(pair, dy=-1), feat_send(pair, dy=2))
    other = tuple(row_send(p, dc=1) for p in own)
    yy, xx = ft & 3, ft >> 2
    at = [((xx ^ i) << 2) | ((yy + off) & 3) for off in (0, -1, 1, 2) for i in range(2)]
    who = jnp.stack([my_c] + at).astype(jnp.int32)
    w_full, og, bias = lay_out(who, own, other)

    b = jnp.concatenate([features, row_send(features, dx=1)], axis=0)
    got = {0: b}
    up = down = b
    for s in range(1, 5):
        up = row_send(up, dz=1)
        got[NZ - s] = up
        if s < 4:
            down = row_send(down, dz=-1)
            got[s] = down
    near = jnp.concatenate([got[k] for k in range(NZ)], axis=0)
    far = row_send(near, dc=1)
    near, far = near.reshape(32, B, B), far.reshape(32, B, B)

    aggregated = aggregate(idx, dest_blocks, adj_tiles, near, far)

    q = jnp.concatenate([aggregated, feat_send(aggregated, dx=1)], axis=0)
    pieces = (q, feat_send(q, dy=1), feat_send(q, dy=-1), feat_send(q, dy=2))
    hidden, prop, wpart = middle(ft[None].astype(jnp.int32), pieces, w_full, og, bias, weight)

    keep = lax.dynamic_slice(wpart, (my_c * 64, 0), (64, 1152))
    give = lax.dynamic_slice(wpart, ((1 - my_c) * 64, 0), (64, 1152))
    keep = keep + row_send(give, dc=1)
    give = lax.dynamic_slice(keep, ((1 - my_x) * 32, 0), (32, 1152)).astype(bf16)
    keep = lax.dynamic_slice(keep, (my_x * 32, 0), (32, 1152))
    keep = (keep + row_send(give, dx=1).astype(f32)).astype(bf16)

    mine, other = spread(idx, dest_blocks, adj_tiles, prop.reshape(2, B, B))
    part = mine + row_send(other, dc=1).astype(f32)
    part = part.reshape(NZ, 2, 256, B)
    sent = row_send(part[:, 1].astype(bf16), dx=1)
    part = part[:, 0] + sent.astype(f32)
    out = part[0]
    low = part.astype(bf16)

    parts = [keep]
    gup = gdown = keep
    for s in range(1, 5):
        gup = row_send(gup, dz=1)
        parts.append(gup)
        if s < 4:
            gdown = row_send(gdown, dz=-1)
            parts.append(gdown)
    order = jnp.array([0, 2, 4, 6, 7, 5, 3, 1], jnp.int32)
    stacked = jnp.stack(parts)
    total = jnp.zeros((32, 1152), f32)
    for z in range(NZ):
        total = total + lax.dynamic_index_in_dim(
            stacked, order[(z - my_z) & 7], 0, keepdims=False
        ).astype(f32)

    for k in (4, 3, 5, 2, 6, 1, 7):
        out = out + row_send(low[k], dz=k).astype(f32)

    grad_scale = float(256 * lax.axis_size("row")) ** (-0.5)
    total = (total * grad_scale).astype(bf16)
    theirs = row_send(total, dx=1)
    first = jnp.where(my_x == 0, total, theirs)
    second = jnp.where(my_x == 0, theirs, total)
    two = jnp.concatenate([first, second], axis=0)
    theirs = row_send(two, dc=1)
    first = jnp.where(my_c == 0, two, theirs)
    second = jnp.where(my_c == 0, theirs, two)
    whole = jnp.concatenate([first, second], axis=0).astype(f32)
    return hidden, out, whole[:, :1024], whole[0, 1024:]


def solution(mesh):
    in_specs = (
        P("row", "feat"),
        P("feat", None),
        P("feat"),
        P("row", None, None),
        P("row"),
        P("row"),
        P("row", "feat"),
    )
    out_specs = (P("row", "feat"), P("row", "feat"), P("feat", None), P("feat"))
    return jax.shard_map(body, mesh=mesh, in_specs=in_specs, out_specs=out_specs, check_vma=False)
```

```python
import functools

import jax
import jax.numpy as jnp
from jax import lax
from jax.experimental import pallas as pl
from jax.experimental.pallas import tpu as pltpu
from jax.sharding import PartitionSpec as P

bf16 = jnp.bfloat16
f32 = jnp.float32
B = 128
NZ = 8
VM = pl.BlockSpec(memory_space=pltpu.VMEM)
SM = pl.BlockSpec(memory_space=pltpu.SMEM)


def row_send(v, dx=0, dz=0, dc=0):
    perm = []
    for i in range(32):
        x, z, c = i >> 4, (i >> 1) & 7, i & 1
        perm.append((i, ((x ^ dx) << 4) | (((z + dz) % NZ) << 1) | (c ^ dc)))
    return lax.ppermute(v, "row", perm)


def feat_send(v, dx=0, dy=0):
    return lax.ppermute(v, "feat", [(i, (((i >> 2) ^ dx) << 2) | ((i + dy) & 3)) for i in range(8)])


def params(mib=20):
    return pltpu.CompilerParams(vmem_limit_bytes=mib << 20)


def spin_send(v, k):
    perm = []
    for i in range(32):
        x, z, c = i >> 4, (i >> 1) & 7, i & 1
        perm.append((i, (x << 4) | (((z + (k if c == 0 else -k)) % NZ) << 1) | c))
    return lax.ppermute(v, "row", perm)


def after(v, *deps):
    return lax.optimization_barrier((v, *deps))[0]


def cost(flops, nbytes):
    return pl.CostEstimate(flops=flops, bytes_accessed=nbytes, transcendentals=0)


def agg_body(ids, idx, dest, tiles, *refs):
    near, far, out, src = refs[0:10], refs[10:19], refs[19], refs[20]
    core = ids[0] & 1

    def put(dc, dz, dx, v):
        src[pl.ds(((dc * NZ + dz) * 2 + dx) * 2, 2)] = v

    both, x0, o4, o1, o2, o3, p4, p1, p2, p3 = near
    put(0, 0, 0, both[0:2])
    put(1, 0, 0, both[2:4])
    put(0, 0, 1, x0[...])
    put(0, 4, 0, o4[...])
    put(0, 4, 1, p4[...])
    put(1, 0, 1, far[0][...])
    put(1, 4, 0, far[1][...])
    put(1, 4, 1, far[5][...])
    for k in (1, 2, 3):
        mine = jnp.where(core == 0, NZ - k, k)
        theirs = NZ - mine
        for dx, (n, f) in enumerate((((o1, o2, o3), far[2:5]), ((p1, p2, p3), far[6:9]))):
            put(0, mine, dx, n[k - 1][0:2])
            put(1, mine, dx, n[k - 1][2:4])
            put(1, theirs, dx, f[k - 1][0:2])
            put(0, theirs, dx, f[k - 1][2:4])
    group = 4

    def step(g, acc):
        lhs, rhs = [], []
        for u in range(group):
            t = g * group + u
            a = tiles[t]
            zero = jnp.zeros_like(a)
            d = dest[t]
            lhs.append(jnp.concatenate([jnp.where(d == 0, a, zero), jnp.where(d == 1, a, zero)], axis=0))
            rhs.append(src[idx[t]])
        return acc + jnp.dot(
            jnp.concatenate(lhs, axis=1), jnp.concatenate(rhs, axis=0), preferred_element_type=f32
        )

    acc = lax.fori_loop(0, 64 // group, step, jnp.zeros((2 * B, B), f32))
    out[...] = acc.astype(bf16)


def aggregate(ids, idx, dest, tiles, near, far):
    parts = [v.reshape(-1, B, B) for v in (*near, *far)]
    return pl.pallas_call(
        agg_body,
        out_shape=jax.ShapeDtypeStruct((2 * B, B), bf16),
        in_specs=[SM, SM, SM] + [VM] * 20,
        out_specs=VM,
        scratch_shapes=[pltpu.VMEM((64, B, B), bf16)],
        compiler_params=params(),
        cost_estimate=cost(2 * 64 * B**3, 4 << 20),
        name="aggregate",
    )(ids, idx, dest, tiles, *parts)


def lay_body(ids, *refs):
    own, other = refs[0:5], refs[5:10]
    w_out, og_out, bias_out = refs[10:13]
    core = ids[0] & 1
    yy, xx = ids[1] & 3, ids[1] >> 2
    for j, off in enumerate((0, -1, 1, 2)):
        for i in range(2):
            k = j * 2 + i
            n, base = (j, i * 784) if j < 3 else (3 + i, 0)
            col = pl.multiple_of((((xx ^ i) << 2) | ((yy + off) & 3)) * B, B)
            for src, c in ((own[n], core), (other[n], 1 - core)):
                for m in range(4):
                    at = pl.multiple_of(c * 512 + m * B, B)
                    w_out[pl.ds(k * B, B), pl.ds(at, B)] = src[pl.ds(base + m * B, B), :]
            og_out[:, pl.ds(col, B)] = own[n][pl.ds(base + 512, 256), :]
            bias_out[:, pl.ds(col, B)] = own[n][pl.ds(base + 768, 16), :].astype(f32)[0:8]


def lay_out(ids, own, other):
    return pl.pallas_call(
        lay_body,
        out_shape=(
            jax.ShapeDtypeStruct((1024, 1024), bf16),
            jax.ShapeDtypeStruct((256, 1024), bf16),
            jax.ShapeDtypeStruct((8, 1024), f32),
        ),
        in_specs=[SM] + [VM] * 10,
        out_specs=(VM, VM, VM),
        compiler_params=params(),
        cost_estimate=cost(0, 5 << 20),
        name="lay_out",
    )(ids, *own, *other)


def mid_body(ids, p0, p1, p2, p3, w_full, og, bias, w_own, hidden, prop, keep, give, agg, pre, gp, wp):
    for j, p in enumerate((p0, p1, p2, p3)):
        for i in range(2):
            agg[:, (j * 2 + i) * B : (j * 2 + i + 1) * B] = p[i * 256 : (i + 1) * 256, :]
    for n in range(4):
        cols = slice(n * 256, (n + 1) * 256)
        v = jnp.dot(agg[...], w_full[:, cols], preferred_element_type=f32) + bias[0:1, cols]
        pre[:, cols] = v
        s = jax.nn.sigmoid(v)
        gp[:, cols] = (og[:, cols].astype(f32) * s * (1.0 + v * (1.0 - s))).astype(bf16)
    mine = pl.ds(pl.multiple_of(ids[1] * B, B), B)
    v = pre[:, mine]
    hidden[...] = v * jax.nn.sigmoid(v)
    prop[...] = lax.dot_general(
        gp[...], w_own[...], (((1,), (1,)), ((), ())), preferred_element_type=f32
    ).astype(bf16)
    wp[:, 0:1024] = lax.dot_general(
        agg[:, 0:B], gp[...], (((0,), (0,)), ((), ())), preferred_element_type=f32
    )
    total = jnp.sum(gp[:, mine].astype(f32), axis=0, keepdims=True)
    wp[:, 1024:1152] = jnp.broadcast_to(total, (B, B))
    x, core = ids[0] >> 4, ids[0] & 1
    for ref, c in ((keep, core), (give, 1 - core)):
        for i in range(2):
            ref[i * 32 : (i + 1) * 32, :] = wp[pl.ds(pl.multiple_of(c * 64 + (x ^ i) * 32, 32), 32), :]


def middle(ids, pieces, w_full, og, bias, w_own):
    return pl.pallas_call(
        mid_body,
        out_shape=(
            jax.ShapeDtypeStruct((256, B), f32),
            jax.ShapeDtypeStruct((256, B), bf16),
            jax.ShapeDtypeStruct((64, 1152), f32),
            jax.ShapeDtypeStruct((64, 1152), f32),
        ),
        in_specs=[SM] + [VM] * 8,
        out_specs=(VM, VM, VM, VM),
        scratch_shapes=[
            pltpu.VMEM((256, 1024), bf16),
            pltpu.VMEM((256, 1024), f32),
            pltpu.VMEM((256, 1024), bf16),
            pltpu.VMEM((B, 1152), f32),
        ],
        compiler_params=params(),
        cost_estimate=cost(2 * 256 * 1024 * 1280, 5 << 20),
        name="middle",
    )(ids, *pieces, w_full, og, bias, w_own)


def spread_body(ids, idx, dest, tiles, prop, keep0, keep1, give, acc):
    acc[...] = jnp.zeros_like(acc)
    core = ids[0] & 1

    def step(g, carry):
        for u in range(4):
            t = g * 4 + u
            i = idx[t]
            acc[i] += lax.dot_general(
                tiles[t], prop[dest[t]], (((0,), (0,)), ((), ())), preferred_element_type=f32
            )
        return carry

    lax.fori_loop(0, 16, step, 0)

    def take(dc, dz, dx):
        return acc[pl.ds(((dc * NZ + dz) * 2 + dx) * 2, 2)]

    for dx in range(2):
        ref = (keep0, keep1)[dx]
        for n, k in enumerate((3, 2, 1)):
            up = jnp.where(core == 0, k, NZ - k)
            ref[4 * n : 4 * n + 2] = take(0, up, dx)
            ref[4 * n + 2 : 4 * n + 4] = take(1, up, dx)
            at = 16 * dx + 4 * n
            give[at : at + 2] = take(1, NZ - up, dx).astype(bf16)
            give[at + 2 : at + 4] = take(0, NZ - up, dx).astype(bf16)
        for n, dz in ((12, 4), (14, 0)):
            ref[n : n + 2] = take(0, dz, dx)
            give[16 * dx + n : 16 * dx + n + 2] = take(1, dz, dx).astype(bf16)


def spread(ids, idx, dest, tiles, prop):
    return pl.pallas_call(
        spread_body,
        out_shape=(
            jax.ShapeDtypeStruct((16, B, B), f32),
            jax.ShapeDtypeStruct((16, B, B), f32),
            jax.ShapeDtypeStruct((32, B, B), bf16),
        ),
        in_specs=[SM, SM, SM, VM, VM],
        out_specs=(VM, VM, VM),
        scratch_shapes=[pltpu.VMEM((64, B, B), f32)],
        compiler_params=params(),
        cost_estimate=cost(2 * 64 * B**3, 6 << 20),
        name="spread",
    )(ids, idx, dest, tiles, prop)


def sum_body(scale, ids, own, d1, d2, d3, d4, e, out, buf):
    core, z = ids[0] & 1, (ids[0] >> 1) & 7
    buf[0] = own[...]
    buf[4] = d4[...]
    for k, d in ((1, d1), (2, d2), (3, d3)):
        mine = jnp.where(core == 0, NZ - k, k)
        buf[mine] = d[0:32, :]
        buf[NZ - mine] = e[(k - 1) * 32 : k * 32, :]
    acc = buf[(NZ - z) & 7].astype(f32)
    for n in range(1, NZ):
        acc = acc + buf[(n - z) & 7].astype(f32)
    out[...] = (acc * scale).astype(bf16)


def sum_z(scale, ids, *parts):
    return pl.pallas_call(
        functools.partial(sum_body, scale),
        out_shape=jax.ShapeDtypeStruct((32, 1152), bf16),
        in_specs=[SM] + [VM] * 6,
        out_specs=VM,
        scratch_shapes=[pltpu.VMEM((NZ, 32, 1152), bf16)],
        compiler_params=params(8),
        cost_estimate=cost(32 * 1152 * 8, 1 << 20),
        name="sum_z",
    )(ids, *parts)


def wout_body(ids, mine, theirs, w_out, b_out, buf):
    x, core = ids[0] >> 4, ids[0] & 1
    for ref, c in ((mine, core), (theirs, 1 - core)):
        for i in range(2):
            at = pl.multiple_of(c * 64 + (x ^ i) * 32, 32)
            buf[pl.ds(at, 32), :] = ref[i * 32 : (i + 1) * 32, :].astype(f32)
    w_out[...] = buf[:, 0:1024]
    b_out[...] = buf[0:8, 1024:1152]


def weight_out(ids, mine, theirs):
    return pl.pallas_call(
        wout_body,
        out_shape=(jax.ShapeDtypeStruct((B, 1024), f32), jax.ShapeDtypeStruct((8, B), f32)),
        in_specs=[SM, VM, VM],
        out_specs=(VM, VM),
        scratch_shapes=[pltpu.VMEM((B, 1152), f32)],
        compiler_params=params(8),
        cost_estimate=cost(0, 1 << 20),
        name="weight_out",
    )(ids, mine, theirs)


def body(features, weight, bias_vector, adj_tiles, col_blocks, dest_blocks, out_grad):
    me = lax.axis_index("row")
    my_x, my_z, my_c = me >> 4, (me >> 1) & 7, me & 1
    ids = jnp.stack([me, lax.axis_index("feat")]).astype(jnp.int32)
    owner = col_blocks >> 1
    ox, oz, oc = owner >> 4, (owner >> 1) & 7, owner & 1
    idx = ((((oc ^ my_c) * NZ + ((oz - my_z) & 7)) * 2 + (ox ^ my_x)) * 2) + (col_blocks & 1)

    both = jnp.concatenate([features, row_send(features, dc=1)], axis=0)
    x0 = row_send(features, dx=1)

    half = lax.dynamic_slice(weight, (0, my_c * 512), (B, 512))
    pack = jnp.concatenate(
        [half[:, m * B : (m + 1) * B] for m in range(4)]
        + [out_grad, jnp.broadcast_to(bias_vector[None, :], (16, B))],
        axis=0,
    )
    pair = jnp.concatenate([pack, feat_send(pack, dx=1)], axis=0)

    o1 = spin_send(both, 1)
    o2 = spin_send(both, 2)
    o3 = spin_send(after(both, pair), 3)
    o4 = row_send(features, dz=4)
    wu, wd = feat_send(pair, dy=1), feat_send(pair, dy=-1)
    p1, p2 = row_send(o1, dx=1), row_send(o2, dx=1)
    p3, p4 = row_send(after(o3, wu, wd), dx=1), row_send(o4, dx=1)
    wa, wb = feat_send(wu[:784], dy=1), feat_send(wd[784:], dy=-1)
    near = (both, x0, o4, o1, o2, o3, p4, p1, p2, p3)
    far = tuple(row_send(v, dc=1) for v in (x0, o4, o1, o2, o3, p4, p1, p2, p3))
    own = (pair, wu, wd, wa, wb)
    other = tuple(row_send(v, dc=1) for v in own)

    aggregated = aggregate(ids, idx, dest_blocks, adj_tiles, near, far)

    q = jnp.concatenate([aggregated, feat_send(after(aggregated, wa, wb), dx=1)], axis=0)
    w_full, og, bias = lay_out(ids, own, other)
    q2 = after(q, w_full)
    pieces = (q, feat_send(q2, dy=1), feat_send(q2, dy=-1), feat_send(q2, dy=2))
    hidden, prop, keep, give = middle(ids, pieces, w_full, og, bias, weight)

    got = row_send(give, dc=1)
    more = row_send((keep[32:] + got[32:]).astype(bf16), dx=1)

    keep0, keep1, away = spread(ids, idx, dest_blocks, adj_tiles, prop.reshape(2, B, B))
    came = row_send(away, dc=1).astype(f32)
    half0, half1 = keep0 + came[:16], (keep1 + came[16:]).astype(bf16)
    xa = row_send(half1[:8], dx=1)
    xb = row_send(half1[8:], dx=1)

    quarter = (keep[:32] + got[:32] + more.astype(f32)).astype(bf16)
    halves = after(jnp.concatenate([quarter, row_send(quarter, dc=1)], axis=0), half1)
    d1, d2, d3 = (spin_send(halves, k) for k in (1, 2, 3))
    d4 = row_send(quarter, dz=4)

    ta = (half0[:8] + xa.astype(f32)).astype(bf16)
    tb = half0[8:] + xb.astype(f32)
    r3, r2 = spin_send(ta[:4], 3), spin_send(ta[4:], 2)
    r1 = spin_send(tb[:4].astype(bf16), 1)
    r4 = row_send(tb[4:6].astype(bf16), dz=4)

    e = row_send(after(jnp.concatenate([d1[32:], d2[32:], d3[32:]], axis=0), ta, tb), dc=1)
    scale = float(256 * lax.axis_size("row")) ** (-0.5)
    total = sum_z(scale, ids, quarter, d1, d2, d3, d4, e)
    two = jnp.concatenate([total, row_send(total, dx=1)], axis=0)
    weight_grad, bias_grad = weight_out(ids, two, row_send(two, dc=1))

    r = r1.astype(f32) + r2.astype(f32) + r3.astype(f32)
    out = tb[6:] + r4.astype(f32) + r[:2] + row_send(r[2:], dc=1)
    return hidden, out.reshape(256, B), weight_grad, bias_grad[0]


def solution(mesh):
    in_specs = (
        P("row", "feat"),
        P("feat", None),
        P("feat"),
        P("row", None, None),
        P("row"),
        P("row"),
        P("row", "feat"),
    )
    out_specs = (P("row", "feat"), P("row", "feat"), P("feat", None), P("feat"))
    return jax.shard_map(body, mesh=mesh, in_specs=in_specs, out_specs=out_specs, check_vma=False)
```

```python
import functools

import jax
import jax.numpy as jnp
from jax import lax
from jax.experimental import pallas as pl
from jax.experimental.pallas import tpu as pltpu
from jax.sharding import PartitionSpec as P

bf16 = jnp.bfloat16
f32 = jnp.float32
B = 128
NZ = 8
VM = pl.BlockSpec(memory_space=pltpu.VMEM)
SM = pl.BlockSpec(memory_space=pltpu.SMEM)
ANY = pl.BlockSpec(memory_space=pl.ANY)


def row_send(v, dx=0, dz=0, dc=0):
    perm = []
    for i in range(32):
        x, z, c = i >> 4, (i >> 1) & 7, i & 1
        perm.append((i, ((x ^ dx) << 4) | (((z + dz) % NZ) << 1) | (c ^ dc)))
    return lax.ppermute(v, "row", perm)


def feat_send(v, dx=0, dy=0):
    return lax.ppermute(v, "feat", [(i, (((i >> 2) ^ dx) << 2) | ((i + dy) & 3)) for i in range(8)])


def params(mib=20):
    return pltpu.CompilerParams(vmem_limit_bytes=mib << 20)


def spin_send(v, k):
    perm = []
    for i in range(32):
        x, z, c = i >> 4, (i >> 1) & 7, i & 1
        perm.append((i, (x << 4) | (((z + (k if c == 0 else -k)) % NZ) << 1) | c))
    return lax.ppermute(v, "row", perm)


def after(v, *deps):
    return lax.optimization_barrier((v, *deps))[0]


def cost(flops, nbytes):
    return pl.CostEstimate(flops=flops, bytes_accessed=nbytes, transcendentals=0)


def pack_body(ids, w, og, bias, out):
    core = ids[0] & 1
    for m in range(4):
        at = pl.multiple_of(core * 512 + m * B, B)
        out[m * B : (m + 1) * B, :] = w[:, pl.ds(at, B)]
    out[512:768, :] = og[...]
    out[768:784, :] = jnp.broadcast_to(bias[...], (16, B))


def pack_up(ids, w, og, bias):
    return pl.pallas_call(
        pack_body,
        out_shape=jax.ShapeDtypeStruct((784, B), bf16),
        in_specs=[SM, VM, VM, VM],
        out_specs=VM,
        compiler_params=params(8),
        cost_estimate=cost(0, 1 << 19),
        name="pack_up",
    )(ids, w, og, bias)


def agg_body(ids, idx, dest, tiles, *refs):
    near, far, out, src, sem = refs[0:10], refs[10:19], refs[19], refs[20], refs[21]
    core = ids[0] & 1
    copies = []

    def put(dc, dz, dx, v):
        at = ((dc * NZ + dz) * 2 + dx) * 2
        copies.append(pltpu.make_async_copy(v, src.at[pl.ds(at, 2)], sem.at[len(copies)]))
        copies[-1].start()

    both, x0, o4, o1, o2, o3, p4, p1, p2, p3 = near
    put(0, 0, 0, both.at[0:2])
    put(1, 0, 0, both.at[2:4])
    put(0, 0, 1, x0)
    put(0, 4, 0, o4)
    put(0, 4, 1, p4)
    put(1, 0, 1, far[0])
    put(1, 4, 0, far[1])
    put(1, 4, 1, far[5])
    for k in (1, 2, 3):
        mine = jnp.where(core == 0, NZ - k, k)
        theirs = NZ - mine
        for dx, (n, f) in enumerate((((o1, o2, o3), far[2:5]), ((p1, p2, p3), far[6:9]))):
            put(0, mine, dx, n[k - 1].at[0:2])
            put(1, mine, dx, n[k - 1].at[2:4])
            put(1, theirs, dx, f[k - 1].at[0:2])
            put(0, theirs, dx, f[k - 1].at[2:4])
    for c in copies:
        c.wait()
    group = 4

    def step(g, acc):
        lhs, rhs = [], []
        for u in range(group):
            t = g * group + u
            a = tiles[t]
            zero = jnp.zeros_like(a)
            d = dest[t]
            lhs.append(jnp.concatenate([jnp.where(d == 0, a, zero), jnp.where(d == 1, a, zero)], axis=0))
            rhs.append(src[idx[t]])
        return acc + jnp.dot(
            jnp.concatenate(lhs, axis=1), jnp.concatenate(rhs, axis=0), preferred_element_type=f32
        )

    acc = lax.fori_loop(0, 64 // group, step, jnp.zeros((2 * B, B), f32))
    out[...] = acc.astype(bf16)


def aggregate(ids, idx, dest, tiles, near, far):
    parts = [v.reshape(-1, B, B) for v in (*near, *far)]
    return pl.pallas_call(
        agg_body,
        out_shape=jax.ShapeDtypeStruct((2 * B, B), bf16),
        in_specs=[SM, SM, SM, VM] + [ANY] * 19,
        out_specs=VM,
        scratch_shapes=[pltpu.VMEM((64, B, B), bf16), pltpu.SemaphoreType.DMA((32,))],
        compiler_params=params(),
        cost_estimate=cost(2 * 64 * B**3, 4 << 20),
        name="aggregate",
    )(ids, idx, dest, tiles, *parts)


def lay_body(ids, *refs):
    own, other = refs[0:5], refs[5:10]
    w_out, og_out, bias_out, rows, sem = refs[10:15]
    core = ids[0] & 1
    yy, xx = ids[1] & 3, ids[1] >> 2
    copies, cols = [], []

    def put(src, dst):
        copies.append(pltpu.make_async_copy(src, dst, sem.at[len(copies)]))
        copies[-1].start()

    for j, off in enumerate((0, -1, 1, 2)):
        for i in range(2):
            k = j * 2 + i
            n, base = (j, i * 784) if j < 3 else (3 + i, 0)
            col = pl.multiple_of((((xx ^ i) << 2) | ((yy + off) & 3)) * B, B)
            cols.append(col)
            for src, c in ((own[n], core), (other[n], 1 - core)):
                for m in range(4):
                    at = pl.multiple_of(c * 512 + m * B, B)
                    put(src.at[pl.ds(base + m * B, B), :], w_out.at[pl.ds(k * B, B), pl.ds(at, B)])
            put(own[n].at[pl.ds(base + 512, 256), :], og_out.at[:, pl.ds(col, B)])
            put(own[n].at[pl.ds(base + 768, 16), :], rows.at[k])
    for c in copies:
        c.wait()
    for k in range(8):
        bias_out[:, pl.ds(cols[k], B)] = rows[k].astype(f32)[0:8]


def lay_out(ids, own, other):
    return pl.pallas_call(
        lay_body,
        out_shape=(
            jax.ShapeDtypeStruct((1024, 1024), bf16),
            jax.ShapeDtypeStruct((256, 1024), bf16),
            jax.ShapeDtypeStruct((8, 1024), f32),
        ),
        in_specs=[SM] + [ANY] * 10,
        out_specs=(VM, VM, VM),
        scratch_shapes=[pltpu.VMEM((8, 16, B), bf16), pltpu.SemaphoreType.DMA((80,))],
        compiler_params=params(),
        cost_estimate=cost(0, 5 << 20),
        name="lay_out",
    )(ids, *own, *other)


def mid_body(ids, p0, p1, p2, p3, w_full, og, bias, w_own, hidden, prop, keep, give, agg, pre, gp, wp):
    for j, p in enumerate((p0, p1, p2, p3)):
        for i in range(2):
            agg[:, (j * 2 + i) * B : (j * 2 + i + 1) * B] = p[i * 256 : (i + 1) * 256, :]
    for n in range(4):
        cols = slice(n * 256, (n + 1) * 256)
        v = jnp.dot(agg[...], w_full[:, cols], preferred_element_type=f32) + bias[0:1, cols]
        pre[:, cols] = v
        s = jax.nn.sigmoid(v)
        gp[:, cols] = (og[:, cols].astype(f32) * s * (1.0 + v * (1.0 - s))).astype(bf16)
    mine = pl.ds(pl.multiple_of(ids[1] * B, B), B)
    v = pre[:, mine]
    hidden[...] = v * jax.nn.sigmoid(v)
    prop[...] = lax.dot_general(
        gp[...], w_own[...], (((1,), (1,)), ((), ())), preferred_element_type=f32
    ).astype(bf16)
    wp[:, 0:1024] = lax.dot_general(
        agg[:, 0:B], gp[...], (((0,), (0,)), ((), ())), preferred_element_type=f32
    )
    total = jnp.sum(gp[:, mine].astype(f32), axis=0, keepdims=True)
    wp[:, 1024:1152] = jnp.broadcast_to(total, (B, B))
    x, core = ids[0] >> 4, ids[0] & 1
    for ref, c in ((keep, core), (give, 1 - core)):
        for i in range(2):
            ref[i * 32 : (i + 1) * 32, :] = wp[pl.ds(pl.multiple_of(c * 64 + (x ^ i) * 32, 32), 32), :]


def middle(ids, pieces, w_full, og, bias, w_own):
    return pl.pallas_call(
        mid_body,
        out_shape=(
            jax.ShapeDtypeStruct((256, B), f32),
            jax.ShapeDtypeStruct((256, B), bf16),
            jax.ShapeDtypeStruct((64, 1152), f32),
            jax.ShapeDtypeStruct((64, 1152), f32),
        ),
        in_specs=[SM] + [VM] * 8,
        out_specs=(VM, VM, VM, VM),
        scratch_shapes=[
            pltpu.VMEM((256, 1024), bf16),
            pltpu.VMEM((256, 1024), f32),
            pltpu.VMEM((256, 1024), bf16),
            pltpu.VMEM((B, 1152), f32),
        ],
        compiler_params=params(),
        cost_estimate=cost(2 * 256 * 1024 * 1280, 5 << 20),
        name="middle",
    )(ids, *pieces, w_full, og, bias, w_own)


def spread_body(ids, idx, dest, tiles, prop, keep0, keep1, give, acc):
    acc[...] = jnp.zeros_like(acc)
    core = ids[0] & 1

    def step(g, carry):
        for u in range(4):
            t = g * 4 + u
            i = idx[t]
            acc[i] += lax.dot_general(
                tiles[t], prop[dest[t]], (((0,), (0,)), ((), ())), preferred_element_type=f32
            )
        return carry

    lax.fori_loop(0, 16, step, 0)

    def take(dc, dz, dx):
        return acc[pl.ds(((dc * NZ + dz) * 2 + dx) * 2, 2)]

    for dx in range(2):
        ref = (keep0, keep1)[dx]
        for n, k in enumerate((3, 2, 1)):
            up = jnp.where(core == 0, k, NZ - k)
            ref[4 * n : 4 * n + 2] = take(0, up, dx)
            ref[4 * n + 2 : 4 * n + 4] = take(1, up, dx)
            at = 16 * dx + 4 * n
            give[at : at + 2] = take(1, NZ - up, dx).astype(bf16)
            give[at + 2 : at + 4] = take(0, NZ - up, dx).astype(bf16)
        for n, dz in ((12, 4), (14, 0)):
            ref[n : n + 2] = take(0, dz, dx)
            give[16 * dx + n : 16 * dx + n + 2] = take(1, dz, dx).astype(bf16)


def spread(ids, idx, dest, tiles, prop):
    return pl.pallas_call(
        spread_body,
        out_shape=(
            jax.ShapeDtypeStruct((16, B, B), f32),
            jax.ShapeDtypeStruct((16, B, B), f32),
            jax.ShapeDtypeStruct((32, B, B), bf16),
        ),
        in_specs=[SM, SM, SM, VM, VM],
        out_specs=(VM, VM, VM),
        scratch_shapes=[pltpu.VMEM((64, B, B), f32)],
        compiler_params=params(),
        cost_estimate=cost(2 * 64 * B**3, 6 << 20),
        name="spread",
    )(ids, idx, dest, tiles, prop)


def sum_body(scale, ids, own, d1, d2, d3, d4, e, out, buf):
    core, z = ids[0] & 1, (ids[0] >> 1) & 7
    buf[0] = own[...]
    buf[4] = d4[...]
    for k, d in ((1, d1), (2, d2), (3, d3)):
        mine = jnp.where(core == 0, NZ - k, k)
        buf[mine] = d[0:32, :]
        buf[NZ - mine] = e[(k - 1) * 32 : k * 32, :]
    acc = buf[(NZ - z) & 7].astype(f32)
    for n in range(1, NZ):
        acc = acc + buf[(n - z) & 7].astype(f32)
    out[...] = (acc * scale).astype(bf16)


def sum_z(scale, ids, *parts):
    return pl.pallas_call(
        functools.partial(sum_body, scale),
        out_shape=jax.ShapeDtypeStruct((32, 1152), bf16),
        in_specs=[SM] + [VM] * 6,
        out_specs=VM,
        scratch_shapes=[pltpu.VMEM((NZ, 32, 1152), bf16)],
        compiler_params=params(8),
        cost_estimate=cost(32 * 1152 * 8, 1 << 20),
        name="sum_z",
    )(ids, *parts)


def wout_body(ids, mine, theirs, w_out, b_out, buf):
    x, core = ids[0] >> 4, ids[0] & 1
    for ref, c in ((mine, core), (theirs, 1 - core)):
        for i in range(2):
            at = pl.multiple_of(c * 64 + (x ^ i) * 32, 32)
            buf[pl.ds(at, 32), :] = ref[i * 32 : (i + 1) * 32, :].astype(f32)
    w_out[...] = buf[:, 0:1024]
    b_out[...] = buf[0:8, 1024:1152]


def weight_out(ids, mine, theirs):
    return pl.pallas_call(
        wout_body,
        out_shape=(jax.ShapeDtypeStruct((B, 1024), f32), jax.ShapeDtypeStruct((8, B), f32)),
        in_specs=[SM, VM, VM],
        out_specs=(VM, VM),
        scratch_shapes=[pltpu.VMEM((B, 1152), f32)],
        compiler_params=params(8),
        cost_estimate=cost(0, 1 << 20),
        name="weight_out",
    )(ids, mine, theirs)


def body(features, weight, bias_vector, adj_tiles, col_blocks, dest_blocks, out_grad):
    me = lax.axis_index("row")
    my_x, my_z, my_c = me >> 4, (me >> 1) & 7, me & 1
    ids = jnp.stack([me, lax.axis_index("feat")]).astype(jnp.int32)
    owner = col_blocks >> 1
    ox, oz, oc = owner >> 4, (owner >> 1) & 7, owner & 1
    idx = ((((oc ^ my_c) * NZ + ((oz - my_z) & 7)) * 2 + (ox ^ my_x)) * 2) + (col_blocks & 1)

    both = jnp.concatenate([features, row_send(features, dc=1)], axis=0)
    x0 = row_send(features, dx=1)

    pack = pack_up(ids, weight, out_grad, bias_vector[None, :])
    pair = jnp.concatenate([pack, feat_send(pack, dx=1)], axis=0)

    o1 = spin_send(both, 1)
    o2 = spin_send(both, 2)
    o3 = spin_send(after(both, pair), 3)
    o4 = spin_send(o3[:256], 1)
    wu, wd = feat_send(pair, dy=1), feat_send(pair, dy=-1)
    p1, p2 = row_send(o1, dx=1), row_send(o2, dx=1)
    p3, p4 = row_send(after(o3, wu, wd), dx=1), row_send(o4, dx=1)
    wa, wb = feat_send(wu[:784], dy=1), feat_send(wd[784:], dy=-1)
    near = (both, x0, o4, o1, o2, o3, p4, p1, p2, p3)
    far = tuple(row_send(v, dc=1) for v in (x0, o4, o1, o2, o3, p4, p1, p2, p3))
    own = (pair, wu, wd, wa, wb)
    other = tuple(row_send(v, dc=1) for v in own)

    aggregated = aggregate(ids, idx, dest_blocks, adj_tiles, near, far)

    q = jnp.concatenate([aggregated, feat_send(after(aggregated, wa, wb), dx=1)], axis=0)
    w_full, og, bias = lay_out(ids, own, other)
    q2 = after(q, w_full)
    pieces = (q, feat_send(q2, dy=1), feat_send(q2, dy=-1), feat_send(q2, dy=2))
    hidden, prop, keep, give = middle(ids, pieces, w_full, og, bias, weight)

    got = row_send(give, dc=1)
    more = row_send((keep[32:] + got[32:]).astype(bf16), dx=1)

    keep0, keep1, away = spread(ids, idx, dest_blocks, adj_tiles, prop.reshape(2, B, B))
    came = row_send(away, dc=1).astype(f32)
    half0, half1 = keep0 + came[:16], (keep1 + came[16:]).astype(bf16)
    xc = row_send(half1[12:], dx=1)
    xb = row_send(half1[4:12], dx=1)
    xa = row_send(half1[:4], dx=1)

    quarter = (keep[:32] + got[:32] + more.astype(f32)).astype(bf16)
    halves = after(jnp.concatenate([quarter, row_send(quarter, dc=1)], axis=0), xc)
    d1, d2, d3 = (spin_send(halves, k) for k in (1, 2, 3))
    d4 = spin_send(d3[:32], 1)

    tc = half0[12:] + xc.astype(f32)
    r4 = spin_send(tc[:2].astype(bf16), 1)
    tb = (half0[4:12] + xb.astype(f32)).astype(bf16)
    r2, r1 = spin_send(tb[:4], 2), spin_send(tb[4:], 1)
    ta = half0[:4] + xa.astype(f32)
    ta = jnp.concatenate([ta[:2] + r4.astype(f32), ta[2:]], axis=0).astype(bf16)
    r3 = spin_send(ta, 3)

    e = row_send(after(jnp.concatenate([d1[32:], d2[32:], d3[32:]], axis=0), ta), dc=1)
    scale = float(256 * lax.axis_size("row")) ** (-0.5)
    total = sum_z(scale, ids, quarter, d1, d2, d3, d4, e)
    two = jnp.concatenate([total, row_send(total, dx=1)], axis=0)
    weight_grad, bias_grad = weight_out(ids, two, row_send(two, dc=1))

    r = r1.astype(f32) + r2.astype(f32) + r3.astype(f32)
    out = tc[2:] + r[:2] + row_send(r[2:], dc=1)
    return hidden, out.reshape(256, B), weight_grad, bias_grad[0]


def solution(mesh):
    in_specs = (
        P("row", "feat"),
        P("feat", None),
        P("feat"),
        P("row", None, None),
        P("row"),
        P("row"),
        P("row", "feat"),
    )
    out_specs = (P("row", "feat"), P("row", "feat"), P("feat", None), P("feat"))
    return jax.shard_map(body, mesh=mesh, in_specs=in_specs, out_specs=out_specs, check_vma=False)
```

```python
import functools

import jax
import jax.numpy as jnp
from jax import lax
from jax.experimental import pallas as pl
from jax.experimental.pallas import tpu as pltpu
from jax.sharding import PartitionSpec as P

bf16 = jnp.bfloat16
f32 = jnp.float32
B = 128
NZ = 8
VM = pl.BlockSpec(memory_space=pltpu.VMEM)
SM = pl.BlockSpec(memory_space=pltpu.SMEM)
HB = pl.BlockSpec(memory_space=pltpu.HBM)
ANY = pl.BlockSpec(memory_space=pl.ANY)


def row_send(v, dx=0, dz=0, dc=0):
    perm = []
    for i in range(32):
        x, z, c = i >> 4, (i >> 1) & 7, i & 1
        perm.append((i, ((x ^ dx) << 4) | (((z + dz) % NZ) << 1) | (c ^ dc)))
    return lax.ppermute(v, "row", perm)


def feat_send(v, dx=0, dy=0):
    return lax.ppermute(v, "feat", [(i, (((i >> 2) ^ dx) << 2) | ((i + dy) & 3)) for i in range(8)])


def params(mib=20):
    return pltpu.CompilerParams(vmem_limit_bytes=mib << 20)


def spin_send(v, k, way=1):
    perm = []
    for i in range(32):
        x, z, c = i >> 4, (i >> 1) & 7, i & 1
        perm.append((i, (x << 4) | (((z + way * (k if c == 0 else -k)) % NZ) << 1) | c))
    return lax.ppermute(v, "row", perm)


def tie(a, b):
    return lax.optimization_barrier((a, b))


def cost(flops, nbytes):
    return pl.CostEstimate(flops=flops, bytes_accessed=nbytes, transcendentals=0)


def pack_body(ids, w, og, bias, out):
    core = ids[0] & 1
    for m in range(4):
        at = pl.multiple_of(core * 512 + m * B, B)
        out[m * B : (m + 1) * B, :] = w[:, pl.ds(at, B)]
    out[512:768, :] = og[...]
    out[768:784, :] = jnp.broadcast_to(bias[...], (16, B))


def pack_up(ids, w, og, bias):
    return pl.pallas_call(
        pack_body,
        out_shape=jax.ShapeDtypeStruct((784, B), bf16),
        in_specs=[SM, VM, VM, VM],
        out_specs=VM,
        compiler_params=params(8),
        cost_estimate=cost(0, 1 << 19),
        name="pack_up",
    )(ids, w, og, bias)


def plan_body(ids, c0, d0, c1, d1, out):
    me = ids[0]
    mx, mz, mc = me >> 4, (me >> 1) & 7, me & 1
    for side, (cols, dest) in enumerate(((c0, d0), (c1, d1))):
        base = 8 + 72 * side

        def step(i, n, cols=cols, dest=dest, base=base, side=side):
            b = cols[i]
            o = b >> 1
            dx, dz, dc = (o >> 4) ^ mx, ((o >> 1) - mz) & 7, (o & 1) ^ mc
            k = jnp.where(mc == 0, dz, NZ - dz)
            edge = (dz & 3) == 0
            held = jnp.where(edge, 1 - dc, jnp.where(k <= 3, 1, 0))
            j = jnp.where(edge, jnp.where(dz == 0, 7, 6), (3 - k) * 2 + dc)
            slot = dx * 16 + j * 2 + (b & 1)
            out[base + n] = i | (slot << 8) | ((dest[i] + 2 * side) << 16)
            return n + held

        n = lax.fori_loop(0, 64, step, 0)
        for u in range(4):
            out[base + n + u] = (32 << 8) | (4 << 16)
        out[side] = (n + 3) >> 2


def plan_tiles(ids, c0, d0, c1, d1):
    return pl.pallas_call(
        plan_body,
        out_shape=jax.ShapeDtypeStruct((160,), jnp.int32),
        in_specs=[SM] * 5,
        out_specs=SM,
        compiler_params=params(4),
        cost_estimate=cost(10000, 4096),
        name="plan_tiles",
    )(ids, c0, d0, c1, d1)


def each_tile(plan, tiles, more, use):
    for side, ref in enumerate((tiles, more)):
        def step(g, carry, side=side, ref=ref):
            for u in range(4):
                e = plan[8 + 72 * side + g * 4 + u]
                use(ref[e & 255], (e >> 8) & 255, e >> 16)
            return carry

        lax.fori_loop(0, plan[side], step, 0)


def agg_body(plan, tiles, more, *refs):
    pieces, mine, theirs, src, acc, sem = refs[0:10], refs[10], refs[11], refs[12], refs[13], refs[14]
    both, x0, o4, o1, o2, o3, p4, p1, p2, p3 = pieces
    copies = []

    def put(dx, j, v):
        n = v.shape[0]
        at = dx * 16 + j * 2
        copies.append(pltpu.make_async_copy(v, src.at[at : at + n], sem.at[len(copies)]))
        copies[-1].start()

    for dx, (v3, v2, v1, v4, v0) in enumerate(((o3, o2, o1, o4, both.at[0:2]), (p3, p2, p1, p4, x0))):
        for j, v in ((0, v3), (2, v2), (4, v1), (6, v4), (7, v0)):
            put(dx, j, v)
    acc[...] = jnp.zeros_like(acc)
    src[32] = jnp.zeros((B, B), bf16)
    for c in copies:
        c.wait()

    def use(tile, slot, dest):
        acc[dest] += jnp.dot(tile, src[slot], preferred_element_type=f32)

    each_tile(plan, tiles, more, use)
    mine[...] = acc[0:2]
    theirs[...] = acc[2:4]


def aggregate(plan, tiles, more, pieces):
    parts = [v.reshape(-1, B, B) for v in pieces]
    return pl.pallas_call(
        agg_body,
        out_shape=(jax.ShapeDtypeStruct((2, B, B), f32), jax.ShapeDtypeStruct((2, B, B), f32)),
        in_specs=[SM, VM, VM] + [HB] * 10,
        out_specs=(VM, VM),
        scratch_shapes=[
            pltpu.VMEM((33, B, B), bf16),
            pltpu.VMEM((5, B, B), f32),
            pltpu.SemaphoreType.DMA((10,)),
        ],
        compiler_params=params(12),
        cost_estimate=cost(2 * 64 * B**3, 4 << 20),
        name="aggregate",
    )(plan, tiles, more, *parts)


def lay_body(ids, *refs):
    own = refs[0:5]
    w_out, og_out, bias_out, rows, sem = refs[5:10]
    yy, xx = ids[1] & 3, ids[1] >> 2
    copies, cols = [], []

    def put(src, dst):
        copies.append(pltpu.make_async_copy(src, dst, sem.at[len(copies)]))
        copies[-1].start()

    for j, off in enumerate((0, -1, 1, 2)):
        for i in range(2):
            k = j * 2 + i
            n, base = (j, i * 784) if j < 3 else (3 + i, 0)
            col = pl.multiple_of((((xx ^ i) << 2) | ((yy + off) & 3)) * B, B)
            cols.append(col)
            for m in range(4):
                put(own[n].at[pl.ds(base + m * B, B), :], w_out.at[pl.ds(k * B, B), pl.ds(m * B, B)])
            put(own[n].at[pl.ds(base + 512, 256), :], og_out.at[:, pl.ds(col, B)])
            put(own[n].at[pl.ds(base + 768, 16), :], rows.at[k])
    for c in copies:
        c.wait()
    for k in range(8):
        bias_out[:, pl.ds(cols[k], B)] = rows[k].astype(f32)[0:8]


def lay_out(ids, own):
    return pl.pallas_call(
        lay_body,
        out_shape=(
            jax.ShapeDtypeStruct((1024, 512), bf16),
            jax.ShapeDtypeStruct((256, 1024), bf16),
            jax.ShapeDtypeStruct((8, 1024), f32),
        ),
        in_specs=[SM] + [HB] * 5,
        out_specs=(VM, VM, VM),
        scratch_shapes=[pltpu.VMEM((8, 16, B), bf16), pltpu.SemaphoreType.DMA((48,))],
        compiler_params=params(8),
        cost_estimate=cost(0, 3 << 20),
        name="lay_out",
    )(ids, *own)


def mid_body(ids, p0, p1, p2, p3, w0, w1, og, bias, w_own, hidden, prop, keep, give, agg, pre, gp, wp):
    x, core = ids[0] >> 4, ids[0] & 1
    for j, p in enumerate((p0, p1, p2, p3)):
        for i in range(2):
            agg[:, (j * 2 + i) * B : (j * 2 + i + 1) * B] = p[i * 256 : (i + 1) * 256, :]
    for w, c in ((w0, core), (w1, 1 - core)):
        for m in range(2):
            cols = pl.ds(pl.multiple_of(c * 512 + m * 256, 256), 256)
            v = jnp.dot(agg[...], w[:, m * 256 : (m + 1) * 256], preferred_element_type=f32)
            v = v + bias[0:1, cols]
            pre[:, cols] = v
            s = jax.nn.sigmoid(v)
            gp[:, cols] = (og[:, cols].astype(f32) * s * (1.0 + v * (1.0 - s))).astype(bf16)
    mine = pl.ds(pl.multiple_of(ids[1] * B, B), B)
    v = pre[:, mine]
    hidden[...] = v * jax.nn.sigmoid(v)
    prop[...] = lax.dot_general(
        gp[...], w_own[...], (((1,), (1,)), ((), ())), preferred_element_type=f32
    ).astype(bf16)
    wp[:, 0:1024] = lax.dot_general(
        agg[:, 0:B], gp[...], (((0,), (0,)), ((), ())), preferred_element_type=f32
    )
    total = jnp.sum(gp[:, mine].astype(f32), axis=0, keepdims=True)
    wp[:, 1024:1152] = jnp.broadcast_to(total, (B, B))
    for ref, c in ((keep, core), (give, 1 - core)):
        for i in range(2):
            ref[i * 32 : (i + 1) * 32, :] = wp[pl.ds(pl.multiple_of(c * 64 + (x ^ i) * 32, 32), 32), :]


def middle(ids, pieces, w0, w1, og, bias, w_own):
    return pl.pallas_call(
        mid_body,
        out_shape=(
            jax.ShapeDtypeStruct((256, B), f32),
            jax.ShapeDtypeStruct((256, B), bf16),
            jax.ShapeDtypeStruct((64, 1152), f32),
            jax.ShapeDtypeStruct((64, 1152), f32),
        ),
        in_specs=[SM] + [VM] * 9,
        out_specs=(VM, VM, VM, VM),
        scratch_shapes=[
            pltpu.VMEM((256, 1024), bf16),
            pltpu.VMEM((256, 1024), f32),
            pltpu.VMEM((256, 1024), bf16),
            pltpu.VMEM((B, 1152), f32),
        ],
        compiler_params=params(),
        cost_estimate=cost(2 * 256 * 1024 * 1280, 5 << 20),
        name="middle",
    )(ids, *pieces, w0, w1, og, bias, w_own)


def spread_body(plan, tiles, more, prop, peer, keep, got, near, first, rest, acc, both):
    acc[...] = jnp.zeros_like(acc)
    both[0:2] = prop[...]
    both[2:4] = peer[...]
    both[4] = jnp.zeros((B, B), bf16)

    def use(tile, slot, dest):
        acc[slot] += lax.dot_general(
            tile, both[dest], (((0,), (0,)), ((), ())), preferred_element_type=f32
        )

    each_tile(plan, tiles, more, use)
    near[...] = acc[0:16]
    for n in range(2):
        first[n * B : (n + 1) * B, :] = acc[28 + n].astype(bf16)
    for n in range(9):
        cols = slice(n * B, (n + 1) * B)
        first[256 + 32 * n : 288 + 32 * n, :] = (keep[32:64, cols] + got[32:64, cols]).astype(bf16)
    rest[0:12] = acc[16:28].astype(bf16)
    rest[12:14] = acc[30:32].astype(bf16)


def spread(plan, tiles, more, prop, peer, keep, got):
    return pl.pallas_call(
        spread_body,
        out_shape=(
            jax.ShapeDtypeStruct((16, B, B), f32),
            jax.ShapeDtypeStruct((544, B), bf16),
            jax.ShapeDtypeStruct((14, B, B), bf16),
        ),
        in_specs=[SM] + [VM] * 6,
        out_specs=(VM, VM, VM),
        scratch_shapes=[pltpu.VMEM((33, B, B), f32), pltpu.VMEM((5, B, B), bf16)],
        compiler_params=params(12),
        cost_estimate=cost(2 * 64 * B**3, 6 << 20),
        name="spread",
    )(plan, tiles, more, prop, peer, keep, got)


def meet_body(keep, got, came, near, quarter, far):
    for n in range(9):
        cols = slice(n * B, (n + 1) * B)
        v = came[256 + 32 * n : 288 + 32 * n, :].astype(f32)
        quarter[:, cols] = (keep[0:32, cols] + got[0:32, cols] + v).astype(bf16)
    for n in range(2):
        far[n] = (near[12 + n] + came[n * B : (n + 1) * B, :].astype(f32)).astype(bf16)


def meet(keep, got, came, near):
    return pl.pallas_call(
        meet_body,
        out_shape=(jax.ShapeDtypeStruct((32, 1152), bf16), jax.ShapeDtypeStruct((2, B, B), bf16)),
        in_specs=[VM] * 4,
        out_specs=(VM, VM),
        compiler_params=params(8),
        cost_estimate=cost(0, 1 << 20),
        name="meet",
    )(keep, got, came, near)


def rows_body(d1, d2, d3, t, out):
    for n, d in enumerate((d1, d2, d3)):
        out[32 * n : 32 * n + 32, :] = d[32:64, :]


def peer_rows(d1, d2, d3, t):
    return pl.pallas_call(
        rows_body,
        out_shape=jax.ShapeDtypeStruct((96, 1152), bf16),
        in_specs=[VM] * 3 + [ANY],
        out_specs=VM,
        compiler_params=params(4),
        cost_estimate=cost(0, 1 << 18),
        name="peer_rows",
    )(d1, d2, d3, t)


def sum_body(scale, ids, own, d1, d2, d3, d4, e, t, out, buf):
    core, z = ids[0] & 1, (ids[0] >> 1) & 7
    buf[0] = own[...]
    buf[4] = d4[...]
    for k, d in ((1, d1), (2, d2), (3, d3)):
        mine = jnp.where(core == 0, k, NZ - k)
        buf[mine] = d[0:32, :]
        buf[NZ - mine] = e[(k - 1) * 32 : k * 32, :]
    acc = buf[(NZ - z) & 7].astype(f32)
    for n in range(1, NZ):
        acc = acc + buf[(n - z) & 7].astype(f32)
    out[...] = (acc * scale).astype(bf16)


def sum_z(scale, ids, *parts):
    return pl.pallas_call(
        functools.partial(sum_body, scale),
        out_shape=jax.ShapeDtypeStruct((32, 1152), bf16),
        in_specs=[SM] + [VM] * 6 + [ANY],
        out_specs=VM,
        scratch_shapes=[pltpu.VMEM((NZ, 32, 1152), bf16)],
        compiler_params=params(8),
        cost_estimate=cost(32 * 1152 * 8, 1 << 20),
        name="sum_z",
    )(ids, *parts)


def wout_body(ids, mine, theirs, w_out, b_out, buf):
    x, core = ids[0] >> 4, ids[0] & 1
    for ref, c in ((mine, core), (theirs, 1 - core)):
        for i in range(2):
            at = pl.multiple_of(c * 64 + (x ^ i) * 32, 32)
            buf[pl.ds(at, 32), :] = ref[i * 32 : (i + 1) * 32, :].astype(f32)
    w_out[...] = buf[:, 0:1024]
    b_out[...] = buf[0:8, 1024:1152]


def weight_out(ids, mine, theirs):
    return pl.pallas_call(
        wout_body,
        out_shape=(jax.ShapeDtypeStruct((B, 1024), f32), jax.ShapeDtypeStruct((8, B), f32)),
        in_specs=[SM, VM, VM],
        out_specs=(VM, VM),
        scratch_shapes=[pltpu.VMEM((B, 1152), f32)],
        compiler_params=params(8),
        cost_estimate=cost(0, 1 << 20),
        name="weight_out",
    )(ids, mine, theirs)


def body(features, weight, bias_vector, adj_tiles, col_blocks, dest_blocks, out_grad):
    ids = jnp.stack([lax.axis_index("row"), lax.axis_index("feat")]).astype(jnp.int32)

    both = jnp.concatenate([features, row_send(features, dc=1)], axis=0)
    x0 = row_send(features, dx=1)
    lists = row_send(jnp.stack([col_blocks, dest_blocks]), dc=1)
    swap, both_a = tie(adj_tiles, both)
    more = row_send(swap, dc=1)

    pack, both_b = tie(pack_up(ids, weight, out_grad, bias_vector[None, :]), both_a)
    pair = jnp.concatenate([pack, feat_send(pack, dx=1)], axis=0)

    o3 = spin_send(both, 3, -1)
    o2 = spin_send(both, 2, -1)
    o1 = spin_send(both, 1, -1)
    o4 = spin_send(o3[:256], 1, -1)
    p3, p2 = row_send(o3, dx=1), row_send(o2, dx=1)
    p1, p4 = row_send(o1, dx=1), row_send(o4, dx=1)
    pair, o1 = tie(pair, o1)
    pair, o2 = tie(pair, o2)
    wu, wd = feat_send(pair, dy=1), feat_send(pair, dy=-1)
    wa, wb = feat_send(wu[:784], dy=1), feat_send(wd[784:], dy=-1)
    plan = plan_tiles(ids, col_blocks, dest_blocks, lists[0], lists[1])

    mine, theirs = aggregate(plan, adj_tiles, more, (both_b, x0, o4, o1, o2, o3, p4, p1, p2, p3))
    aggregated = (mine + row_send(theirs, dc=1)).astype(bf16).reshape(256, B)

    q = jnp.concatenate([aggregated, feat_send(aggregated, dx=1)], axis=0)
    w0, og, bias = lay_out(ids, (pair, wu, wd, wa, wb))
    pieces = (q, feat_send(q, dy=1), feat_send(q, dy=-1), feat_send(q, dy=2))
    hidden, prop, keep, give = middle(ids, pieces, w0, row_send(w0, dc=1), og, bias, weight)
    prop = prop.reshape(2, B, B)

    peer = row_send(prop, dc=1)
    got = row_send(give, dc=1)
    near, first, rest = spread(plan, adj_tiles, more, prop, peer, keep, got)
    came, came_rest = row_send(first, dx=1), row_send(rest, dx=1)
    quarter, t4 = meet(keep, got, came, near)

    r4 = spin_send(t4, 1)
    halves = jnp.concatenate([quarter, row_send(quarter, dc=1)], axis=0)
    d3, d2, d1 = (spin_send(halves, k, -1) for k in (3, 2, 1))
    d4 = spin_send(d3[:32], 1, -1)

    t = near[:12] + came_rest[:12].astype(f32)
    t0 = near[14:] + came_rest[12:].astype(f32)
    low = t[4:12].astype(bf16)
    r2, r1 = spin_send(low[:4], 2), spin_send(low[4:], 1)
    t3 = jnp.concatenate([t[:2] + r4.astype(f32), t[2:4]], axis=0).astype(bf16)
    r3 = spin_send(t3, 3)

    e = row_send(peer_rows(d1, d2, d3, low), dc=1)
    scale = float(256 * lax.axis_size("row")) ** (-0.5)
    total = sum_z(scale, ids, quarter, d1, d2, d3, d4, e, t3)
    two = jnp.concatenate([total, row_send(total, dx=1)], axis=0)
    weight_grad, bias_grad = weight_out(ids, two, row_send(two, dc=1))

    r = r1.astype(f32) + r2.astype(f32) + r3.astype(f32)
    out = t0 + r[:2] + row_send(r[2:], dc=1)
    return hidden, out.reshape(256, B), weight_grad, bias_grad[0]


def solution(mesh):
    in_specs = (
        P("row", "feat"),
        P("feat", None),
        P("feat"),
        P("row", None, None),
        P("row"),
        P("row"),
        P("row", "feat"),
    )
    out_specs = (P("row", "feat"), P("row", "feat"), P("feat", None), P("feat"))
    return jax.shard_map(body, mesh=mesh, in_specs=in_specs, out_specs=out_specs, check_vma=False)
```

```python
import functools

import jax
import jax.numpy as jnp
from jax import lax
from jax.experimental import pallas as pl
from jax.experimental.pallas import tpu as pltpu
from jax.sharding import PartitionSpec as P

bf16 = jnp.bfloat16
f32 = jnp.float32
B = 128
NZ = 8
VM = pl.BlockSpec(memory_space=pltpu.VMEM)
SM = pl.BlockSpec(memory_space=pltpu.SMEM)
HB = pl.BlockSpec(memory_space=pltpu.HBM)
ANY = pl.BlockSpec(memory_space=pl.ANY)


def row_send(v, dx=0, dz=0, dc=0):
    perm = []
    for i in range(32):
        x, z, c = i >> 4, (i >> 1) & 7, i & 1
        perm.append((i, ((x ^ dx) << 4) | (((z + dz) % NZ) << 1) | (c ^ dc)))
    return lax.ppermute(v, "row", perm)


def feat_send(v, dx=0, dy=0):
    return lax.ppermute(v, "feat", [(i, (((i >> 2) ^ dx) << 2) | ((i + dy) & 3)) for i in range(8)])


def params(mib=20):
    return pltpu.CompilerParams(vmem_limit_bytes=mib << 20)


def spin_send(v, k, way=1):
    perm = []
    for i in range(32):
        x, z, c = i >> 4, (i >> 1) & 7, i & 1
        perm.append((i, (x << 4) | (((z + way * (k if c == 0 else -k)) % NZ) << 1) | c))
    return lax.ppermute(v, "row", perm)


def tie(a, b):
    return lax.optimization_barrier((a, b))


def cost(flops, nbytes):
    return pl.CostEstimate(flops=flops, bytes_accessed=nbytes, transcendentals=0)


def pack_body(ids, w, og, bias, *refs):
    out, sem = refs[-2:]
    core = ids[0] & 1
    copies = []
    for m in range(4):
        at = pl.multiple_of(core * 512 + m * B, B)
        copies.append(
            pltpu.make_async_copy(w.at[:, pl.ds(at, B)], out.at[m * B : (m + 1) * B, :], sem.at[m])
        )
    copies.append(pltpu.make_async_copy(og, out.at[512:768, :], sem.at[4]))
    for c in copies:
        c.start()
    out[768:784, :] = jnp.broadcast_to(bias[...], (16, B))
    for c in copies:
        c.wait()


def pack_up(ids, w, og, bias, *ready):
    return pl.pallas_call(
        pack_body,
        out_shape=jax.ShapeDtypeStruct((784, B), bf16),
        in_specs=[SM, HB, HB, VM] + [ANY] * len(ready),
        out_specs=VM,
        scratch_shapes=[pltpu.SemaphoreType.DMA((5,))],
        compiler_params=params(4),
        cost_estimate=cost(0, 1 << 19),
        name="pack_up",
    )(ids, w, og, bias, *ready)


def pair_body(a, b, *refs):
    out = refs[-1]
    out[0:784, :] = a[...]
    out[784:1568, :] = b[...]


def pair_up(a, b, *ready):
    return pl.pallas_call(
        pair_body,
        out_shape=jax.ShapeDtypeStruct((1568, B), bf16),
        in_specs=[VM, VM] + [ANY] * len(ready),
        out_specs=VM,
        compiler_params=params(4),
        cost_estimate=cost(0, 1 << 19),
        name="pair_up",
    )(a, b, *ready)


def plan_body(ids, c0, d0, c1, d1, out):
    me = ids[0]
    mx, mz, mc = me >> 4, (me >> 1) & 7, me & 1
    for side, (cols, dest) in enumerate(((c0, d0), (c1, d1))):
        base = 8 + 72 * side

        def step(i, n, cols=cols, dest=dest, base=base, side=side):
            b = cols[i]
            o = b >> 1
            dx, dz, dc = (o >> 4) ^ mx, ((o >> 1) - mz) & 7, (o & 1) ^ mc
            k = jnp.where(mc == 0, dz, NZ - dz)
            edge = (dz & 3) == 0
            held = jnp.where(edge, 1 - dc, jnp.where(k <= 3, 1, 0))
            j = jnp.where(edge, jnp.where(dz == 0, 7, 6), (3 - k) * 2 + dc)
            slot = dx * 16 + j * 2 + (b & 1)
            out[base + n] = i | (slot << 8) | ((dest[i] + 2 * side) << 16)
            return n + held

        n = lax.fori_loop(0, 64, step, 0)
        for u in range(4):
            out[base + n + u] = (32 << 8) | (4 << 16)
        out[side] = (n + 3) >> 2


def plan_tiles(ids, c0, d0, c1, d1):
    return pl.pallas_call(
        plan_body,
        out_shape=jax.ShapeDtypeStruct((160,), jnp.int32),
        in_specs=[SM] * 5,
        out_specs=SM,
        compiler_params=params(4),
        cost_estimate=cost(10000, 4096),
        name="plan_tiles",
    )(ids, c0, d0, c1, d1)


def each_tile(plan, tiles, more, use):
    for side, ref in enumerate((tiles, more)):
        def step(g, carry, side=side, ref=ref):
            for u in range(4):
                e = plan[8 + 72 * side + g * 4 + u]
                use(ref[e & 255], (e >> 8) & 255, e >> 16)
            return carry

        lax.fori_loop(0, plan[side], step, 0)


def agg_body(plan, tiles, more, *refs):
    pieces, mine, theirs, src, acc, sem = refs[0:10], refs[10], refs[11], refs[12], refs[13], refs[14]
    both, x0, o4, o1, o2, o3, p4, p1, p2, p3 = pieces
    copies = []

    def put(dx, j, v):
        n = v.shape[0]
        at = dx * 16 + j * 2
        copies.append(pltpu.make_async_copy(v, src.at[at : at + n], sem.at[len(copies)]))
        copies[-1].start()

    for dx, (v3, v2, v1, v4, v0) in enumerate(((o3, o2, o1, o4, both.at[0:2]), (p3, p2, p1, p4, x0))):
        for j, v in ((0, v3), (2, v2), (4, v1), (6, v4), (7, v0)):
            put(dx, j, v)
    acc[...] = jnp.zeros_like(acc)
    src[32] = jnp.zeros((B, B), bf16)
    for c in copies:
        c.wait()

    def use(tile, slot, dest):
        acc[dest] += jnp.dot(tile, src[slot], preferred_element_type=f32)

    each_tile(plan, tiles, more, use)
    mine[...] = acc[0:2]
    theirs[...] = acc[2:4]


def aggregate(plan, tiles, more, pieces):
    parts = [v.reshape(-1, B, B) for v in pieces]
    return pl.pallas_call(
        agg_body,
        out_shape=(jax.ShapeDtypeStruct((2, B, B), f32), jax.ShapeDtypeStruct((2, B, B), f32)),
        in_specs=[SM, VM, VM] + [HB] * 10,
        out_specs=(VM, VM),
        scratch_shapes=[
            pltpu.VMEM((33, B, B), bf16),
            pltpu.VMEM((5, B, B), f32),
            pltpu.SemaphoreType.DMA((10,)),
        ],
        compiler_params=params(12),
        cost_estimate=cost(2 * 64 * B**3, 4 << 20),
        name="aggregate",
    )(plan, tiles, more, *parts)


def lay_body(ids, *refs):
    own = refs[0:5]
    w_out, og_out, bias_out, rows, sem = refs[5:10]
    yy, xx = ids[1] & 3, ids[1] >> 2
    copies, cols = [], []

    def put(src, dst):
        copies.append(pltpu.make_async_copy(src, dst, sem.at[len(copies)]))
        copies[-1].start()

    for j, off in enumerate((0, -1, 1, 2)):
        for i in range(2):
            k = j * 2 + i
            n, base = (j, i * 784) if j < 3 else (3 + i, 0)
            col = pl.multiple_of((((xx ^ i) << 2) | ((yy + off) & 3)) * B, B)
            cols.append(col)
            for m in range(4):
                put(own[n].at[pl.ds(base + m * B, B), :], w_out.at[pl.ds(k * B, B), pl.ds(m * B, B)])
            put(own[n].at[pl.ds(base + 512, 256), :], og_out.at[:, pl.ds(col, B)])
            put(own[n].at[pl.ds(base + 768, 16), :], rows.at[k])
    for c in copies:
        c.wait()
    for k in range(8):
        bias_out[:, pl.ds(cols[k], B)] = rows[k].astype(f32)[0:8]


def lay_out(ids, own):
    return pl.pallas_call(
        lay_body,
        out_shape=(
            jax.ShapeDtypeStruct((1024, 512), bf16),
            jax.ShapeDtypeStruct((256, 1024), bf16),
            jax.ShapeDtypeStruct((8, 1024), f32),
        ),
        in_specs=[SM] + [HB] * 5,
        out_specs=(VM, VM, VM),
        scratch_shapes=[pltpu.VMEM((8, 16, B), bf16), pltpu.SemaphoreType.DMA((48,))],
        compiler_params=params(8),
        cost_estimate=cost(0, 3 << 20),
        name="lay_out",
    )(ids, *own)


def mid_body(ids, p0, p1, p2, p3, w0, w1, og, bias, w_own, hidden, prop, keep, give, agg, pre, gp, wp):
    x, core = ids[0] >> 4, ids[0] & 1
    for j, p in enumerate((p0, p1, p2, p3)):
        for i in range(2):
            agg[:, (j * 2 + i) * B : (j * 2 + i + 1) * B] = p[i * 256 : (i + 1) * 256, :]
    for w, c in ((w0, core), (w1, 1 - core)):
        for m in range(2):
            cols = pl.ds(pl.multiple_of(c * 512 + m * 256, 256), 256)
            v = jnp.dot(agg[...], w[:, m * 256 : (m + 1) * 256], preferred_element_type=f32)
            v = v + bias[0:1, cols]
            pre[:, cols] = v
            s = jax.nn.sigmoid(v)
            gp[:, cols] = (og[:, cols].astype(f32) * s * (1.0 + v * (1.0 - s))).astype(bf16)
    mine = pl.ds(pl.multiple_of(ids[1] * B, B), B)
    v = pre[:, mine]
    hidden[...] = v * jax.nn.sigmoid(v)
    prop[...] = lax.dot_general(
        gp[...], w_own[...], (((1,), (1,)), ((), ())), preferred_element_type=f32
    ).astype(bf16)
    wp[:, 0:1024] = lax.dot_general(
        agg[:, 0:B], gp[...], (((0,), (0,)), ((), ())), preferred_element_type=f32
    )
    total = jnp.sum(gp[:, mine].astype(f32), axis=0, keepdims=True)
    wp[:, 1024:1152] = jnp.broadcast_to(total, (B, B))
    for ref, c in ((keep, core), (give, 1 - core)):
        for i in range(2):
            ref[i * 32 : (i + 1) * 32, :] = wp[pl.ds(pl.multiple_of(c * 64 + (x ^ i) * 32, 32), 32), :]


def middle(ids, pieces, w0, w1, og, bias, w_own):
    return pl.pallas_call(
        mid_body,
        out_shape=(
            jax.ShapeDtypeStruct((256, B), f32),
            jax.ShapeDtypeStruct((256, B), bf16),
            jax.ShapeDtypeStruct((64, 1152), f32),
            jax.ShapeDtypeStruct((64, 1152), f32),
        ),
        in_specs=[SM] + [VM] * 9,
        out_specs=(VM, VM, VM, VM),
        scratch_shapes=[
            pltpu.VMEM((256, 1024), bf16),
            pltpu.VMEM((256, 1024), f32),
            pltpu.VMEM((256, 1024), bf16),
            pltpu.VMEM((B, 1152), f32),
        ],
        compiler_params=params(),
        cost_estimate=cost(2 * 256 * 1024 * 1280, 5 << 20),
        name="middle",
    )(ids, *pieces, w0, w1, og, bias, w_own)


def spread_body(plan, tiles, more, prop, peer, send, near, first, rest, acc, both):
    acc[...] = jnp.zeros_like(acc)
    both[0:2] = prop[...]
    both[2:4] = peer[...]
    both[4] = jnp.zeros((B, B), bf16)

    def use(tile, slot, dest):
        acc[slot] += lax.dot_general(
            tile, both[dest], (((0,), (0,)), ((), ())), preferred_element_type=f32
        )

    each_tile(plan, tiles, more, use)
    near[...] = acc[0:16]
    first[...] = acc[28:30].astype(bf16)
    rest[0:12] = acc[16:28].astype(bf16)
    rest[12:14] = acc[30:32].astype(bf16)


def spread(plan, tiles, more, prop, peer, send):
    return pl.pallas_call(
        spread_body,
        out_shape=(
            jax.ShapeDtypeStruct((16, B, B), f32),
            jax.ShapeDtypeStruct((2, B, B), bf16),
            jax.ShapeDtypeStruct((14, B, B), bf16),
        ),
        in_specs=[SM] + [VM] * 4 + [ANY],
        out_specs=(VM, VM, VM),
        scratch_shapes=[pltpu.VMEM((33, B, B), f32), pltpu.VMEM((5, B, B), bf16)],
        compiler_params=params(12),
        cost_estimate=cost(2 * 64 * B**3, 6 << 20),
        name="spread",
    )(plan, tiles, more, prop, peer, send)


def rows_body(d1, d2, d3, t, out):
    for n, d in enumerate((d1, d2, d3)):
        out[32 * n : 32 * n + 32, :] = d[32:64, :]


def peer_rows(d1, d2, d3, t):
    return pl.pallas_call(
        rows_body,
        out_shape=jax.ShapeDtypeStruct((96, 1152), bf16),
        in_specs=[VM] * 3 + [ANY],
        out_specs=VM,
        compiler_params=params(4),
        cost_estimate=cost(0, 1 << 18),
        name="peer_rows",
    )(d1, d2, d3, t)


def sum_body(scale, ids, own, d1, d2, d3, d4, e, t, out, buf):
    core, z = ids[0] & 1, (ids[0] >> 1) & 7
    buf[0] = own[...]
    buf[4] = d4[...]
    for k, d in ((1, d1), (2, d2), (3, d3)):
        mine = jnp.where(core == 0, k, NZ - k)
        buf[mine] = d[0:32, :]
        buf[NZ - mine] = e[(k - 1) * 32 : k * 32, :]
    acc = buf[(NZ - z) & 7].astype(f32)
    for n in range(1, NZ):
        acc = acc + buf[(n - z) & 7].astype(f32)
    out[...] = (acc * scale).astype(bf16)


def sum_z(scale, ids, *parts):
    return pl.pallas_call(
        functools.partial(sum_body, scale),
        out_shape=jax.ShapeDtypeStruct((32, 1152), bf16),
        in_specs=[SM] + [VM] * 6 + [ANY],
        out_specs=VM,
        scratch_shapes=[pltpu.VMEM((NZ, 32, 1152), bf16)],
        compiler_params=params(8),
        cost_estimate=cost(32 * 1152 * 8, 1 << 20),
        name="sum_z",
    )(ids, *parts)


def wout_body(ids, mine, theirs, w_out, b_out, buf):
    x, core = ids[0] >> 4, ids[0] & 1
    for ref, c in ((mine, core), (theirs, 1 - core)):
        for i in range(2):
            at = pl.multiple_of(c * 64 + (x ^ i) * 32, 32)
            buf[pl.ds(at, 32), :] = ref[i * 32 : (i + 1) * 32, :].astype(f32)
    w_out[...] = buf[:, 0:1024]
    b_out[...] = buf[0:8, 1024:1152]


def weight_out(ids, mine, theirs):
    return pl.pallas_call(
        wout_body,
        out_shape=(jax.ShapeDtypeStruct((B, 1024), f32), jax.ShapeDtypeStruct((8, B), f32)),
        in_specs=[SM, VM, VM],
        out_specs=(VM, VM),
        scratch_shapes=[pltpu.VMEM((B, 1152), f32)],
        compiler_params=params(8),
        cost_estimate=cost(0, 1 << 20),
        name="weight_out",
    )(ids, mine, theirs)


def body(features, weight, bias_vector, adj_tiles, col_blocks, dest_blocks, out_grad):
    ids = jnp.stack([lax.axis_index("row"), lax.axis_index("feat")]).astype(jnp.int32)

    both = jnp.concatenate([features, row_send(features, dc=1)], axis=0)
    x0 = row_send(features, dx=1)
    lists = row_send(jnp.stack([col_blocks, dest_blocks]), dc=1)
    swap, both_a = tie(adj_tiles, both)
    more = row_send(swap, dc=1)
    o3 = spin_send(both, 3, -1)
    o2 = spin_send(both, 2, -1)
    o1 = spin_send(both, 1, -1)
    o4 = spin_send(o3[:256], 1, -1)
    p3, p2 = row_send(o3, dx=1), row_send(o2, dx=1)
    p1, p4 = row_send(o1, dx=1), row_send(o4, dx=1)
    plan = plan_tiles(ids, col_blocks, dest_blocks, lists[0], lists[1])

    pack = pack_up(ids, weight, out_grad, bias_vector[None, :], o1, o2, o3)
    pair = pair_up(pack, feat_send(pack, dx=1), p1, p2, p3, p4, plan)
    wu, wd = feat_send(pair, dy=1), feat_send(pair, dy=-1)
    wa, wb = feat_send(wu[:784], dy=1), feat_send(wd[784:], dy=-1)

    mine, theirs = aggregate(plan, adj_tiles, more, (both_a, x0, o4, o1, o2, o3, p4, p1, p2, p3))
    aggregated = (mine + row_send(theirs, dc=1)).astype(bf16).reshape(256, B)

    q = jnp.concatenate([aggregated, feat_send(aggregated, dx=1)], axis=0)
    w0, og, bias = lay_out(ids, (pair, wu, wd, wa, wb))
    pieces = (q, feat_send(q, dy=1), feat_send(q, dy=-1), feat_send(q, dy=2))
    hidden, prop, keep, give = middle(ids, pieces, w0, row_send(w0, dc=1), og, bias, weight)
    prop = prop.reshape(2, B, B)

    peer = row_send(prop, dc=1)
    got = row_send(give, dc=1)
    send = (keep[32:] + got[32:]).astype(bf16)
    got_x = row_send(send, dx=1)
    near, first, rest = spread(plan, adj_tiles, more, prop, peer, send)
    came, came_rest = row_send(first, dx=1), row_send(rest, dx=1)
    quarter = (keep[:32] + got[:32] + got_x.astype(f32)).astype(bf16)

    r4 = spin_send((near[12:14] + came.astype(f32)).astype(bf16), 1)
    halves = jnp.concatenate([quarter, row_send(quarter, dc=1)], axis=0)
    d3, d2, d1 = (spin_send(halves, k, -1) for k in (3, 2, 1))
    d4 = spin_send(d3[:32], 1, -1)

    t = near[:12] + came_rest[:12].astype(f32)
    t0 = near[14:] + came_rest[12:].astype(f32)
    low = t[4:12].astype(bf16)
    r2, r1 = spin_send(low[:4], 2), spin_send(low[4:], 1)
    t3 = jnp.concatenate([t[:2] + r4.astype(f32), t[2:4]], axis=0).astype(bf16)
    r3 = spin_send(t3, 3)

    e = row_send(peer_rows(d1, d2, d3, low), dc=1)
    scale = float(256 * lax.axis_size("row")) ** (-0.5)
    total = sum_z(scale, ids, quarter, d1, d2, d3, d4, e, t3)
    two = jnp.concatenate([total, row_send(total, dx=1)], axis=0)
    weight_grad, bias_grad = weight_out(ids, two, row_send(two, dc=1))

    r = r1.astype(f32) + r2.astype(f32) + r3.astype(f32)
    out = t0 + r[:2] + row_send(r[2:], dc=1)
    return hidden, out.reshape(256, B), weight_grad, bias_grad[0]


def solution(mesh):
    in_specs = (
        P("row", "feat"),
        P("feat", None),
        P("feat"),
        P("row", None, None),
        P("row"),
        P("row"),
        P("row", "feat"),
    )
    out_specs = (P("row", "feat"), P("row", "feat"), P("feat", None), P("feat"))
    return jax.shard_map(body, mesh=mesh, in_specs=in_specs, out_specs=out_specs, check_vma=False)
```

```python
import functools

import jax
import jax.numpy as jnp
from jax import lax
from jax.experimental import pallas as pl
from jax.experimental.pallas import tpu as pltpu
from jax.sharding import PartitionSpec as P

bf16 = jnp.bfloat16
f32 = jnp.float32
B = 128
NZ = 8
VM = pl.BlockSpec(memory_space=pltpu.VMEM)
SM = pl.BlockSpec(memory_space=pltpu.SMEM)
HB = pl.BlockSpec(memory_space=pltpu.HBM)
ANY = pl.BlockSpec(memory_space=pl.ANY)


def row_send(v, dx=0, dz=0, dc=0):
    perm = []
    for i in range(32):
        x, z, c = i >> 4, (i >> 1) & 7, i & 1
        perm.append((i, ((x ^ dx) << 4) | (((z + dz) % NZ) << 1) | (c ^ dc)))
    return lax.ppermute(v, "row", perm)


def feat_send(v, dx=0, dy=0):
    return lax.ppermute(v, "feat", [(i, (((i >> 2) ^ dx) << 2) | ((i + dy) & 3)) for i in range(8)])


def params(mib=20):
    return pltpu.CompilerParams(vmem_limit_bytes=mib << 20)


def spin_send(v, k, way=1):
    perm = []
    for i in range(32):
        x, z, c = i >> 4, (i >> 1) & 7, i & 1
        perm.append((i, (x << 4) | (((z + way * (k if c == 0 else -k)) % NZ) << 1) | c))
    return lax.ppermute(v, "row", perm)


def tie(a, b):
    return lax.optimization_barrier((a, b))


def cost(flops, nbytes):
    return pl.CostEstimate(flops=flops, bytes_accessed=nbytes, transcendentals=0)


def pack_body(ids, w, og, bias, *refs):
    out, sem = refs[-2:]
    core = ids[0] & 1
    copies = []
    for m in range(4):
        at = pl.multiple_of(core * 512 + m * B, B)
        copies.append(
            pltpu.make_async_copy(w.at[:, pl.ds(at, B)], out.at[m * B : (m + 1) * B, :], sem.at[m])
        )
    copies.append(pltpu.make_async_copy(og, out.at[512:768, :], sem.at[4]))
    for c in copies:
        c.start()
    out[768:784, :] = jnp.broadcast_to(bias[...], (16, B))
    for c in copies:
        c.wait()


def pack_up(ids, w, og, bias, *ready):
    return pl.pallas_call(
        pack_body,
        out_shape=jax.ShapeDtypeStruct((784, B), bf16),
        in_specs=[SM, HB, HB, VM] + [ANY] * len(ready),
        out_specs=VM,
        scratch_shapes=[pltpu.SemaphoreType.DMA((5,))],
        compiler_params=params(4),
        cost_estimate=cost(0, 1 << 19),
        name="pack_up",
    )(ids, w, og, bias, *ready)


def append_body(a, b, *refs):
    out = refs[-1]
    rows = a.shape[0]
    out[0:rows, :] = a[...]
    out[rows:, :] = b[0 : out.shape[0] - rows, :]


def append(n, a, b, *ready):
    return pl.pallas_call(
        append_body,
        out_shape=jax.ShapeDtypeStruct((n, a.shape[1]), a.dtype),
        in_specs=[VM, VM] + [ANY] * len(ready),
        out_specs=VM,
        compiler_params=params(4),
        cost_estimate=cost(0, 1 << 18),
        name="append",
    )(a, b, *ready)


def settle_body(mine, came, u, d, agg, a, b):
    agg[...] = (mine[...] + came[...]).astype(bf16)
    a[...] = u[0:784, :]
    b[...] = d[784:1568, :]


def settle(mine, came, u, d):
    half = jax.ShapeDtypeStruct((784, B), bf16)
    return pl.pallas_call(
        settle_body,
        out_shape=(jax.ShapeDtypeStruct((2, B, B), bf16), half, half),
        in_specs=[VM] * 4,
        out_specs=(VM, VM, VM),
        compiler_params=params(4),
        cost_estimate=cost(0, 1 << 18),
        name="settle",
    )(mine, came, u, d)


def plan_body(ids, c0, d0, c1, d1, out):
    me = ids[0]
    mx, mz, mc = me >> 4, (me >> 1) & 7, me & 1
    for side, (cols, dest) in enumerate(((c0, d0), (c1, d1))):
        base = 8 + 72 * side

        def step(i, n, cols=cols, dest=dest, base=base, side=side):
            b = cols[i]
            o = b >> 1
            dx, dz, dc = (o >> 4) ^ mx, ((o >> 1) - mz) & 7, (o & 1) ^ mc
            k = jnp.where(mc == 0, dz, NZ - dz)
            edge = (dz & 3) == 0
            held = jnp.where(edge, 1 - dc, jnp.where(k <= 3, 1, 0))
            j = jnp.where(edge, jnp.where(dz == 0, 7, 6), (3 - k) * 2 + dc)
            slot = dx * 16 + j * 2 + (b & 1)
            out[base + n] = i | (slot << 8) | ((dest[i] + 2 * side) << 16)
            return n + held

        n = lax.fori_loop(0, 64, step, 0, unroll=8)
        for u in range(4):
            out[base + n + u] = (32 << 8) | (4 << 16)
        out[side] = (n + 3) >> 2


def plan_tiles(ids, c0, d0, c1, d1):
    return pl.pallas_call(
        plan_body,
        out_shape=jax.ShapeDtypeStruct((160,), jnp.int32),
        in_specs=[SM] * 5,
        out_specs=SM,
        compiler_params=params(4),
        cost_estimate=cost(10000, 4096),
        name="plan_tiles",
    )(ids, c0, d0, c1, d1)


def each_tile(plan, tiles, more, use):
    for side, ref in enumerate((tiles, more)):
        def step(g, carry, side=side, ref=ref):
            for u in range(4):
                e = plan[8 + 72 * side + g * 4 + u]
                use(ref[e & 255], (e >> 8) & 255, e >> 16)
            return carry

        lax.fori_loop(0, plan[side], step, 0)


def agg_body(plan, tiles, more, *refs):
    mine, theirs, src, acc, sem = refs[8:]
    both, x0, o14, o2, o3, p14, p2, p3 = refs[0:8]
    copies = []

    def put(dx, j, v):
        n = v.shape[0]
        at = dx * 16 + j * 2
        copies.append(pltpu.make_async_copy(v, src.at[at : at + n], sem.at[len(copies)]))
        copies[-1].start()

    for dx, (v3, v2, v14, v0) in enumerate(((o3, o2, o14, both.at[0:2]), (p3, p2, p14, x0))):
        for j, v in ((0, v3), (2, v2), (4, v14), (7, v0)):
            put(dx, j, v)
    acc[...] = jnp.zeros_like(acc)
    src[32] = jnp.zeros((B, B), bf16)
    for c in copies:
        c.wait()

    def use(tile, slot, dest):
        acc[dest] += jnp.dot(tile, src[slot], preferred_element_type=f32)

    each_tile(plan, tiles, more, use)
    mine[...] = acc[0:2]
    theirs[...] = acc[2:4]


def aggregate(plan, tiles, more, pieces):
    parts = [v.reshape(-1, B, B) for v in pieces]
    return pl.pallas_call(
        agg_body,
        out_shape=(jax.ShapeDtypeStruct((2, B, B), f32), jax.ShapeDtypeStruct((2, B, B), f32)),
        in_specs=[SM, VM, VM] + [HB] * 8,
        out_specs=(VM, VM),
        scratch_shapes=[
            pltpu.VMEM((33, B, B), bf16),
            pltpu.VMEM((5, B, B), f32),
            pltpu.SemaphoreType.DMA((8,)),
        ],
        compiler_params=params(12),
        cost_estimate=cost(2 * 64 * B**3, 4 << 20),
        name="aggregate",
    )(plan, tiles, more, *parts)


def lay_body(ids, *refs):
    own = refs[0:5]
    w_out, og_out, bias_out, rows, sem = refs[5:10]
    yy, xx = ids[1] & 3, ids[1] >> 2
    copies, cols = [], []

    def put(src, dst):
        copies.append(pltpu.make_async_copy(src, dst, sem.at[len(copies)]))
        copies[-1].start()

    for j, off in enumerate((0, -1, 1, 2)):
        for i in range(2):
            k = j * 2 + i
            n, base = (j, i * 784) if j < 3 else (3 + i, 0)
            col = pl.multiple_of((((xx ^ i) << 2) | ((yy + off) & 3)) * B, B)
            cols.append(col)
            for m in range(4):
                put(own[n].at[pl.ds(base + m * B, B), :], w_out.at[pl.ds(k * B, B), pl.ds(m * B, B)])
            put(own[n].at[pl.ds(base + 512, 256), :], og_out.at[:, pl.ds(col, B)])
            put(own[n].at[pl.ds(base + 768, 16), :], rows.at[k])
    for c in copies:
        c.wait()
    for k in range(8):
        bias_out[:, pl.ds(cols[k], B)] = rows[k].astype(f32)[0:8]


def lay_out(ids, own):
    return pl.pallas_call(
        lay_body,
        out_shape=(
            jax.ShapeDtypeStruct((1024, 512), bf16),
            jax.ShapeDtypeStruct((256, 1024), bf16),
            jax.ShapeDtypeStruct((8, 1024), f32),
        ),
        in_specs=[SM] + [HB] * 5,
        out_specs=(VM, VM, VM),
        scratch_shapes=[pltpu.VMEM((8, 16, B), bf16), pltpu.SemaphoreType.DMA((48,))],
        compiler_params=params(8),
        cost_estimate=cost(0, 3 << 20),
        name="lay_out",
    )(ids, *own)


def mid_body(ids, p0, p1, p2, p3, w0, w1, og, bias, w_own, hidden, prop, keep, give, agg, pre, gp, wp):
    x, core = ids[0] >> 4, ids[0] & 1
    for j, p in enumerate((p0, p1, p2, p3)):
        for i in range(2):
            agg[:, (j * 2 + i) * B : (j * 2 + i + 1) * B] = p[i * 256 : (i + 1) * 256, :]
    for w, c in ((w0, core), (w1, 1 - core)):
        for m in range(2):
            cols = pl.ds(pl.multiple_of(c * 512 + m * 256, 256), 256)
            v = jnp.dot(agg[...], w[:, m * 256 : (m + 1) * 256], preferred_element_type=f32)
            v = v + bias[0:1, cols]
            pre[:, cols] = v
            s = jax.nn.sigmoid(v)
            gp[:, cols] = (og[:, cols].astype(f32) * s * (1.0 + v * (1.0 - s))).astype(bf16)
    mine = pl.ds(pl.multiple_of(ids[1] * B, B), B)
    v = pre[:, mine]
    hidden[...] = v * jax.nn.sigmoid(v)
    prop[...] = lax.dot_general(
        gp[...], w_own[...], (((1,), (1,)), ((), ())), preferred_element_type=f32
    ).astype(bf16)
    wp[:, 0:1024] = lax.dot_general(
        agg[:, 0:B], gp[...], (((0,), (0,)), ((), ())), preferred_element_type=f32
    )
    total = jnp.sum(gp[:, mine].astype(f32), axis=0, keepdims=True)
    wp[:, 1024:1152] = jnp.broadcast_to(total, (B, B))
    for ref, c in ((keep, core), (give, 1 - core)):
        for i in range(2):
            ref[i * 32 : (i + 1) * 32, :] = wp[pl.ds(pl.multiple_of(c * 64 + (x ^ i) * 32, 32), 32), :]


def middle(ids, pieces, w0, w1, og, bias, w_own):
    return pl.pallas_call(
        mid_body,
        out_shape=(
            jax.ShapeDtypeStruct((256, B), f32),
            jax.ShapeDtypeStruct((256, B), bf16),
            jax.ShapeDtypeStruct((64, 1152), f32),
            jax.ShapeDtypeStruct((64, 1152), f32),
        ),
        in_specs=[SM] + [VM] * 9,
        out_specs=(VM, VM, VM, VM),
        scratch_shapes=[
            pltpu.VMEM((256, 1024), bf16),
            pltpu.VMEM((256, 1024), f32),
            pltpu.VMEM((256, 1024), bf16),
            pltpu.VMEM((B, 1152), f32),
        ],
        compiler_params=params(),
        cost_estimate=cost(2 * 256 * 1024 * 1280, 5 << 20),
        name="middle",
    )(ids, *pieces, w0, w1, og, bias, w_own)


def spread_body(plan, tiles, more, prop, peer, send, near, far, acc, both):
    acc[...] = jnp.zeros_like(acc)
    both[0:2] = prop[...]
    both[2:4] = peer[...]
    both[4] = jnp.zeros((B, B), bf16)

    def use(tile, slot, dest):
        acc[slot] += lax.dot_general(
            tile, both[dest], (((0,), (0,)), ((), ())), preferred_element_type=f32
        )

    each_tile(plan, tiles, more, use)
    near[...] = acc[0:16]
    far[...] = acc[16:32].astype(bf16)


def spread(plan, tiles, more, prop, peer, send):
    return pl.pallas_call(
        spread_body,
        out_shape=(
            jax.ShapeDtypeStruct((16, B, B), f32),
            jax.ShapeDtypeStruct((16, B, B), bf16),
        ),
        in_specs=[SM] + [VM] * 4 + [ANY],
        out_specs=(VM, VM),
        scratch_shapes=[pltpu.VMEM((33, B, B), f32), pltpu.VMEM((5, B, B), bf16)],
        compiler_params=params(12),
        cost_estimate=cost(2 * 64 * B**3, 6 << 20),
        name="spread",
    )(plan, tiles, more, prop, peer, send)


def quarter_body(keep, got, came, far, out):
    out[...] = (keep[0:32, :] + got[0:32, :] + came[...].astype(f32)).astype(bf16)


def quarter_up(keep, got, came, far):
    return pl.pallas_call(
        quarter_body,
        out_shape=jax.ShapeDtypeStruct((32, 1152), bf16),
        in_specs=[VM] * 3 + [ANY],
        out_specs=VM,
        compiler_params=params(4),
        cost_estimate=cost(0, 1 << 18),
        name="quarter_up",
    )(keep, got, came, far)


def join_body(near, came, ready, t14, t2, t3, t0):
    t3[...] = near[0:4] + came[0:4].astype(f32)
    t2[...] = (near[4:8] + came[4:8].astype(f32)).astype(bf16)
    t14[...] = (near[8:14] + came[8:14].astype(f32)).astype(bf16)
    t0[...] = near[14:16] + came[14:16].astype(f32)


def join(near, came, ready):
    return pl.pallas_call(
        join_body,
        out_shape=(
            jax.ShapeDtypeStruct((6, B, B), bf16),
            jax.ShapeDtypeStruct((4, B, B), bf16),
            jax.ShapeDtypeStruct((4, B, B), f32),
            jax.ShapeDtypeStruct((2, B, B), f32),
        ),
        in_specs=[VM, VM, ANY],
        out_specs=(VM, VM, VM, VM),
        compiler_params=params(8),
        cost_estimate=cost(0, 2 << 20),
        name="join",
    )(near, came, ready)


def ride_body(t3, r14, ready, out):
    out[0:2] = (t3[0:2] + r14[4:6].astype(f32)).astype(bf16)
    out[2:4] = t3[2:4].astype(bf16)


def ride(t3, r14, ready):
    return pl.pallas_call(
        ride_body,
        out_shape=jax.ShapeDtypeStruct((4, B, B), bf16),
        in_specs=[VM, VM, ANY],
        out_specs=VM,
        compiler_params=params(4),
        cost_estimate=cost(0, 1 << 18),
        name="ride",
    )(t3, r14, ready)


def rows_body(d1, d2, d3, t, out):
    for n, d in enumerate((d1, d2, d3)):
        out[32 * n : 32 * n + 32, :] = d[32:64, :]


def peer_rows(d1, d2, d3, t):
    return pl.pallas_call(
        rows_body,
        out_shape=jax.ShapeDtypeStruct((96, 1152), bf16),
        in_specs=[VM] * 3 + [ANY],
        out_specs=VM,
        compiler_params=params(4),
        cost_estimate=cost(0, 1 << 18),
        name="peer_rows",
    )(d1, d2, d3, t)


def sum_body(scale, ids, own, d1, d2, d3, e, t, out, buf):
    core, z = ids[0] & 1, (ids[0] >> 1) & 7
    buf[0] = own[...]
    buf[4] = d1[64:96, :]
    for k, d in ((1, d1), (2, d2), (3, d3)):
        mine = jnp.where(core == 0, k, NZ - k)
        buf[mine] = d[0:32, :]
        buf[NZ - mine] = e[(k - 1) * 32 : k * 32, :]
    acc = buf[(NZ - z) & 7].astype(f32)
    for n in range(1, NZ):
        acc = acc + buf[(n - z) & 7].astype(f32)
    out[...] = (acc * scale).astype(bf16)


def sum_z(scale, ids, *parts):
    return pl.pallas_call(
        functools.partial(sum_body, scale),
        out_shape=jax.ShapeDtypeStruct((32, 1152), bf16),
        in_specs=[SM] + [VM] * 5 + [ANY],
        out_specs=VM,
        scratch_shapes=[pltpu.VMEM((NZ, 32, 1152), bf16)],
        compiler_params=params(8),
        cost_estimate=cost(32 * 1152 * 8, 1 << 20),
        name="sum_z",
    )(ids, *parts)


def wout_body(ids, mine, theirs, w_out, b_out, buf):
    x, core = ids[0] >> 4, ids[0] & 1
    for ref, c in ((mine, core), (theirs, 1 - core)):
        for i in range(2):
            at = pl.multiple_of(c * 64 + (x ^ i) * 32, 32)
            buf[pl.ds(at, 32), :] = ref[i * 32 : (i + 1) * 32, :].astype(f32)
    w_out[...] = buf[:, 0:1024]
    b_out[...] = buf[0:8, 1024:1152]


def weight_out(ids, mine, theirs):
    return pl.pallas_call(
        wout_body,
        out_shape=(jax.ShapeDtypeStruct((B, 1024), f32), jax.ShapeDtypeStruct((8, B), f32)),
        in_specs=[SM, VM, VM],
        out_specs=(VM, VM),
        scratch_shapes=[pltpu.VMEM((B, 1152), f32)],
        compiler_params=params(8),
        cost_estimate=cost(0, 1 << 20),
        name="weight_out",
    )(ids, mine, theirs)


def body(features, weight, bias_vector, adj_tiles, col_blocks, dest_blocks, out_grad):
    ids = jnp.stack([lax.axis_index("row"), lax.axis_index("feat")]).astype(jnp.int32)

    both = jnp.concatenate([features, row_send(features, dc=1)], axis=0)
    x0 = row_send(features, dx=1)
    lists = row_send(jnp.stack([col_blocks, dest_blocks]), dc=1)
    swap, both_a = tie(adj_tiles, both)
    more = row_send(swap, dc=1)
    o3, o2 = spin_send(both, 3, -1), spin_send(both, 2, -1)
    plan = plan_tiles(ids, col_blocks, dest_blocks, lists[0], lists[1])
    o14 = spin_send(append(768, both, o3, o2, x0, plan), 1, -1)
    p3, p2, p14 = row_send(o3, dx=1), row_send(o2, dx=1), row_send(o14, dx=1)

    pack = pack_up(ids, weight, out_grad, bias_vector[None, :], plan)
    pair = append(1568, pack, feat_send(pack, dx=1), o14)
    wu, wd = feat_send(pair, dy=1), feat_send(pair, dy=-1)

    mine, theirs = aggregate(plan, adj_tiles, more, (both_a, x0, o14, o2, o3, p14, p2, p3))
    aggregated, wa, wb = settle(mine, row_send(theirs, dc=1), wu, wd)
    aggregated = aggregated.reshape(256, B)
    wa, wb = feat_send(wa, dy=1), feat_send(wb, dy=-1)

    q = jnp.concatenate([aggregated, feat_send(aggregated, dx=1)], axis=0)
    w0, og, bias = lay_out(ids, (pair, wu, wd, wa, wb))
    pieces = (q, feat_send(q, dy=1), feat_send(q, dy=-1), feat_send(q, dy=2))
    hidden, prop, keep, give = middle(ids, pieces, w0, row_send(w0, dc=1), og, bias, weight)
    prop = prop.reshape(2, B, B)

    peer = row_send(prop, dc=1)
    got = row_send(give, dc=1)
    send = (keep[32:] + got[32:]).astype(bf16)
    got_x = row_send(send, dx=1)
    near, far = spread(plan, adj_tiles, more, prop, peer, send)
    came = row_send(far, dx=1)
    quarter = quarter_up(keep, got, got_x, far)
    halves = jnp.concatenate([quarter, row_send(quarter, dc=1)], axis=0)
    d3, d2 = spin_send(halves, 3, -1), spin_send(halves, 2, -1)
    last = append(96, halves, d3, d2)
    d1 = spin_send(last, 1, -1)

    t14, t2, t3, t0 = join(near, came, last)
    r14, r2 = spin_send(t14, 1), spin_send(t2, 2)
    t3 = ride(t3, r14, r2)
    r3 = spin_send(t3, 3)

    e = row_send(peer_rows(d1, d2, d3, t2), dc=1)
    scale = float(256 * lax.axis_size("row")) ** (-0.5)
    total = sum_z(scale, ids, quarter, d1, d2, d3, e, t3)
    two = jnp.concatenate([total, row_send(total, dx=1)], axis=0)
    weight_grad, bias_grad = weight_out(ids, two, row_send(two, dc=1))

    r = r14[:4].astype(f32) + r2.astype(f32) + r3.astype(f32)
    out = t0 + r[:2] + row_send(r[2:], dc=1)
    return hidden, out.reshape(256, B), weight_grad, bias_grad[0]


def solution(mesh):
    in_specs = (
        P("row", "feat"),
        P("feat", None),
        P("feat"),
        P("row", None, None),
        P("row"),
        P("row"),
        P("row", "feat"),
    )
    out_specs = (P("row", "feat"), P("row", "feat"), P("feat", None), P("feat"))
    return jax.shard_map(body, mesh=mesh, in_specs=in_specs, out_specs=out_specs, check_vma=False)
```

```python
import functools

import jax
import jax.numpy as jnp
from jax import lax
from jax.experimental import pallas as pl
from jax.experimental.pallas import tpu as pltpu
from jax.sharding import PartitionSpec as P

bf16 = jnp.bfloat16
f32 = jnp.float32
B = 128
NZ = 8
VM = pl.BlockSpec(memory_space=pltpu.VMEM)
SM = pl.BlockSpec(memory_space=pltpu.SMEM)
HB = pl.BlockSpec(memory_space=pltpu.HBM)
ANY = pl.BlockSpec(memory_space=pl.ANY)


def row_send(v, dx=0, dz=0, dc=0):
    perm = []
    for i in range(32):
        x, z, c = i >> 4, (i >> 1) & 7, i & 1
        perm.append((i, ((x ^ dx) << 4) | (((z + dz) % NZ) << 1) | (c ^ dc)))
    return lax.ppermute(v, "row", perm)


def feat_send(v, dx=0, dy=0):
    return lax.ppermute(v, "feat", [(i, (((i >> 2) ^ dx) << 2) | ((i + dy) & 3)) for i in range(8)])


def params(mib=20):
    return pltpu.CompilerParams(vmem_limit_bytes=mib << 20)


def spin_send(v, k, way=1):
    perm = []
    for i in range(32):
        x, z, c = i >> 4, (i >> 1) & 7, i & 1
        perm.append((i, (x << 4) | (((z + way * (k if c == 0 else -k)) % NZ) << 1) | c))
    return lax.ppermute(v, "row", perm)


def tie(a, b):
    return lax.optimization_barrier((a, b))


def cost(flops, nbytes):
    return pl.CostEstimate(flops=flops, bytes_accessed=nbytes, transcendentals=0)


def pack_body(ids, w, og, bias, *refs):
    out, sem = refs[-2:]
    core = ids[0] & 1
    copies = []
    for m in range(4):
        at = pl.multiple_of(core * 512 + m * B, B)
        copies.append(
            pltpu.make_async_copy(w.at[:, pl.ds(at, B)], out.at[m * B : (m + 1) * B, :], sem.at[m])
        )
    copies.append(pltpu.make_async_copy(og, out.at[512:768, :], sem.at[4]))
    for c in copies:
        c.start()
    out[768:784, :] = jnp.broadcast_to(bias[...], (16, B))
    for c in copies:
        c.wait()


def pack_up(ids, w, og, bias, *ready):
    return pl.pallas_call(
        pack_body,
        out_shape=jax.ShapeDtypeStruct((784, B), bf16),
        in_specs=[SM, HB, HB, VM] + [ANY] * len(ready),
        out_specs=VM,
        scratch_shapes=[pltpu.SemaphoreType.DMA((5,))],
        compiler_params=params(4),
        cost_estimate=cost(0, 1 << 19),
        name="pack_up",
    )(ids, w, og, bias, *ready)


def append_body(a, b, *refs):
    out = refs[-1]
    rows = a.shape[0]
    out[0:rows, :] = a[...]
    out[rows:, :] = b[0 : out.shape[0] - rows, :]


def append(n, a, b, *ready):
    return pl.pallas_call(
        append_body,
        out_shape=jax.ShapeDtypeStruct((n, a.shape[1]), a.dtype),
        in_specs=[VM, VM] + [ANY] * len(ready),
        out_specs=VM,
        compiler_params=params(4),
        cost_estimate=cost(0, 1 << 18),
        name="append",
    )(a, b, *ready)


def settle_body(mine, came, u, d, agg, a, b):
    agg[...] = (mine[...] + came[...]).astype(bf16)
    a[...] = u[0:784, :]
    b[...] = d[784:1568, :]


def settle(mine, came, u, d):
    half = jax.ShapeDtypeStruct((784, B), bf16)
    return pl.pallas_call(
        settle_body,
        out_shape=(jax.ShapeDtypeStruct((2, B, B), bf16), half, half),
        in_specs=[VM] * 4,
        out_specs=(VM, VM, VM),
        compiler_params=params(4),
        cost_estimate=cost(0, 1 << 18),
        name="settle",
    )(mine, came, u, d)


def plan_body(ids, c0, d0, c1, d1, out):
    me = ids[0]
    mx, mz, mc = me >> 4, (me >> 1) & 7, me & 1
    for side, (cols, dest) in enumerate(((c0, d0), (c1, d1))):
        base = 8 + 72 * side

        def step(i, n, cols=cols, dest=dest, base=base, side=side):
            b = cols[i]
            o = b >> 1
            dx, dz, dc = (o >> 4) ^ mx, ((o >> 1) - mz) & 7, (o & 1) ^ mc
            k = jnp.where(mc == 0, dz, NZ - dz)
            edge = (dz & 3) == 0
            held = jnp.where(edge, 1 - dc, jnp.where(k <= 3, 1, 0))
            j = jnp.where(edge, jnp.where(dz == 0, 7, 6), (3 - k) * 2 + dc)
            slot = dx * 16 + j * 2 + (b & 1)
            out[base + n] = i | (slot << 8) | ((dest[i] + 2 * side) << 16)
            return n + held

        n = lax.fori_loop(0, 64, step, 0, unroll=8)
        for u in range(4):
            out[base + n + u] = (32 << 8) | (4 << 16)
        out[side] = (n + 3) >> 2


def plan_tiles(ids, c0, d0, c1, d1):
    return pl.pallas_call(
        plan_body,
        out_shape=jax.ShapeDtypeStruct((160,), jnp.int32),
        in_specs=[SM] * 5,
        out_specs=SM,
        compiler_params=params(4),
        cost_estimate=cost(10000, 4096),
        name="plan_tiles",
    )(ids, c0, d0, c1, d1)


def each_tile(plan, tiles, more, use):
    for side, ref in enumerate((tiles, more)):
        def step(g, carry, side=side, ref=ref):
            for u in range(4):
                e = plan[8 + 72 * side + g * 4 + u]
                use(ref[e & 255], (e >> 8) & 255, e >> 16)
            return carry

        lax.fori_loop(0, plan[side], step, 0)


def agg_body(plan, tiles, more, *refs):
    mine, theirs, src, acc, sem = refs[8:]
    both, x0, o14, o2, o3, p14, p2, p3 = refs[0:8]
    copies = []

    def put(dx, j, v):
        n = v.shape[0]
        at = dx * 16 + j * 2
        copies.append(pltpu.make_async_copy(v, src.at[at : at + n], sem.at[len(copies)]))
        copies[-1].start()

    for dx, (v3, v2, v14, v0) in enumerate(((o3, o2, o14, both.at[0:2]), (p3, p2, p14, x0))):
        for j, v in ((0, v3), (2, v2), (4, v14), (7, v0)):
            put(dx, j, v)
    acc[...] = jnp.zeros_like(acc)
    src[32] = jnp.zeros((B, B), bf16)
    for c in copies:
        c.wait()

    def use(tile, slot, dest):
        acc[dest] += jnp.dot(tile, src[slot], preferred_element_type=f32)

    each_tile(plan, tiles, more, use)
    mine[...] = acc[0:2]
    theirs[...] = acc[2:4]


def aggregate(plan, tiles, more, pieces):
    parts = [v.reshape(-1, B, B) for v in pieces]
    return pl.pallas_call(
        agg_body,
        out_shape=(jax.ShapeDtypeStruct((2, B, B), f32), jax.ShapeDtypeStruct((2, B, B), f32)),
        in_specs=[SM, VM, VM] + [HB] * 8,
        out_specs=(VM, VM),
        scratch_shapes=[
            pltpu.VMEM((33, B, B), bf16),
            pltpu.VMEM((5, B, B), f32),
            pltpu.SemaphoreType.DMA((8,)),
        ],
        compiler_params=params(12),
        cost_estimate=cost(2 * 64 * B**3, 4 << 20),
        name="aggregate",
    )(plan, tiles, more, *parts)


def lay_body(ids, *refs):
    own = refs[0:5]
    w_out, og_out, bias_out, rows, sem = refs[6:11]
    yy, xx = ids[1] & 3, ids[1] >> 2
    copies, cols = [], []

    def put(src, dst):
        copies.append(pltpu.make_async_copy(src, dst, sem.at[len(copies)]))
        copies[-1].start()

    for j, off in enumerate((0, -1, 1, 2)):
        for i in range(2):
            k = j * 2 + i
            n, base = (j, i * 784) if j < 3 else (3 + i, 0)
            col = pl.multiple_of((((xx ^ i) << 2) | ((yy + off) & 3)) * B, B)
            cols.append(col)
            for m in range(4):
                put(own[n].at[pl.ds(base + m * B, B), :], w_out.at[pl.ds(k * B, B), pl.ds(m * B, B)])
            put(own[n].at[pl.ds(base + 512, 256), :], og_out.at[:, pl.ds(col, B)])
            put(own[n].at[pl.ds(base + 768, 16), :], rows.at[k])
    for c in copies:
        c.wait()
    for k in range(8):
        bias_out[:, pl.ds(cols[k], B)] = rows[k].astype(f32)[0:8]


def lay_out(ids, own, ready):
    return pl.pallas_call(
        lay_body,
        out_shape=(
            jax.ShapeDtypeStruct((1024, 512), bf16),
            jax.ShapeDtypeStruct((256, 1024), bf16),
            jax.ShapeDtypeStruct((8, 1024), f32),
        ),
        in_specs=[SM] + [HB] * 5 + [ANY],
        out_specs=(VM, VM, VM),
        scratch_shapes=[pltpu.VMEM((8, 16, B), bf16), pltpu.SemaphoreType.DMA((48,))],
        compiler_params=params(8),
        cost_estimate=cost(0, 3 << 20),
        name="lay_out",
    )(ids, *own, ready)


def mid_body(ids, p0, p1, p2, p3, w0, w1, og, bias, w_own, hidden, prop, keep, give, agg, pre, gp, wp):
    x, core = ids[0] >> 4, ids[0] & 1
    for j, p in enumerate((p0, p1, p2, p3)):
        for i in range(2):
            agg[:, (j * 2 + i) * B : (j * 2 + i + 1) * B] = p[i * 256 : (i + 1) * 256, :]
    for w, c in ((w0, core), (w1, 1 - core)):
        for m in range(2):
            cols = pl.ds(pl.multiple_of(c * 512 + m * 256, 256), 256)
            v = jnp.dot(agg[...], w[:, m * 256 : (m + 1) * 256], preferred_element_type=f32)
            v = v + bias[0:1, cols]
            pre[:, cols] = v
            s = jax.nn.sigmoid(v)
            gp[:, cols] = (og[:, cols].astype(f32) * s * (1.0 + v * (1.0 - s))).astype(bf16)
    mine = pl.ds(pl.multiple_of(ids[1] * B, B), B)
    v = pre[:, mine]
    hidden[...] = v * jax.nn.sigmoid(v)
    prop[...] = lax.dot_general(
        gp[...], w_own[...], (((1,), (1,)), ((), ())), preferred_element_type=f32
    ).astype(bf16)
    wp[:, 0:1024] = lax.dot_general(
        agg[:, 0:B], gp[...], (((0,), (0,)), ((), ())), preferred_element_type=f32
    )
    total = jnp.sum(gp[:, mine].astype(f32), axis=0, keepdims=True)
    wp[:, 1024:1152] = jnp.broadcast_to(total, (B, B))
    for ref, c in ((keep, core), (give, 1 - core)):
        for i in range(2):
            ref[i * 32 : (i + 1) * 32, :] = wp[pl.ds(pl.multiple_of(c * 64 + (x ^ i) * 32, 32), 32), :]


def middle(ids, pieces, w0, w1, og, bias, w_own):
    return pl.pallas_call(
        mid_body,
        out_shape=(
            jax.ShapeDtypeStruct((256, B), f32),
            jax.ShapeDtypeStruct((256, B), bf16),
            jax.ShapeDtypeStruct((64, 1152), f32),
            jax.ShapeDtypeStruct((64, 1152), f32),
        ),
        in_specs=[SM] + [VM] * 9,
        out_specs=(VM, VM, VM, VM),
        scratch_shapes=[
            pltpu.VMEM((256, 1024), bf16),
            pltpu.VMEM((256, 1024), f32),
            pltpu.VMEM((256, 1024), bf16),
            pltpu.VMEM((B, 1152), f32),
        ],
        compiler_params=params(),
        cost_estimate=cost(2 * 256 * 1024 * 1280, 5 << 20),
        name="middle",
    )(ids, *pieces, w0, w1, og, bias, w_own)


def spread_body(plan, tiles, more, prop, peer, send, near, far, acc, both):
    acc[...] = jnp.zeros_like(acc)
    both[0:2] = prop[...]
    both[2:4] = peer[...]
    both[4] = jnp.zeros((B, B), bf16)

    def use(tile, slot, dest):
        acc[slot] += lax.dot_general(
            tile, both[dest], (((0,), (0,)), ((), ())), preferred_element_type=f32
        )

    each_tile(plan, tiles, more, use)
    near[...] = acc[0:16]
    far[...] = acc[16:32].astype(bf16)


def spread(plan, tiles, more, prop, peer, send):
    return pl.pallas_call(
        spread_body,
        out_shape=(
            jax.ShapeDtypeStruct((16, B, B), f32),
            jax.ShapeDtypeStruct((16, B, B), bf16),
        ),
        in_specs=[SM] + [VM] * 4 + [ANY],
        out_specs=(VM, VM),
        scratch_shapes=[pltpu.VMEM((33, B, B), f32), pltpu.VMEM((5, B, B), bf16)],
        compiler_params=params(12),
        cost_estimate=cost(2 * 64 * B**3, 6 << 20),
        name="spread",
    )(plan, tiles, more, prop, peer, send)


def quarter_body(keep, got, came, far, out):
    out[...] = (keep[0:32, :] + got[0:32, :] + came[...].astype(f32)).astype(bf16)


def quarter_up(keep, got, came, far):
    return pl.pallas_call(
        quarter_body,
        out_shape=jax.ShapeDtypeStruct((32, 1152), bf16),
        in_specs=[VM] * 3 + [ANY],
        out_specs=VM,
        compiler_params=params(4),
        cost_estimate=cost(0, 1 << 18),
        name="quarter_up",
    )(keep, got, came, far)


def join_body(near, came, ready, t14, t2, t3, t0):
    t3[...] = near[0:4] + came[0:4].astype(f32)
    t2[...] = (near[4:8] + came[4:8].astype(f32)).astype(bf16)
    t14[...] = (near[8:14] + came[8:14].astype(f32)).astype(bf16)
    t0[...] = near[14:16] + came[14:16].astype(f32)


def join(near, came, ready):
    return pl.pallas_call(
        join_body,
        out_shape=(
            jax.ShapeDtypeStruct((6, B, B), bf16),
            jax.ShapeDtypeStruct((4, B, B), bf16),
            jax.ShapeDtypeStruct((4, B, B), f32),
            jax.ShapeDtypeStruct((2, B, B), f32),
        ),
        in_specs=[VM, VM, ANY],
        out_specs=(VM, VM, VM, VM),
        compiler_params=params(8),
        cost_estimate=cost(0, 2 << 20),
        name="join",
    )(near, came, ready)


def ride_body(t3, r14, ready, out):
    out[0:2] = (t3[0:2] + r14[4:6].astype(f32)).astype(bf16)
    out[2:4] = t3[2:4].astype(bf16)


def ride(t3, r14, ready):
    return pl.pallas_call(
        ride_body,
        out_shape=jax.ShapeDtypeStruct((4, B, B), bf16),
        in_specs=[VM, VM, ANY],
        out_specs=VM,
        compiler_params=params(4),
        cost_estimate=cost(0, 1 << 18),
        name="ride",
    )(t3, r14, ready)


def rows_body(d1, d2, d3, t, out):
    for n, d in enumerate((d1, d2, d3)):
        out[32 * n : 32 * n + 32, :] = d[32:64, :]


def peer_rows(d1, d2, d3, t):
    return pl.pallas_call(
        rows_body,
        out_shape=jax.ShapeDtypeStruct((96, 1152), bf16),
        in_specs=[VM] * 3 + [ANY],
        out_specs=VM,
        compiler_params=params(4),
        cost_estimate=cost(0, 1 << 18),
        name="peer_rows",
    )(d1, d2, d3, t)


def sum_body(scale, ids, own, d1, d2, d3, e, t, out, buf):
    core, z = ids[0] & 1, (ids[0] >> 1) & 7
    buf[0] = own[...]
    buf[4] = d1[64:96, :]
    for k, d in ((1, d1), (2, d2), (3, d3)):
        mine = jnp.where(core == 0, k, NZ - k)
        buf[mine] = d[0:32, :]
        buf[NZ - mine] = e[(k - 1) * 32 : k * 32, :]
    acc = buf[(NZ - z) & 7].astype(f32)
    for n in range(1, NZ):
        acc = acc + buf[(n - z) & 7].astype(f32)
    out[...] = (acc * scale).astype(bf16)


def sum_z(scale, ids, *parts):
    return pl.pallas_call(
        functools.partial(sum_body, scale),
        out_shape=jax.ShapeDtypeStruct((32, 1152), bf16),
        in_specs=[SM] + [VM] * 5 + [ANY],
        out_specs=VM,
        scratch_shapes=[pltpu.VMEM((NZ, 32, 1152), bf16)],
        compiler_params=params(8),
        cost_estimate=cost(32 * 1152 * 8, 1 << 20),
        name="sum_z",
    )(ids, *parts)


def wout_body(ids, mine, theirs, w_out, b_out, buf):
    x, core = ids[0] >> 4, ids[0] & 1
    for ref, c in ((mine, core), (theirs, 1 - core)):
        for i in range(2):
            at = pl.multiple_of(c * 64 + (x ^ i) * 32, 32)
            buf[pl.ds(at, 32), :] = ref[i * 32 : (i + 1) * 32, :].astype(f32)
    w_out[...] = buf[:, 0:1024]
    b_out[...] = buf[0:8, 1024:1152]


def weight_out(ids, mine, theirs):
    return pl.pallas_call(
        wout_body,
        out_shape=(jax.ShapeDtypeStruct((B, 1024), f32), jax.ShapeDtypeStruct((8, B), f32)),
        in_specs=[SM, VM, VM],
        out_specs=(VM, VM),
        scratch_shapes=[pltpu.VMEM((B, 1152), f32)],
        compiler_params=params(8),
        cost_estimate=cost(0, 1 << 20),
        name="weight_out",
    )(ids, mine, theirs)


def body(features, weight, bias_vector, adj_tiles, col_blocks, dest_blocks, out_grad):
    ids = jnp.stack([lax.axis_index("row"), lax.axis_index("feat")]).astype(jnp.int32)

    both = jnp.concatenate([features, row_send(features, dc=1)], axis=0)
    x0 = row_send(features, dx=1)
    lists = row_send(jnp.stack([col_blocks, dest_blocks]), dc=1)
    swap, both_a = tie(adj_tiles, both)
    more = row_send(swap, dc=1)
    o3, o2 = spin_send(both, 3, -1), spin_send(both, 2, -1)
    plan = plan_tiles(ids, col_blocks, dest_blocks, lists[0], lists[1])
    ext = append(768, both, o3, o2, x0, plan)
    o14 = spin_send(ext, 1, -1)
    p3, p2, p14 = row_send(o3, dx=1), row_send(o2, dx=1), row_send(o14, dx=1)

    pack = pack_up(ids, weight, out_grad, bias_vector[None, :], ext)
    pair = append(1568, pack, feat_send(pack, dx=1), p3, p2, p14)
    wu, wd = feat_send(pair, dy=1), feat_send(pair, dy=-1)

    mine, theirs = aggregate(plan, adj_tiles, more, (both_a, x0, o14, o2, o3, p14, p2, p3))
    aggregated, wa, wb = settle(mine, row_send(theirs, dc=1), wu, wd)
    aggregated = aggregated.reshape(256, B)
    wa, wb = feat_send(wa, dy=1), feat_send(wb, dy=-1)

    q = jnp.concatenate([aggregated, feat_send(aggregated, dx=1)], axis=0)
    w0, og, bias = lay_out(ids, (pair, wu, wd, wa, wb), q)
    pieces = (q, feat_send(q, dy=1), feat_send(q, dy=-1), feat_send(q, dy=2))
    hidden, prop, keep, give = middle(ids, pieces, w0, row_send(w0, dc=1), og, bias, weight)
    prop = prop.reshape(2, B, B)

    peer = row_send(prop, dc=1)
    got = row_send(give, dc=1)
    send = (keep[32:] + got[32:]).astype(bf16)
    got_x = row_send(send, dx=1)
    near, far = spread(plan, adj_tiles, more, prop, peer, send)
    came = row_send(far, dx=1)
    quarter = quarter_up(keep, got, got_x, far)
    halves = jnp.concatenate([quarter, row_send(quarter, dc=1)], axis=0)
    d3, d2 = spin_send(halves, 3, -1), spin_send(halves, 2, -1)
    last = append(96, halves, d3, d2)
    d1 = spin_send(last, 1, -1)

    t14, t2, t3, t0 = join(near, came, last)
    r14, r2 = spin_send(t14, 1), spin_send(t2, 2)
    t3 = ride(t3, r14, r2)
    r3 = spin_send(t3, 3)

    e = row_send(peer_rows(d1, d2, d3, t3), dc=1)
    scale = float(256 * lax.axis_size("row")) ** (-0.5)
    total = sum_z(scale, ids, quarter, d1, d2, d3, e, t3)
    two = jnp.concatenate([total, row_send(total, dx=1)], axis=0)
    weight_grad, bias_grad = weight_out(ids, two, row_send(two, dc=1))

    r = r14[:4].astype(f32) + r2.astype(f32) + r3.astype(f32)
    out = t0 + r[:2] + row_send(r[2:], dc=1)
    return hidden, out.reshape(256, B), weight_grad, bias_grad[0]


def solution(mesh):
    in_specs = (
        P("row", "feat"),
        P("feat", None),
        P("feat"),
        P("row", None, None),
        P("row"),
        P("row"),
        P("row", "feat"),
    )
    out_specs = (P("row", "feat"), P("row", "feat"), P("feat", None), P("feat"))
    return jax.shard_map(body, mesh=mesh, in_specs=in_specs, out_specs=out_specs, check_vma=False)
```

```python
import functools

import jax
import jax.numpy as jnp
from jax import lax
from jax.experimental import pallas as pl
from jax.experimental.pallas import tpu as pltpu
from jax.sharding import PartitionSpec as P

bf16 = jnp.bfloat16
f32 = jnp.float32
B = 128
NZ = 8
VM = pl.BlockSpec(memory_space=pltpu.VMEM)
SM = pl.BlockSpec(memory_space=pltpu.SMEM)
HB = pl.BlockSpec(memory_space=pltpu.HBM)
ANY = pl.BlockSpec(memory_space=pl.ANY)


def row_send(v, dx=0, dz=0, dc=0):
    perm = []
    for i in range(32):
        x, z, c = i >> 4, (i >> 1) & 7, i & 1
        perm.append((i, ((x ^ dx) << 4) | (((z + dz) % NZ) << 1) | (c ^ dc)))
    return lax.ppermute(v, "row", perm)


def feat_send(v, dx=0, dy=0):
    return lax.ppermute(v, "feat", [(i, (((i >> 2) ^ dx) << 2) | ((i + dy) & 3)) for i in range(8)])


def params(mib=20):
    return pltpu.CompilerParams(vmem_limit_bytes=mib << 20)


def spin_send(v, k, way=1):
    perm = []
    for i in range(32):
        x, z, c = i >> 4, (i >> 1) & 7, i & 1
        perm.append((i, (x << 4) | (((z + way * (k if c == 0 else -k)) % NZ) << 1) | c))
    return lax.ppermute(v, "row", perm)


def tie(a, b):
    return lax.optimization_barrier((a, b))


def cost(flops, nbytes):
    return pl.CostEstimate(flops=flops, bytes_accessed=nbytes, transcendentals=0)


def pack_body(ids, w, og, bias, *refs):
    out, sem = refs[-2:]
    core = ids[0] & 1
    copies = []
    for m in range(4):
        at = pl.multiple_of(core * 512 + m * B, B)
        copies.append(
            pltpu.make_async_copy(w.at[:, pl.ds(at, B)], out.at[m * B : (m + 1) * B, :], sem.at[m])
        )
    copies.append(pltpu.make_async_copy(og, out.at[512:768, :], sem.at[4]))
    for c in copies:
        c.start()
    out[768:784, :] = jnp.broadcast_to(bias[...], (16, B))
    for c in copies:
        c.wait()


def pack_up(ids, w, og, bias, *ready):
    return pl.pallas_call(
        pack_body,
        out_shape=jax.ShapeDtypeStruct((784, B), bf16),
        in_specs=[SM, HB, HB, VM] + [ANY] * len(ready),
        out_specs=VM,
        scratch_shapes=[pltpu.SemaphoreType.DMA((5,))],
        compiler_params=params(60),
        cost_estimate=cost(0, 1 << 19),
        name="pack_up",
    )(ids, w, og, bias, *ready)


def append_body(a, b, *refs):
    out = refs[-1]
    rows = a.shape[0]
    out[0:rows, :] = a[...]
    out[rows:, :] = b[0 : out.shape[0] - rows, :]


def append(n, a, b, *ready):
    return pl.pallas_call(
        append_body,
        out_shape=jax.ShapeDtypeStruct((n, a.shape[1]), a.dtype),
        in_specs=[VM, VM] + [ANY] * len(ready),
        out_specs=VM,
        compiler_params=params(4),
        cost_estimate=cost(0, 1 << 18),
        name="append",
    )(a, b, *ready)


def turn_body(u, d, a, b):
    a[...] = u[0:784, :]
    b[...] = d[784:1568, :]


def turn(u, d):
    half = jax.ShapeDtypeStruct((784, B), bf16)
    return pl.pallas_call(
        turn_body,
        out_shape=(half, half),
        in_specs=[VM, VM],
        out_specs=(VM, VM),
        compiler_params=params(4),
        cost_estimate=cost(0, 1 << 18),
        name="turn",
    )(u, d)


def settle_body(mine, came, a, b, agg):
    agg[...] = (mine[...] + came[...]).astype(bf16)


def settle(mine, came, a, b):
    return pl.pallas_call(
        settle_body,
        out_shape=jax.ShapeDtypeStruct((2, B, B), bf16),
        in_specs=[VM, VM, ANY, ANY],
        out_specs=VM,
        compiler_params=params(4),
        cost_estimate=cost(0, 1 << 18),
        name="settle",
    )(mine, came, a, b)


def plan_body(ids, c0, d0, c1, d1, out):
    me = ids[0]
    mx, mz, mc = me >> 4, (me >> 1) & 7, me & 1
    for side, (cols, dest) in enumerate(((c0, d0), (c1, d1))):
        base = 8 + 72 * side

        def step(i, n, cols=cols, dest=dest, base=base, side=side):
            b = cols[i]
            o = b >> 1
            dx, dz, dc = (o >> 4) ^ mx, ((o >> 1) - mz) & 7, (o & 1) ^ mc
            k = jnp.where(mc == 0, dz, NZ - dz)
            edge = (dz & 3) == 0
            held = jnp.where(edge, 1 - dc, jnp.where(k <= 3, 1, 0))
            j = jnp.where(edge, jnp.where(dz == 0, 7, 6), (3 - k) * 2 + dc)
            slot = dx * 16 + j * 2 + (b & 1)
            out[base + n] = i | (slot << 8) | ((dest[i] + 2 * side) << 16)
            return n + held

        n = lax.fori_loop(0, 64, step, 0, unroll=8)
        for u in range(4):
            out[base + n + u] = (32 << 8) | (4 << 16)
        out[side] = (n + 3) >> 2


def plan_tiles(ids, c0, d0, c1, d1):
    return pl.pallas_call(
        plan_body,
        out_shape=jax.ShapeDtypeStruct((160,), jnp.int32),
        in_specs=[SM] * 5,
        out_specs=SM,
        compiler_params=params(4),
        cost_estimate=cost(10000, 4096),
        name="plan_tiles",
    )(ids, c0, d0, c1, d1)


def each_tile(plan, tiles, more, use):
    for side, ref in enumerate((tiles, more)):
        def step(g, carry, side=side, ref=ref):
            for u in range(4):
                e = plan[8 + 72 * side + g * 4 + u]
                use(ref[e & 255], (e >> 8) & 255, e >> 16)
            return carry

        lax.fori_loop(0, plan[side], step, 0)


def agg_body(plan, tiles, more, *refs):
    mine, theirs, src, acc, sem = refs[10:]
    both, x0, o14, o2, o3, p14, p2, p3 = refs[0:8]
    copies = []

    def put(dx, j, v):
        n = v.shape[0]
        at = dx * 16 + j * 2
        copies.append(pltpu.make_async_copy(v, src.at[at : at + n], sem.at[len(copies)]))
        copies[-1].start()

    for dx, (v3, v2, v14, v0) in enumerate(((o3, o2, o14, both.at[0:2]), (p3, p2, p14, x0))):
        for j, v in ((0, v3), (2, v2), (4, v14), (7, v0)):
            put(dx, j, v)
    acc[...] = jnp.zeros_like(acc)
    src[32] = jnp.zeros((B, B), bf16)
    for c in copies:
        c.wait()

    def use(tile, slot, dest):
        acc[dest] += jnp.dot(tile, src[slot], preferred_element_type=f32)

    each_tile(plan, tiles, more, use)
    mine[...] = acc[0:2]
    theirs[...] = acc[2:4]


def aggregate(plan, tiles, more, pieces, *ready):
    parts = [v.reshape(-1, B, B) for v in pieces]
    return pl.pallas_call(
        agg_body,
        out_shape=(jax.ShapeDtypeStruct((2, B, B), f32), jax.ShapeDtypeStruct((2, B, B), f32)),
        in_specs=[SM, VM, VM] + [HB] * 8 + [ANY] * 2,
        out_specs=(VM, VM),
        scratch_shapes=[
            pltpu.VMEM((33, B, B), bf16),
            pltpu.VMEM((5, B, B), f32),
            pltpu.SemaphoreType.DMA((8,)),
        ],
        compiler_params=params(12),
        cost_estimate=cost(2 * 64 * B**3, 4 << 20),
        name="aggregate",
    )(plan, tiles, more, *parts, *ready)


def lay_body(ids, *refs):
    own = refs[0:5]
    w_out, og_out, bias_out, rows, sem = refs[6:11]
    yy, xx = ids[1] & 3, ids[1] >> 2
    copies, cols = [], []

    def put(src, dst):
        copies.append(pltpu.make_async_copy(src, dst, sem.at[len(copies)]))
        copies[-1].start()

    for j, off in enumerate((0, -1, 1, 2)):
        for i in range(2):
            k = j * 2 + i
            n, base = (j, i * 784) if j < 3 else (3 + i, 0)
            col = pl.multiple_of((((xx ^ i) << 2) | ((yy + off) & 3)) * B, B)
            cols.append(col)
            for m in range(4):
                put(own[n].at[pl.ds(base + m * B, B), :], w_out.at[pl.ds(k * B, B), pl.ds(m * B, B)])
            put(own[n].at[pl.ds(base + 512, 256), :], og_out.at[:, pl.ds(col, B)])
            put(own[n].at[pl.ds(base + 768, 16), :], rows.at[k])
    for c in copies:
        c.wait()
    for k in range(8):
        bias_out[:, pl.ds(cols[k], B)] = rows[k].astype(f32)[0:8]


def lay_out(ids, own, ready):
    return pl.pallas_call(
        lay_body,
        out_shape=(
            jax.ShapeDtypeStruct((1024, 512), bf16),
            jax.ShapeDtypeStruct((256, 1024), bf16),
            jax.ShapeDtypeStruct((8, 1024), f32),
        ),
        in_specs=[SM] + [HB] * 5 + [ANY],
        out_specs=(VM, VM, VM),
        scratch_shapes=[pltpu.VMEM((8, 16, B), bf16), pltpu.SemaphoreType.DMA((48,))],
        compiler_params=params(8),
        cost_estimate=cost(0, 3 << 20),
        name="lay_out",
    )(ids, *own, ready)


def mid_body(ids, p0, p1, p2, p3, w0, w1, og, bias, w_own, hidden, prop, keep, give, agg, pre, gp, wp):
    x, core = ids[0] >> 4, ids[0] & 1
    for j, p in enumerate((p0, p1, p2, p3)):
        for i in range(2):
            agg[:, (j * 2 + i) * B : (j * 2 + i + 1) * B] = p[i * 256 : (i + 1) * 256, :]
    for w, c in ((w0, core), (w1, 1 - core)):
        for m in range(2):
            cols = pl.ds(pl.multiple_of(c * 512 + m * 256, 256), 256)
            v = jnp.dot(agg[...], w[:, m * 256 : (m + 1) * 256], preferred_element_type=f32)
            v = v + bias[0:1, cols]
            pre[:, cols] = v
            s = jax.nn.sigmoid(v)
            gp[:, cols] = (og[:, cols].astype(f32) * s * (1.0 + v * (1.0 - s))).astype(bf16)
    mine = pl.ds(pl.multiple_of(ids[1] * B, B), B)
    v = pre[:, mine]
    hidden[...] = v * jax.nn.sigmoid(v)
    prop[...] = lax.dot_general(
        gp[...], w_own[...], (((1,), (1,)), ((), ())), preferred_element_type=f32
    ).astype(bf16)
    wp[:, 0:1024] = lax.dot_general(
        agg[:, 0:B], gp[...], (((0,), (0,)), ((), ())), preferred_element_type=f32
    )
    total = jnp.sum(gp[:, mine].astype(f32), axis=0, keepdims=True)
    wp[:, 1024:1152] = jnp.broadcast_to(total, (B, B))
    for ref, c in ((keep, core), (give, 1 - core)):
        for i in range(2):
            ref[i * 32 : (i + 1) * 32, :] = wp[pl.ds(pl.multiple_of(c * 64 + (x ^ i) * 32, 32), 32), :]


def middle(ids, pieces, w0, w1, og, bias, w_own):
    return pl.pallas_call(
        mid_body,
        out_shape=(
            jax.ShapeDtypeStruct((256, B), f32),
            jax.ShapeDtypeStruct((256, B), bf16),
            jax.ShapeDtypeStruct((64, 1152), f32),
            jax.ShapeDtypeStruct((64, 1152), f32),
        ),
        in_specs=[SM] + [VM] * 9,
        out_specs=(VM, VM, VM, VM),
        scratch_shapes=[
            pltpu.VMEM((256, 1024), bf16),
            pltpu.VMEM((256, 1024), f32),
            pltpu.VMEM((256, 1024), bf16),
            pltpu.VMEM((B, 1152), f32),
        ],
        compiler_params=params(),
        cost_estimate=cost(2 * 256 * 1024 * 1280, 5 << 20),
        name="middle",
    )(ids, *pieces, w0, w1, og, bias, w_own)


def spread_body(plan, tiles, more, prop, peer, send, near, far, acc, both):
    acc[...] = jnp.zeros_like(acc)
    both[0:2] = prop[...]
    both[2:4] = peer[...]
    both[4] = jnp.zeros((B, B), bf16)

    def use(tile, slot, dest):
        acc[slot] += lax.dot_general(
            tile, both[dest], (((0,), (0,)), ((), ())), preferred_element_type=f32
        )

    each_tile(plan, tiles, more, use)
    near[...] = acc[0:16]
    far[...] = acc[16:32].astype(bf16)


def spread(plan, tiles, more, prop, peer, send):
    return pl.pallas_call(
        spread_body,
        out_shape=(
            jax.ShapeDtypeStruct((16, B, B), f32),
            jax.ShapeDtypeStruct((16, B, B), bf16),
        ),
        in_specs=[SM] + [VM] * 4 + [ANY],
        out_specs=(VM, VM),
        scratch_shapes=[pltpu.VMEM((33, B, B), f32), pltpu.VMEM((5, B, B), bf16)],
        compiler_params=params(12),
        cost_estimate=cost(2 * 64 * B**3, 6 << 20),
        name="spread",
    )(plan, tiles, more, prop, peer, send)


def quarter_body(keep, got, came, far, out):
    out[...] = (keep[0:32, :] + got[0:32, :] + came[...].astype(f32)).astype(bf16)


def quarter_up(keep, got, came, far):
    return pl.pallas_call(
        quarter_body,
        out_shape=jax.ShapeDtypeStruct((32, 1152), bf16),
        in_specs=[VM] * 3 + [ANY],
        out_specs=VM,
        compiler_params=params(4),
        cost_estimate=cost(0, 1 << 18),
        name="quarter_up",
    )(keep, got, came, far)


def join_body(near, came, ready, t14, t2, t3, t0):
    t3[...] = near[0:4] + came[0:4].astype(f32)
    t2[...] = (near[4:8] + came[4:8].astype(f32)).astype(bf16)
    t14[...] = (near[8:14] + came[8:14].astype(f32)).astype(bf16)
    t0[...] = near[14:16] + came[14:16].astype(f32)


def join(near, came, ready):
    return pl.pallas_call(
        join_body,
        out_shape=(
            jax.ShapeDtypeStruct((6, B, B), bf16),
            jax.ShapeDtypeStruct((4, B, B), bf16),
            jax.ShapeDtypeStruct((4, B, B), f32),
            jax.ShapeDtypeStruct((2, B, B), f32),
        ),
        in_specs=[VM, VM, ANY],
        out_specs=(VM, VM, VM, VM),
        compiler_params=params(8),
        cost_estimate=cost(0, 2 << 20),
        name="join",
    )(near, came, ready)


def ride_body(t3, r14, out):
    out[0:2] = (t3[0:2] + r14[4:6].astype(f32)).astype(bf16)
    out[2:4] = t3[2:4].astype(bf16)


def ride(t3, r14):
    return pl.pallas_call(
        ride_body,
        out_shape=jax.ShapeDtypeStruct((4, B, B), bf16),
        in_specs=[VM, VM],
        out_specs=VM,
        compiler_params=params(4),
        cost_estimate=cost(0, 1 << 18),
        name="ride",
    )(t3, r14)


def rows_body(d1, d2, d3, t, out):
    for n, d in enumerate((d1, d2, d3)):
        out[32 * n : 32 * n + 32, :] = d[32:64, :]


def peer_rows(d1, d2, d3, t):
    return pl.pallas_call(
        rows_body,
        out_shape=jax.ShapeDtypeStruct((96, 1152), bf16),
        in_specs=[VM] * 3 + [ANY],
        out_specs=VM,
        compiler_params=params(4),
        cost_estimate=cost(0, 1 << 18),
        name="peer_rows",
    )(d1, d2, d3, t)


def sum_body(scale, ids, own, d1, d2, d3, e, t, out, buf):
    core, z = ids[0] & 1, (ids[0] >> 1) & 7
    buf[0] = own[...]
    buf[4] = d1[64:96, :]
    for k, d in ((1, d1), (2, d2), (3, d3)):
        mine = jnp.where(core == 0, k, NZ - k)
        buf[mine] = d[0:32, :]
        buf[NZ - mine] = e[(k - 1) * 32 : k * 32, :]
    acc = buf[(NZ - z) & 7].astype(f32)
    for n in range(1, NZ):
        acc = acc + buf[(n - z) & 7].astype(f32)
    out[...] = (acc * scale).astype(bf16)


def sum_z(scale, ids, *parts):
    return pl.pallas_call(
        functools.partial(sum_body, scale),
        out_shape=jax.ShapeDtypeStruct((32, 1152), bf16),
        in_specs=[SM] + [VM] * 5 + [ANY],
        out_specs=VM,
        scratch_shapes=[pltpu.VMEM((NZ, 32, 1152), bf16)],
        compiler_params=params(8),
        cost_estimate=cost(32 * 1152 * 8, 1 << 20),
        name="sum_z",
    )(ids, *parts)


def wout_body(ids, mine, theirs, w_out, b_out, buf):
    x, core = ids[0] >> 4, ids[0] & 1
    for ref, c in ((mine, core), (theirs, 1 - core)):
        for i in range(2):
            at = pl.multiple_of(c * 64 + (x ^ i) * 32, 32)
            buf[pl.ds(at, 32), :] = ref[i * 32 : (i + 1) * 32, :].astype(f32)
    w_out[...] = buf[:, 0:1024]
    b_out[...] = buf[0:8, 1024:1152]


def weight_out(ids, mine, theirs):
    return pl.pallas_call(
        wout_body,
        out_shape=(jax.ShapeDtypeStruct((B, 1024), f32), jax.ShapeDtypeStruct((8, B), f32)),
        in_specs=[SM, VM, VM],
        out_specs=(VM, VM),
        scratch_shapes=[pltpu.VMEM((B, 1152), f32)],
        compiler_params=params(8),
        cost_estimate=cost(0, 1 << 20),
        name="weight_out",
    )(ids, mine, theirs)


def body(features, weight, bias_vector, adj_tiles, col_blocks, dest_blocks, out_grad):
    ids = jnp.stack([lax.axis_index("row"), lax.axis_index("feat")]).astype(jnp.int32)

    both = jnp.concatenate([features, row_send(features, dc=1)], axis=0)
    x0 = row_send(features, dx=1)
    lists = row_send(jnp.stack([col_blocks, dest_blocks]), dc=1)
    swap, both_a = tie(adj_tiles, both)
    more = row_send(swap, dc=1)
    o3, o2 = spin_send(both, 3, -1), spin_send(both, 2, -1)
    plan = plan_tiles(ids, col_blocks, dest_blocks, lists[0], lists[1])

    pack = pack_up(ids, weight, out_grad, bias_vector[None, :])
    pack_x = feat_send(pack, dx=1)

    pair = append(1568, pack, pack_x)
    ext = append(768, both, o3, o2, x0, plan, pair)
    o14 = spin_send(ext, 1, -1)
    p3, p2, p14 = row_send(o3, dx=1), row_send(o2, dx=1), row_send(o14, dx=1)
    wu, wd = feat_send(pair, dy=1), feat_send(pair, dy=-1)

    wa, wb = turn(wu, wd)
    mine, theirs = aggregate(plan, adj_tiles, more, (both_a, x0, o14, o2, o3, p14, p2, p3), wa, wb)
    wa, wb = feat_send(wa, dy=1), feat_send(wb, dy=-1)
    aggregated = settle(mine, row_send(theirs, dc=1), wa, wb).reshape(256, B)

    q = jnp.concatenate([aggregated, feat_send(aggregated, dx=1)], axis=0)
    w0, og, bias = lay_out(ids, (pair, wu, wd, wa, wb), q)
    pieces = (q, feat_send(q, dy=1), feat_send(q, dy=-1), feat_send(q, dy=2))
    hidden, prop, keep, give = middle(ids, pieces, w0, row_send(w0, dc=1), og, bias, weight)
    prop = prop.reshape(2, B, B)

    peer = row_send(prop, dc=1)
    got = row_send(give, dc=1)
    send = (keep[32:] + got[32:]).astype(bf16)
    got_x = row_send(send, dx=1)
    near, far = spread(plan, adj_tiles, more, prop, peer, send)
    came = row_send(far, dx=1)
    quarter = quarter_up(keep, got, got_x, far)
    halves = jnp.concatenate([quarter, row_send(quarter, dc=1)], axis=0)
    d3, d2 = spin_send(halves, 3, -1), spin_send(halves, 2, -1)
    last = append(96, halves, d3, d2)
    d1 = spin_send(last, 1, -1)

    t14, t2, t3, t0 = join(near, came, last)
    r14, r2 = spin_send(t14, 1), spin_send(t2, 2)
    t3 = ride(t3, r14)
    r3 = spin_send(t3, 3)

    e = row_send(peer_rows(d1, d2, d3, r2), dc=1)
    scale = float(256 * lax.axis_size("row")) ** (-0.5)
    total = sum_z(scale, ids, quarter, d1, d2, d3, e, t3)
    two = jnp.concatenate([total, row_send(total, dx=1)], axis=0)
    weight_grad, bias_grad = weight_out(ids, two, row_send(two, dc=1))

    r = r14[:4].astype(f32) + r2.astype(f32) + r3.astype(f32)
    out = t0 + r[:2] + row_send(r[2:], dc=1)
    return hidden, out.reshape(256, B), weight_grad, bias_grad[0]


def solution(mesh):
    in_specs = (
        P("row", "feat"),
        P("feat", None),
        P("feat"),
        P("row", None, None),
        P("row"),
        P("row"),
        P("row", "feat"),
    )
    out_specs = (P("row", "feat"), P("row", "feat"), P("feat", None), P("feat"))
    return jax.shard_map(body, mesh=mesh, in_specs=in_specs, out_specs=out_specs, check_vma=False)
```

```python
import functools

import jax
import jax.numpy as jnp
from jax import lax
from jax.experimental import pallas as pl
from jax.experimental.pallas import tpu as pltpu
from jax.sharding import PartitionSpec as P

bf16 = jnp.bfloat16
f32 = jnp.float32
B = 128
NZ = 8
VM = pl.BlockSpec(memory_space=pltpu.VMEM)
SM = pl.BlockSpec(memory_space=pltpu.SMEM)
HB = pl.BlockSpec(memory_space=pltpu.HBM)
ANY = pl.BlockSpec(memory_space=pl.ANY)


def row_send(v, dx=0, dz=0, dc=0):
    perm = []
    for i in range(32):
        x, z, c = i >> 4, (i >> 1) & 7, i & 1
        perm.append((i, ((x ^ dx) << 4) | (((z + dz) % NZ) << 1) | (c ^ dc)))
    return lax.ppermute(v, "row", perm)


def feat_send(v, dx=0, dy=0):
    return lax.ppermute(v, "feat", [(i, (((i >> 2) ^ dx) << 2) | ((i + dy) & 3)) for i in range(8)])


def params(mib=20):
    return pltpu.CompilerParams(vmem_limit_bytes=mib << 20)


def spin_send(v, k, way=1):
    perm = []
    for i in range(32):
        x, z, c = i >> 4, (i >> 1) & 7, i & 1
        perm.append((i, (x << 4) | (((z + way * (k if c == 0 else -k)) % NZ) << 1) | c))
    return lax.ppermute(v, "row", perm)


def tie(a, b):
    return lax.optimization_barrier((a, b))


def cost(flops, nbytes):
    return pl.CostEstimate(flops=flops, bytes_accessed=nbytes, transcendentals=0)


def pack_body(ids, w, og, bias, *refs):
    out, sem = refs[-2:]
    core = ids[0] & 1
    copies = []
    for m in range(4):
        at = pl.multiple_of(core * 512 + m * B, B)
        copies.append(
            pltpu.make_async_copy(w.at[:, pl.ds(at, B)], out.at[m * B : (m + 1) * B, :], sem.at[m])
        )
    copies.append(pltpu.make_async_copy(og, out.at[512:768, :], sem.at[4]))
    for c in copies:
        c.start()
    out[768:784, :] = jnp.broadcast_to(bias[...], (16, B))
    for c in copies:
        c.wait()


def pack_up(ids, w, og, bias, *ready):
    return pl.pallas_call(
        pack_body,
        out_shape=jax.ShapeDtypeStruct((784, B), bf16),
        in_specs=[SM, HB, HB, VM] + [ANY] * len(ready),
        out_specs=VM,
        scratch_shapes=[pltpu.SemaphoreType.DMA((5,))],
        compiler_params=params(60),
        cost_estimate=cost(0, 1 << 19),
        name="pack_up",
    )(ids, w, og, bias, *ready)


def append_body(a, b, *refs):
    out = refs[-1]
    rows = a.shape[0]
    out[0:rows, :] = a[...]
    out[rows:, :] = b[0 : out.shape[0] - rows, :]


def append(n, a, b, *ready):
    return pl.pallas_call(
        append_body,
        out_shape=jax.ShapeDtypeStruct((n, a.shape[1]), a.dtype),
        in_specs=[VM, VM] + [ANY] * len(ready),
        out_specs=VM,
        compiler_params=params(4),
        cost_estimate=cost(0, 1 << 18),
        name="append",
    )(a, b, *ready)


def turn_body(u, d, r0, r1, a, b):
    a[...] = u[0:784, :]
    b[...] = d[784:1568, :]


def turn(u, d, *ready):
    half = jax.ShapeDtypeStruct((784, B), bf16)
    return pl.pallas_call(
        turn_body,
        out_shape=(half, half),
        in_specs=[VM, VM, ANY, ANY],
        out_specs=(VM, VM),
        compiler_params=params(4),
        cost_estimate=cost(0, 1 << 18),
        name="turn",
    )(u, d, *ready)


def settle_body(mine, came, r0, r1, agg):
    agg[...] = (mine[...] + came[...]).astype(bf16)


def settle(mine, came, *ready):
    return pl.pallas_call(
        settle_body,
        out_shape=jax.ShapeDtypeStruct((2, B, B), bf16),
        in_specs=[VM, VM, ANY, ANY],
        out_specs=VM,
        compiler_params=params(4),
        cost_estimate=cost(0, 1 << 18),
        name="settle",
    )(mine, came, *ready)


def plan_body(ids, c0, d0, c1, d1, out):
    me = ids[0]
    mx, mz, mc = me >> 4, (me >> 1) & 7, me & 1
    for side, (cols, dest) in enumerate(((c0, d0), (c1, d1))):
        base = 8 + 72 * side

        def step(i, n, cols=cols, dest=dest, base=base, side=side):
            b = cols[i]
            o = b >> 1
            dx, dz, dc = (o >> 4) ^ mx, ((o >> 1) - mz) & 7, (o & 1) ^ mc
            k = jnp.where(mc == 0, dz, NZ - dz)
            edge = (dz & 3) == 0
            held = jnp.where(edge, 1 - dc, jnp.where(k <= 3, 1, 0))
            j = jnp.where(edge, jnp.where(dz == 0, 7, 6), (3 - k) * 2 + dc)
            slot = dx * 16 + j * 2 + (b & 1)
            out[base + n] = i | (slot << 8) | ((dest[i] + 2 * side) << 16)
            return n + held

        n = lax.fori_loop(0, 64, step, 0, unroll=8)
        for u in range(4):
            out[base + n + u] = (32 << 8) | (4 << 16)
        out[side] = (n + 3) >> 2


def plan_tiles(ids, c0, d0, c1, d1):
    return pl.pallas_call(
        plan_body,
        out_shape=jax.ShapeDtypeStruct((160,), jnp.int32),
        in_specs=[SM] * 5,
        out_specs=SM,
        compiler_params=params(4),
        cost_estimate=cost(10000, 4096),
        name="plan_tiles",
    )(ids, c0, d0, c1, d1)


def each_tile(plan, tiles, more, use):
    for side, ref in enumerate((tiles, more)):
        def step(g, carry, side=side, ref=ref):
            for u in range(4):
                e = plan[8 + 72 * side + g * 4 + u]
                use(ref[e & 255], (e >> 8) & 255, e >> 16)
            return carry

        lax.fori_loop(0, plan[side], step, 0)


def agg_body(plan, tiles, more, *refs):
    mine, theirs, src, acc, sem = refs[12:]
    both, x0, o4, o1, o2, o3, p4, p1, p2, p3 = refs[0:10]
    copies = []

    def put(dx, j, v):
        n = v.shape[0]
        at = dx * 16 + j * 2
        copies.append(pltpu.make_async_copy(v, src.at[at : at + n], sem.at[len(copies)]))
        copies[-1].start()

    for dx, (v3, v2, v1, v4, v0) in enumerate(((o3, o2, o1, o4, both.at[0:2]), (p3, p2, p1, p4, x0))):
        for j, v in ((0, v3), (2, v2), (4, v1), (6, v4), (7, v0)):
            put(dx, j, v)
    acc[...] = jnp.zeros_like(acc)
    src[32] = jnp.zeros((B, B), bf16)
    for c in copies:
        c.wait()

    def use(tile, slot, dest):
        acc[dest] += jnp.dot(tile, src[slot], preferred_element_type=f32)

    each_tile(plan, tiles, more, use)
    mine[...] = acc[0:2]
    theirs[...] = acc[2:4]


def aggregate(plan, tiles, more, pieces, *ready):
    parts = [v.reshape(-1, B, B) for v in pieces]
    return pl.pallas_call(
        agg_body,
        out_shape=(jax.ShapeDtypeStruct((2, B, B), f32), jax.ShapeDtypeStruct((2, B, B), f32)),
        in_specs=[SM, VM, VM] + [HB] * 10 + [ANY] * 2,
        out_specs=(VM, VM),
        scratch_shapes=[
            pltpu.VMEM((33, B, B), bf16),
            pltpu.VMEM((5, B, B), f32),
            pltpu.SemaphoreType.DMA((10,)),
        ],
        compiler_params=params(12),
        cost_estimate=cost(2 * 64 * B**3, 4 << 20),
        name="aggregate",
    )(plan, tiles, more, *parts, *ready)


def lay_body(ids, *refs):
    own = refs[0:5]
    w_out, og_out, bias_out, rows, sem = refs[6:11]
    yy, xx = ids[1] & 3, ids[1] >> 2
    copies, cols = [], []

    def put(src, dst):
        copies.append(pltpu.make_async_copy(src, dst, sem.at[len(copies)]))
        copies[-1].start()

    for j, off in enumerate((0, -1, 1, 2)):
        for i in range(2):
            k = j * 2 + i
            n, base = (j, i * 784) if j < 3 else (3 + i, 0)
            col = pl.multiple_of((((xx ^ i) << 2) | ((yy + off) & 3)) * B, B)
            cols.append(col)
            for m in range(4):
                put(own[n].at[pl.ds(base + m * B, B), :], w_out.at[pl.ds(k * B, B), pl.ds(m * B, B)])
            put(own[n].at[pl.ds(base + 512, 256), :], og_out.at[:, pl.ds(col, B)])
            put(own[n].at[pl.ds(base + 768, 16), :], rows.at[k])
    for c in copies:
        c.wait()
    for k in range(8):
        bias_out[:, pl.ds(cols[k], B)] = rows[k].astype(f32)[0:8]


def lay_out(ids, own, ready):
    return pl.pallas_call(
        lay_body,
        out_shape=(
            jax.ShapeDtypeStruct((1024, 512), bf16),
            jax.ShapeDtypeStruct((256, 1024), bf16),
            jax.ShapeDtypeStruct((8, 1024), f32),
        ),
        in_specs=[SM] + [HB] * 5 + [ANY],
        out_specs=(VM, VM, VM),
        scratch_shapes=[pltpu.VMEM((8, 16, B), bf16), pltpu.SemaphoreType.DMA((48,))],
        compiler_params=params(8),
        cost_estimate=cost(0, 3 << 20),
        name="lay_out",
    )(ids, *own, ready)


def mid_body(ids, p0, p1, p2, p3, w0, w1, og, bias, w_own, hidden, prop, keep, give, agg, pre, gp, wp):
    x, core = ids[0] >> 4, ids[0] & 1
    for j, p in enumerate((p0, p1, p2, p3)):
        for i in range(2):
            agg[:, (j * 2 + i) * B : (j * 2 + i + 1) * B] = p[i * 256 : (i + 1) * 256, :]
    for w, c in ((w0, core), (w1, 1 - core)):
        for m in range(2):
            cols = pl.ds(pl.multiple_of(c * 512 + m * 256, 256), 256)
            v = jnp.dot(agg[...], w[:, m * 256 : (m + 1) * 256], preferred_element_type=f32)
            v = v + bias[0:1, cols]
            pre[:, cols] = v
            s = jax.nn.sigmoid(v)
            gp[:, cols] = (og[:, cols].astype(f32) * s * (1.0 + v * (1.0 - s))).astype(bf16)
    mine = pl.ds(pl.multiple_of(ids[1] * B, B), B)
    v = pre[:, mine]
    hidden[...] = v * jax.nn.sigmoid(v)
    prop[...] = lax.dot_general(
        gp[...], w_own[...], (((1,), (1,)), ((), ())), preferred_element_type=f32
    ).astype(bf16)
    wp[:, 0:1024] = lax.dot_general(
        agg[:, 0:B], gp[...], (((0,), (0,)), ((), ())), preferred_element_type=f32
    )
    total = jnp.sum(gp[:, mine].astype(f32), axis=0, keepdims=True)
    wp[:, 1024:1152] = jnp.broadcast_to(total, (B, B))
    for ref, c in ((keep, core), (give, 1 - core)):
        for i in range(2):
            ref[i * 32 : (i + 1) * 32, :] = wp[pl.ds(pl.multiple_of(c * 64 + (x ^ i) * 32, 32), 32), :]


def middle(ids, pieces, w0, w1, og, bias, w_own):
    return pl.pallas_call(
        mid_body,
        out_shape=(
            jax.ShapeDtypeStruct((256, B), f32),
            jax.ShapeDtypeStruct((256, B), bf16),
            jax.ShapeDtypeStruct((64, 1152), f32),
            jax.ShapeDtypeStruct((64, 1152), f32),
        ),
        in_specs=[SM] + [VM] * 9,
        out_specs=(VM, VM, VM, VM),
        scratch_shapes=[
            pltpu.VMEM((256, 1024), bf16),
            pltpu.VMEM((256, 1024), f32),
            pltpu.VMEM((256, 1024), bf16),
            pltpu.VMEM((B, 1152), f32),
        ],
        compiler_params=params(),
        cost_estimate=cost(2 * 256 * 1024 * 1280, 5 << 20),
        name="middle",
    )(ids, *pieces, w0, w1, og, bias, w_own)


def spread_body(plan, tiles, more, prop, peer, send, near, far, acc, both):
    acc[...] = jnp.zeros_like(acc)
    both[0:2] = prop[...]
    both[2:4] = peer[...]
    both[4] = jnp.zeros((B, B), bf16)

    def use(tile, slot, dest):
        acc[slot] += lax.dot_general(
            tile, both[dest], (((0,), (0,)), ((), ())), preferred_element_type=f32
        )

    each_tile(plan, tiles, more, use)
    near[...] = acc[0:16]
    far[...] = acc[16:32].astype(bf16)


def spread(plan, tiles, more, prop, peer, send):
    return pl.pallas_call(
        spread_body,
        out_shape=(
            jax.ShapeDtypeStruct((16, B, B), f32),
            jax.ShapeDtypeStruct((16, B, B), bf16),
        ),
        in_specs=[SM] + [VM] * 4 + [ANY],
        out_specs=(VM, VM),
        scratch_shapes=[pltpu.VMEM((33, B, B), f32), pltpu.VMEM((5, B, B), bf16)],
        compiler_params=params(12),
        cost_estimate=cost(2 * 64 * B**3, 6 << 20),
        name="spread",
    )(plan, tiles, more, prop, peer, send)


def quarter_body(keep, got, came, far, out):
    out[...] = (keep[0:32, :] + got[0:32, :] + came[...].astype(f32)).astype(bf16)


def quarter_up(keep, got, came, far):
    return pl.pallas_call(
        quarter_body,
        out_shape=jax.ShapeDtypeStruct((32, 1152), bf16),
        in_specs=[VM] * 3 + [ANY],
        out_specs=VM,
        compiler_params=params(4),
        cost_estimate=cost(0, 1 << 18),
        name="quarter_up",
    )(keep, got, came, far)


def join_body(near, came, ready, t14, t2, t3, t0):
    for ref, n in ((t3, 0), (t2, 4), (t14, 8), (t0, 14)):
        m = n + ref.shape[0]
        ref[...] = (near[n:m] + came[n:m].astype(f32)).astype(ref.dtype)


def join(near, came, ready):
    return pl.pallas_call(
        join_body,
        out_shape=(
            jax.ShapeDtypeStruct((6, B, B), bf16),
            jax.ShapeDtypeStruct((4, B, B), bf16),
            jax.ShapeDtypeStruct((4, B, B), f32),
            jax.ShapeDtypeStruct((2, B, B), f32),
        ),
        in_specs=[VM, VM, ANY],
        out_specs=(VM,) * 4,
        compiler_params=params(8),
        cost_estimate=cost(0, 2 << 20),
        name="join",
    )(near, came, ready)


def ride_body(t3, r14, ready, out):
    out[0:2] = (t3[0:2] + r14[4:6].astype(f32)).astype(bf16)
    out[2:4] = t3[2:4].astype(bf16)


def ride(t3, r14, ready):
    return pl.pallas_call(
        ride_body,
        out_shape=jax.ShapeDtypeStruct((4, B, B), bf16),
        in_specs=[VM, VM, ANY],
        out_specs=VM,
        compiler_params=params(4),
        cost_estimate=cost(0, 1 << 18),
        name="ride",
    )(t3, r14, ready)


def rows_body(d1, d2, d3, t, out):
    for n, d in enumerate((d1, d2, d3)):
        out[32 * n : 32 * n + 32, :] = d[32:64, :]


def peer_rows(d1, d2, d3, t):
    return pl.pallas_call(
        rows_body,
        out_shape=jax.ShapeDtypeStruct((96, 1152), bf16),
        in_specs=[VM] * 3 + [ANY],
        out_specs=VM,
        compiler_params=params(4),
        cost_estimate=cost(0, 1 << 18),
        name="peer_rows",
    )(d1, d2, d3, t)


def sum_body(scale, ids, own, d1, d2, d3, e, t, out, buf):
    core, z = ids[0] & 1, (ids[0] >> 1) & 7
    buf[0] = own[...]
    buf[4] = d1[64:96, :]
    for k, d in ((1, d1), (2, d2), (3, d3)):
        mine = jnp.where(core == 0, k, NZ - k)
        buf[mine] = d[0:32, :]
        buf[NZ - mine] = e[(k - 1) * 32 : k * 32, :]
    acc = buf[(NZ - z) & 7].astype(f32)
    for n in range(1, NZ):
        acc = acc + buf[(n - z) & 7].astype(f32)
    out[...] = (acc * scale).astype(bf16)


def sum_z(scale, ids, *parts):
    return pl.pallas_call(
        functools.partial(sum_body, scale),
        out_shape=jax.ShapeDtypeStruct((32, 1152), bf16),
        in_specs=[SM] + [VM] * 5 + [ANY],
        out_specs=VM,
        scratch_shapes=[pltpu.VMEM((NZ, 32, 1152), bf16)],
        compiler_params=params(8),
        cost_estimate=cost(32 * 1152 * 8, 1 << 20),
        name="sum_z",
    )(ids, *parts)


def wout_body(ids, mine, theirs, w_out, b_out, buf):
    x, core = ids[0] >> 4, ids[0] & 1
    for ref, c in ((mine, core), (theirs, 1 - core)):
        for i in range(2):
            at = pl.multiple_of(c * 64 + (x ^ i) * 32, 32)
            buf[pl.ds(at, 32), :] = ref[i * 32 : (i + 1) * 32, :].astype(f32)
    w_out[...] = buf[:, 0:1024]
    b_out[...] = buf[0:8, 1024:1152]


def weight_out(ids, mine, theirs):
    return pl.pallas_call(
        wout_body,
        out_shape=(jax.ShapeDtypeStruct((B, 1024), f32), jax.ShapeDtypeStruct((8, B), f32)),
        in_specs=[SM, VM, VM],
        out_specs=(VM, VM),
        scratch_shapes=[pltpu.VMEM((B, 1152), f32)],
        compiler_params=params(8),
        cost_estimate=cost(0, 1 << 20),
        name="weight_out",
    )(ids, mine, theirs)


def body(features, weight, bias_vector, adj_tiles, col_blocks, dest_blocks, out_grad):
    ids = jnp.stack([lax.axis_index("row"), lax.axis_index("feat")]).astype(jnp.int32)

    both = jnp.concatenate([features, row_send(features, dc=1)], axis=0)
    x0 = row_send(features, dx=1)
    lists = row_send(jnp.stack([col_blocks, dest_blocks]), dc=1)
    swap, both_a = tie(adj_tiles, both)
    more = row_send(swap, dc=1)
    o3, o2, o1 = (spin_send(both, k, -1) for k in (3, 2, 1))
    o4 = row_send(features, dz=4)
    plan = plan_tiles(ids, col_blocks, dest_blocks, lists[0], lists[1])

    pack = pack_up(ids, weight, out_grad, bias_vector[None, :])
    pack_x = feat_send(pack, dx=1)

    p3, p2, p1, p4 = (row_send(v, dx=1) for v in (o3, o2, o1, o4))
    pair = append(1568, pack, pack_x, o1, o4, x0, p3, p2, plan)
    wu, wd = feat_send(pair, dy=1), feat_send(pair, dy=-1)

    wa, wb = turn(wu, wd, p1, p4)
    mine, theirs = aggregate(plan, adj_tiles, more, (both_a, x0, o4, o1, o2, o3, p4, p1, p2, p3), wa, wb)
    wa, wb = feat_send(wa, dy=1), feat_send(wb, dy=-1)
    aggregated = settle(mine, row_send(theirs, dc=1), wa, wb).reshape(256, B)

    q = jnp.concatenate([aggregated, feat_send(aggregated, dx=1)], axis=0)
    w0, og, bias = lay_out(ids, (pair, wu, wd, wa, wb), q)
    pieces = (q, feat_send(q, dy=1), feat_send(q, dy=-1), feat_send(q, dy=2))
    hidden, prop, keep, give = middle(ids, pieces, w0, row_send(w0, dc=1), og, bias, weight)
    prop = prop.reshape(2, B, B)

    peer = row_send(prop, dc=1)
    got = row_send(give, dc=1)
    send = (keep[32:] + got[32:]).astype(bf16)
    got_x = row_send(send, dx=1)
    near, far = spread(plan, adj_tiles, more, prop, peer, send)
    came = row_send(far, dx=1)
    quarter = quarter_up(keep, got, got_x, far)
    halves = jnp.concatenate([quarter, row_send(quarter, dc=1)], axis=0)
    d3, d2 = spin_send(halves, 3, -1), spin_send(halves, 2, -1)
    last = append(96, halves, d3, d2)
    d1 = spin_send(last, 1, -1)

    t14, t2, t3, t0 = join(near, came, last)
    r14, r2 = spin_send(t14, 1), spin_send(t2, 2)
    t3 = ride(t3, r14, r2)
    r3 = spin_send(t3, 3)

    e = row_send(peer_rows(d1, d2, d3, r14), dc=1)
    scale = float(256 * lax.axis_size("row")) ** (-0.5)
    total = sum_z(scale, ids, quarter, d1, d2, d3, e, t3)
    two = jnp.concatenate([total, row_send(total, dx=1)], axis=0)
    weight_grad, bias_grad = weight_out(ids, two, row_send(two, dc=1))

    r = r14[:4].astype(f32) + r2.astype(f32) + r3.astype(f32)
    out = t0 + r[:2] + row_send(r[2:], dc=1)
    return hidden, out.reshape(256, B), weight_grad, bias_grad[0]


def solution(mesh):
    in_specs = (
        P("row", "feat"),
        P("feat", None),
        P("feat"),
        P("row", None, None),
        P("row"),
        P("row"),
        P("row", "feat"),
    )
    out_specs = (P("row", "feat"), P("row", "feat"), P("feat", None), P("feat"))
    return jax.shard_map(body, mesh=mesh, in_specs=in_specs, out_specs=out_specs, check_vma=False)
```

```python
import functools

import jax
import jax.numpy as jnp
from jax import lax
from jax.experimental import pallas as pl
from jax.experimental.pallas import tpu as pltpu
from jax.sharding import PartitionSpec as P

bf16 = jnp.bfloat16
f32 = jnp.float32
B = 128
NZ = 8
VM = pl.BlockSpec(memory_space=pltpu.VMEM)
SM = pl.BlockSpec(memory_space=pltpu.SMEM)
HB = pl.BlockSpec(memory_space=pltpu.HBM)
ANY = pl.BlockSpec(memory_space=pl.ANY)


def row_send(v, dx=0, dz=0, dc=0):
    perm = []
    for i in range(32):
        x, z, c = i >> 4, (i >> 1) & 7, i & 1
        perm.append((i, ((x ^ dx) << 4) | (((z + dz) % NZ) << 1) | (c ^ dc)))
    return lax.ppermute(v, "row", perm)


def feat_send(v, dx=0, dy=0):
    return lax.ppermute(v, "feat", [(i, (((i >> 2) ^ dx) << 2) | ((i + dy) & 3)) for i in range(8)])


def params(mib=20):
    return pltpu.CompilerParams(vmem_limit_bytes=mib << 20)


def spin_send(v, k, way=1):
    perm = []
    for i in range(32):
        x, z, c = i >> 4, (i >> 1) & 7, i & 1
        perm.append((i, (x << 4) | (((z + way * (k if c == 0 else -k)) % NZ) << 1) | c))
    return lax.ppermute(v, "row", perm)


def tie(a, b):
    return lax.optimization_barrier((a, b))


def cost(flops, nbytes):
    return pl.CostEstimate(flops=flops, bytes_accessed=nbytes, transcendentals=0)


def pack_body(ids, w, og, bias, *refs):
    out, sem = refs[-2:]
    core = ids[0] & 1
    copies = []
    for m in range(4):
        at = pl.multiple_of(core * 512 + m * B, B)
        copies.append(
            pltpu.make_async_copy(w.at[:, pl.ds(at, B)], out.at[m * B : (m + 1) * B, :], sem.at[m])
        )
    copies.append(pltpu.make_async_copy(og, out.at[512:768, :], sem.at[4]))
    for c in copies:
        c.start()
    out[768:784, :] = jnp.broadcast_to(bias[...], (16, B))
    for c in copies:
        c.wait()


def pack_up(ids, w, og, bias, *ready):
    return pl.pallas_call(
        pack_body,
        out_shape=jax.ShapeDtypeStruct((784, B), bf16),
        in_specs=[SM, HB, HB, VM] + [ANY] * len(ready),
        out_specs=VM,
        scratch_shapes=[pltpu.SemaphoreType.DMA((5,))],
        compiler_params=params(60),
        cost_estimate=cost(0, 1 << 19),
        name="pack_up",
    )(ids, w, og, bias, *ready)


def append_body(a, b, *refs):
    out = refs[-1]
    rows = a.shape[0]
    out[0:rows, :] = a[...]
    out[rows:, :] = b[0 : out.shape[0] - rows, :]


def append(n, a, b, *ready):
    return pl.pallas_call(
        append_body,
        out_shape=jax.ShapeDtypeStruct((n, a.shape[1]), a.dtype),
        in_specs=[VM, VM] + [ANY] * len(ready),
        out_specs=VM,
        compiler_params=params(4),
        cost_estimate=cost(0, 1 << 18),
        name="append",
    )(a, b, *ready)


def turn_body(u, d, *refs):
    a, b = refs[-2:]
    a[...] = u[0:784, :]
    b[...] = d[784:1568, :]


def turn(u, d, *ready):
    half = jax.ShapeDtypeStruct((784, B), bf16)
    return pl.pallas_call(
        turn_body,
        out_shape=(half, half),
        in_specs=[VM, VM] + [ANY] * len(ready),
        out_specs=(VM, VM),
        compiler_params=params(4),
        cost_estimate=cost(0, 1 << 18),
        name="turn",
    )(u, d, *ready)


def settle_body(mine, came, a, b, agg):
    agg[...] = (mine[0:2] + came[...]).astype(bf16)


def settle(mine, came, a, b):
    return pl.pallas_call(
        settle_body,
        out_shape=jax.ShapeDtypeStruct((2, B, B), bf16),
        in_specs=[VM, VM, ANY, ANY],
        out_specs=VM,
        compiler_params=params(4),
        cost_estimate=cost(0, 1 << 18),
        name="settle",
    )(mine, came, a, b)


def plan_body(ids, c0, d0, c1, d1, out):
    me = ids[0]
    mx, mz, mc = me >> 4, (me >> 1) & 7, me & 1
    for side, (cols, dest) in enumerate(((c0, d0), (c1, d1))):
        base = 8 + 144 * side

        def step(i, count, cols=cols, dest=dest, base=base, side=side):
            b = cols[i]
            o = b >> 1
            dx, dz, dc = (o >> 4) ^ mx, ((o >> 1) - mz) & 7, (o & 1) ^ mc
            k = jnp.where(mc == 0, dz, NZ - dz)
            edge = (dz & 3) == 0
            held = jnp.where(edge, 1 - dc, jnp.where(k <= 3, 1, 0))
            j = jnp.where(edge, jnp.where(dz == 0, 7, 6), (3 - k) * 2 + dc)
            slot = j * 2 + (b & 1)
            n = jnp.where(dx == 0, count[0], count[1])
            out[base + dx * 72 + n] = i | (slot << 8) | ((dest[i] + 2 * side) << 16)
            return count[0] + held * (1 - dx), count[1] + held * dx

        count = lax.fori_loop(0, 64, step, (0, 0), unroll=8)
        for dx in range(2):
            for u in range(4):
                out[base + dx * 72 + count[dx] + u] = (16 << 8) | (4 << 16)
            out[side * 2 + dx] = (count[dx] + 3) >> 2


def plan_tiles(ids, c0, d0, c1, d1):
    return pl.pallas_call(
        plan_body,
        out_shape=jax.ShapeDtypeStruct((304,), jnp.int32),
        in_specs=[SM] * 5,
        out_specs=SM,
        compiler_params=params(4),
        cost_estimate=cost(10000, 4096),
        name="plan_tiles",
    )(ids, c0, d0, c1, d1)


def each_tile(plan, dx, tiles, more, use):
    for side, ref in enumerate((tiles, more)):
        base = 8 + 144 * side + 72 * dx

        def step(g, carry, base=base, ref=ref):
            for u in range(4):
                e = plan[base + g * 4 + u]
                use(ref[e & 255], (e >> 8) & 255, e >> 16)
            return carry

        lax.fori_loop(0, plan[side * 2 + dx], step, 0)


def agg_body(dx, plan, tiles, more, v3, v2, v14, v0, *refs):
    start, out, src, acc, sem = refs[0], *refs[-4:]
    copies = []
    for n, v in ((0, v3), (4, v2), (8, v14), (14, v0.at[0:2])):
        at = src.at[n : n + v.shape[0]]
        copies.append(pltpu.make_async_copy(v, at, sem.at[len(copies)]))
        copies[-1].start()
    if dx == 0:
        acc[...] = jnp.zeros_like(acc)
    else:
        acc[0:4] = start[...]
    src[16] = jnp.zeros((B, B), bf16)
    for c in copies:
        c.wait()

    def use(tile, slot, dest):
        acc[dest] += jnp.dot(tile, src[slot], preferred_element_type=f32)

    each_tile(plan, dx, tiles, more, use)
    out[...] = acc[0:4]


def aggregate(dx, plan, tiles, more, pieces, start, *ready):
    parts = [v.reshape(-1, B, B) for v in pieces]
    return pl.pallas_call(
        functools.partial(agg_body, dx),
        out_shape=jax.ShapeDtypeStruct((4, B, B), f32),
        in_specs=[SM, VM, VM] + [HB] * 4 + [VM if dx else ANY] + [ANY] * len(ready),
        out_specs=VM,
        scratch_shapes=[
            pltpu.VMEM((17, B, B), bf16),
            pltpu.VMEM((5, B, B), f32),
            pltpu.SemaphoreType.DMA((4,)),
        ],
        compiler_params=params(8),
        cost_estimate=cost(2 * 32 * B**3, 3 << 20),
        name="aggregate",
    )(plan, tiles, more, *parts, start, *ready)


def lay_body(ids, *refs):
    own = refs[0:5]
    w_out, og_out, bias_out, rows, sem = refs[6:11]
    yy, xx = ids[1] & 3, ids[1] >> 2
    copies, cols = [], []

    def put(src, dst):
        copies.append(pltpu.make_async_copy(src, dst, sem.at[len(copies)]))
        copies[-1].start()

    for j, off in enumerate((0, -1, 1, 2)):
        for i in range(2):
            k = j * 2 + i
            n, base = (j, i * 784) if j < 3 else (3 + i, 0)
            col = pl.multiple_of((((xx ^ i) << 2) | ((yy + off) & 3)) * B, B)
            cols.append(col)
            for m in range(4):
                put(own[n].at[pl.ds(base + m * B, B), :], w_out.at[pl.ds(k * B, B), pl.ds(m * B, B)])
            put(own[n].at[pl.ds(base + 512, 256), :], og_out.at[:, pl.ds(col, B)])
            put(own[n].at[pl.ds(base + 768, 16), :], rows.at[k])
    for c in copies:
        c.wait()
    for k in range(8):
        bias_out[:, pl.ds(cols[k], B)] = rows[k].astype(f32)[0:8]


def lay_out(ids, own, ready):
    return pl.pallas_call(
        lay_body,
        out_shape=(
            jax.ShapeDtypeStruct((1024, 512), bf16),
            jax.ShapeDtypeStruct((256, 1024), bf16),
            jax.ShapeDtypeStruct((8, 1024), f32),
        ),
        in_specs=[SM] + [HB] * 5 + [ANY],
        out_specs=(VM, VM, VM),
        scratch_shapes=[pltpu.VMEM((8, 16, B), bf16), pltpu.SemaphoreType.DMA((48,))],
        compiler_params=params(8),
        cost_estimate=cost(0, 3 << 20),
        name="lay_out",
    )(ids, *own, ready)


def mid_body(ids, p0, p1, p2, p3, w0, w1, og, bias, w_own, hidden, prop, keep, give, agg, pre, gp, wp):
    x, core = ids[0] >> 4, ids[0] & 1
    for j, p in enumerate((p0, p1, p2, p3)):
        for i in range(2):
            agg[:, (j * 2 + i) * B : (j * 2 + i + 1) * B] = p[i * 256 : (i + 1) * 256, :]
    for w, c in ((w0, core), (w1, 1 - core)):
        for m in range(2):
            cols = pl.ds(pl.multiple_of(c * 512 + m * 256, 256), 256)
            v = jnp.dot(agg[...], w[:, m * 256 : (m + 1) * 256], preferred_element_type=f32)
            v = v + bias[0:1, cols]
            pre[:, cols] = v
            s = jax.nn.sigmoid(v)
            gp[:, cols] = (og[:, cols].astype(f32) * s * (1.0 + v * (1.0 - s))).astype(bf16)
    mine = pl.ds(pl.multiple_of(ids[1] * B, B), B)
    v = pre[:, mine]
    hidden[...] = v * jax.nn.sigmoid(v)
    prop[...] = lax.dot_general(
        gp[...], w_own[...], (((1,), (1,)), ((), ())), preferred_element_type=f32
    ).astype(bf16)
    wp[:, 0:1024] = lax.dot_general(
        agg[:, 0:B], gp[...], (((0,), (0,)), ((), ())), preferred_element_type=f32
    )
    total = jnp.sum(gp[:, mine].astype(f32), axis=0, keepdims=True)
    wp[:, 1024:1152] = jnp.broadcast_to(total, (B, B))
    for ref, c in ((keep, core), (give, 1 - core)):
        for i in range(2):
            ref[i * 32 : (i + 1) * 32, :] = wp[pl.ds(pl.multiple_of(c * 64 + (x ^ i) * 32, 32), 32), :]


def middle(ids, pieces, w0, w1, og, bias, w_own):
    return pl.pallas_call(
        mid_body,
        out_shape=(
            jax.ShapeDtypeStruct((256, B), f32),
            jax.ShapeDtypeStruct((256, B), bf16),
            jax.ShapeDtypeStruct((64, 1152), f32),
            jax.ShapeDtypeStruct((64, 1152), f32),
        ),
        in_specs=[SM] + [VM] * 9,
        out_specs=(VM, VM, VM, VM),
        scratch_shapes=[
            pltpu.VMEM((256, 1024), bf16),
            pltpu.VMEM((256, 1024), f32),
            pltpu.VMEM((256, 1024), bf16),
            pltpu.VMEM((B, 1152), f32),
        ],
        compiler_params=params(),
        cost_estimate=cost(2 * 256 * 1024 * 1280, 5 << 20),
        name="middle",
    )(ids, *pieces, w0, w1, og, bias, w_own)


def spread_body(dx, plan, tiles, more, prop, peer, ready, out, acc, both):
    acc[...] = jnp.zeros_like(acc)
    both[0:2] = prop[...]
    both[2:4] = peer[...]
    both[4] = jnp.zeros((B, B), bf16)

    def use(tile, slot, dest):
        acc[slot] += lax.dot_general(
            tile, both[dest], (((0,), (0,)), ((), ())), preferred_element_type=f32
        )

    each_tile(plan, dx, tiles, more, use)
    out[...] = acc[0:16].astype(out.dtype)


def spread(dx, plan, tiles, more, prop, peer, ready):
    return pl.pallas_call(
        functools.partial(spread_body, dx),
        out_shape=jax.ShapeDtypeStruct((16, B, B), bf16 if dx else f32),
        in_specs=[SM] + [VM] * 4 + [ANY],
        out_specs=VM,
        scratch_shapes=[pltpu.VMEM((17, B, B), f32), pltpu.VMEM((5, B, B), bf16)],
        compiler_params=params(8),
        cost_estimate=cost(2 * 32 * B**3, 4 << 20),
        name="spread",
    )(plan, tiles, more, prop, peer, ready)


def quarter_body(keep, got, came, far, out):
    out[...] = (keep[0:32, :] + got[0:32, :] + came[...].astype(f32)).astype(bf16)


def quarter_up(keep, got, came, far):
    return pl.pallas_call(
        quarter_body,
        out_shape=jax.ShapeDtypeStruct((32, 1152), bf16),
        in_specs=[VM] * 3 + [ANY],
        out_specs=VM,
        compiler_params=params(4),
        cost_estimate=cost(0, 1 << 18),
        name="quarter_up",
    )(keep, got, came, far)


def join_body(near, came, ready, t14, t2, t3, t0):
    t3[...] = near[0:4] + came[0:4].astype(f32)
    t2[...] = (near[4:8] + came[4:8].astype(f32)).astype(bf16)
    t14[...] = (near[8:14] + came[8:14].astype(f32)).astype(bf16)
    t0[...] = near[14:16] + came[14:16].astype(f32)


def join(near, came, ready):
    return pl.pallas_call(
        join_body,
        out_shape=(
            jax.ShapeDtypeStruct((6, B, B), bf16),
            jax.ShapeDtypeStruct((4, B, B), bf16),
            jax.ShapeDtypeStruct((4, B, B), f32),
            jax.ShapeDtypeStruct((2, B, B), f32),
        ),
        in_specs=[VM, VM, ANY],
        out_specs=(VM, VM, VM, VM),
        compiler_params=params(8),
        cost_estimate=cost(0, 2 << 20),
        name="join",
    )(near, came, ready)


def ride_body(t3, r14, out):
    out[0:2] = (t3[0:2] + r14[4:6].astype(f32)).astype(bf16)
    out[2:4] = t3[2:4].astype(bf16)


def ride(t3, r14):
    return pl.pallas_call(
        ride_body,
        out_shape=jax.ShapeDtypeStruct((4, B, B), bf16),
        in_specs=[VM, VM],
        out_specs=VM,
        compiler_params=params(4),
        cost_estimate=cost(0, 1 << 18),
        name="ride",
    )(t3, r14)


def rows_body(d1, d2, d3, t, out):
    for n, d in enumerate((d1, d2, d3)):
        out[32 * n : 32 * n + 32, :] = d[32:64, :]


def peer_rows(d1, d2, d3, t):
    return pl.pallas_call(
        rows_body,
        out_shape=jax.ShapeDtypeStruct((96, 1152), bf16),
        in_specs=[VM] * 3 + [ANY],
        out_specs=VM,
        compiler_params=params(4),
        cost_estimate=cost(0, 1 << 18),
        name="peer_rows",
    )(d1, d2, d3, t)


def sum_body(scale, ids, own, d1, d2, d3, e, t, out, buf):
    core, z = ids[0] & 1, (ids[0] >> 1) & 7
    buf[0] = own[...]
    buf[4] = d1[64:96, :]
    for k, d in ((1, d1), (2, d2), (3, d3)):
        mine = jnp.where(core == 0, k, NZ - k)
        buf[mine] = d[0:32, :]
        buf[NZ - mine] = e[(k - 1) * 32 : k * 32, :]
    acc = buf[(NZ - z) & 7].astype(f32)
    for n in range(1, NZ):
        acc = acc + buf[(n - z) & 7].astype(f32)
    out[...] = (acc * scale).astype(bf16)


def sum_z(scale, ids, *parts):
    return pl.pallas_call(
        functools.partial(sum_body, scale),
        out_shape=jax.ShapeDtypeStruct((32, 1152), bf16),
        in_specs=[SM] + [VM] * 5 + [ANY],
        out_specs=VM,
        scratch_shapes=[pltpu.VMEM((NZ, 32, 1152), bf16)],
        compiler_params=params(8),
        cost_estimate=cost(32 * 1152 * 8, 1 << 20),
        name="sum_z",
    )(ids, *parts)


def wout_body(ids, mine, theirs, w_out, b_out, buf):
    x, core = ids[0] >> 4, ids[0] & 1
    for ref, c in ((mine, core), (theirs, 1 - core)):
        for i in range(2):
            at = pl.multiple_of(c * 64 + (x ^ i) * 32, 32)
            buf[pl.ds(at, 32), :] = ref[i * 32 : (i + 1) * 32, :].astype(f32)
    w_out[...] = buf[:, 0:1024]
    b_out[...] = buf[0:8, 1024:1152]


def weight_out(ids, mine, theirs):
    return pl.pallas_call(
        wout_body,
        out_shape=(jax.ShapeDtypeStruct((B, 1024), f32), jax.ShapeDtypeStruct((8, B), f32)),
        in_specs=[SM, VM, VM],
        out_specs=(VM, VM),
        scratch_shapes=[pltpu.VMEM((B, 1152), f32)],
        compiler_params=params(8),
        cost_estimate=cost(0, 1 << 20),
        name="weight_out",
    )(ids, mine, theirs)


def body(features, weight, bias_vector, adj_tiles, col_blocks, dest_blocks, out_grad):
    ids = jnp.stack([lax.axis_index("row"), lax.axis_index("feat")]).astype(jnp.int32)

    both = jnp.concatenate([features, row_send(features, dc=1)], axis=0)
    x0 = row_send(features, dx=1)
    lists = row_send(jnp.stack([col_blocks, dest_blocks]), dc=1)
    swap, both_a = tie(adj_tiles, both)
    more = row_send(swap, dc=1)
    o3, o2 = spin_send(both, 3, -1), spin_send(both, 2, -1)
    plan = plan_tiles(ids, col_blocks, dest_blocks, lists[0], lists[1])

    pack = pack_up(ids, weight, out_grad, bias_vector[None, :])
    pack_x = feat_send(pack, dx=1)

    pair = append(1568, pack, pack_x, o3, o2, x0)
    o14 = spin_send(append(768, both, o3), 1, -1)
    p3, p2, p14 = row_send(o3, dx=1), row_send(o2, dx=1), row_send(o14, dx=1)
    wu, wd = feat_send(pair, dy=1), feat_send(pair, dy=-1)

    wa, wb = turn(wu, wd, plan, p3, p2)
    sums = aggregate(0, plan, adj_tiles, more, (o3, o2, o14, both_a), ids)
    sums = aggregate(1, plan, adj_tiles, more, (p3, p2, p14, x0), sums, wa, wb)
    wa, wb = feat_send(wa, dy=1), feat_send(wb, dy=-1)
    aggregated = settle(sums, row_send(sums[2:], dc=1), wa, wb).reshape(256, B)

    q = jnp.concatenate([aggregated, feat_send(aggregated, dx=1)], axis=0)
    w0, og, bias = lay_out(ids, (pair, wu, wd, wa, wb), q)
    pieces = (q, feat_send(q, dy=1), feat_send(q, dy=-1), feat_send(q, dy=2))
    hidden, prop, keep, give = middle(ids, pieces, w0, row_send(w0, dc=1), og, bias, weight)
    prop = prop.reshape(2, B, B)

    peer = row_send(prop, dc=1)
    got = row_send(give, dc=1)
    send = (keep[32:] + got[32:]).astype(bf16)
    got_x = row_send(send, dx=1)
    far = spread(1, plan, adj_tiles, more, prop, peer, send)
    came = row_send(far, dx=1)
    near = spread(0, plan, adj_tiles, more, prop, peer, far)
    quarter = quarter_up(keep, got, got_x, near)
    halves = jnp.concatenate([quarter, row_send(quarter, dc=1)], axis=0)
    d3, d2 = spin_send(halves, 3, -1), spin_send(halves, 2, -1)
    last = append(96, halves, d3, d2)
    d1 = spin_send(last, 1, -1)

    t14, t2, t3, t0 = join(near, came, last)
    r14, r2 = spin_send(t14, 1), spin_send(t2, 2)
    t3 = ride(t3, r14)
    r3 = spin_send(t3, 3)

    e = row_send(peer_rows(d1, d2, d3, r2), dc=1)
    scale = float(256 * lax.axis_size("row")) ** (-0.5)
    total = sum_z(scale, ids, quarter, d1, d2, d3, e, t3)
    two = jnp.concatenate([total, row_send(total, dx=1)], axis=0)
    weight_grad, bias_grad = weight_out(ids, two, row_send(two, dc=1))

    r = r14[:4].astype(f32) + r2.astype(f32) + r3.astype(f32)
    out = t0 + r[:2] + row_send(r[2:], dc=1)
    return hidden, out.reshape(256, B), weight_grad, bias_grad[0]


def solution(mesh):
    in_specs = (
        P("row", "feat"),
        P("feat", None),
        P("feat"),
        P("row", None, None),
        P("row"),
        P("row"),
        P("row", "feat"),
    )
    out_specs = (P("row", "feat"), P("row", "feat"), P("feat", None), P("feat"))
    return jax.shard_map(body, mesh=mesh, in_specs=in_specs, out_specs=out_specs, check_vma=False)
```

```python
import functools

import jax
import jax.numpy as jnp
from jax import lax
from jax.experimental import pallas as pl
from jax.experimental.pallas import tpu as pltpu
from jax.sharding import PartitionSpec as P

bf16 = jnp.bfloat16
f32 = jnp.float32
B = 128
NZ = 8
VM = pl.BlockSpec(memory_space=pltpu.VMEM)
SM = pl.BlockSpec(memory_space=pltpu.SMEM)
HB = pl.BlockSpec(memory_space=pltpu.HBM)
ANY = pl.BlockSpec(memory_space=pl.ANY)


def row_send(v, dx=0, dz=0, dc=0):
    perm = []
    for i in range(32):
        x, z, c = i >> 4, (i >> 1) & 7, i & 1
        perm.append((i, ((x ^ dx) << 4) | (((z + dz) % NZ) << 1) | (c ^ dc)))
    return lax.ppermute(v, "row", perm)


def feat_send(v, dx=0, dy=0):
    return lax.ppermute(v, "feat", [(i, (((i >> 2) ^ dx) << 2) | ((i + dy) & 3)) for i in range(8)])


def params(mib=20):
    return pltpu.CompilerParams(vmem_limit_bytes=mib << 20)


def spin_send(v, k, way=1):
    perm = []
    for i in range(32):
        x, z, c = i >> 4, (i >> 1) & 7, i & 1
        perm.append((i, (x << 4) | (((z + way * (k if c == 0 else -k)) % NZ) << 1) | c))
    return lax.ppermute(v, "row", perm)


def tie(a, b):
    return lax.optimization_barrier((a, b))


def cost(flops, nbytes):
    return pl.CostEstimate(flops=flops, bytes_accessed=nbytes, transcendentals=0)


def pack_body(ids, w, og, bias, *refs):
    out, sem = refs[-2:]
    core = ids[0] & 1
    copies = []
    for m in range(4):
        at = pl.multiple_of(core * 512 + m * B, B)
        copies.append(
            pltpu.make_async_copy(w.at[:, pl.ds(at, B)], out.at[m * B : (m + 1) * B, :], sem.at[m])
        )
    copies.append(pltpu.make_async_copy(og, out.at[512:768, :], sem.at[4]))
    for c in copies:
        c.start()
    out[768:784, :] = jnp.broadcast_to(bias[...], (16, B))
    for c in copies:
        c.wait()


def pack_up(ids, w, og, bias, *ready):
    return pl.pallas_call(
        pack_body,
        out_shape=jax.ShapeDtypeStruct((784, B), bf16),
        in_specs=[SM, HB, HB, VM] + [ANY] * len(ready),
        out_specs=VM,
        scratch_shapes=[pltpu.SemaphoreType.DMA((5,))],
        compiler_params=params(60),
        cost_estimate=cost(0, 1 << 19),
        name="pack_up",
    )(ids, w, og, bias, *ready)


def append_body(a, b, *refs):
    out = refs[-1]
    rows = a.shape[0]
    out[0:rows, :] = a[...]
    out[rows:, :] = b[0 : out.shape[0] - rows, :]


def append(n, a, b, *ready):
    return pl.pallas_call(
        append_body,
        out_shape=jax.ShapeDtypeStruct((n, a.shape[1]), a.dtype),
        in_specs=[VM, VM] + [ANY] * len(ready),
        out_specs=VM,
        compiler_params=params(4),
        cost_estimate=cost(0, 1 << 18),
        name="append",
    )(a, b, *ready)


def turn_body(u, d, *refs):
    a, b = refs[-2:]
    a[...] = u[0:784, :]
    b[...] = d[784:1568, :]


def turn(u, d, *ready):
    half = jax.ShapeDtypeStruct((784, B), bf16)
    return pl.pallas_call(
        turn_body,
        out_shape=(half, half),
        in_specs=[VM, VM] + [ANY] * len(ready),
        out_specs=(VM, VM),
        compiler_params=params(4),
        cost_estimate=cost(0, 1 << 18),
        name="turn",
    )(u, d, *ready)


def hold_body(v, r0, r1, out):
    out[...] = v[...]


def hold(v, *ready):
    return pl.pallas_call(
        hold_body,
        out_shape=jax.ShapeDtypeStruct(v.shape, v.dtype),
        in_specs=[VM, ANY, ANY],
        out_specs=VM,
        compiler_params=params(4),
        cost_estimate=cost(0, 1 << 18),
        name="hold",
    )(v, *ready)


def settle_body(mine, came, a, b, agg):
    agg[...] = (mine[...] + came[...]).astype(bf16)


def settle(mine, came, a, b):
    return pl.pallas_call(
        settle_body,
        out_shape=jax.ShapeDtypeStruct((2, B, B), bf16),
        in_specs=[VM, VM, ANY, ANY],
        out_specs=VM,
        compiler_params=params(4),
        cost_estimate=cost(0, 1 << 18),
        name="settle",
    )(mine, came, a, b)


def plan_body(ids, c0, d0, c1, d1, out):
    me = ids[0]
    mx, mz, mc = me >> 4, (me >> 1) & 7, me & 1
    for side, (cols, dest) in enumerate(((c0, d0), (c1, d1))):
        base = 8 + 72 * side

        def step(i, n, cols=cols, dest=dest, base=base, side=side):
            b = cols[i]
            o = b >> 1
            dx, dz, dc = (o >> 4) ^ mx, ((o >> 1) - mz) & 7, (o & 1) ^ mc
            k = jnp.where(mc == 0, dz, NZ - dz)
            edge = (dz & 3) == 0
            held = jnp.where(edge, 1 - dc, jnp.where(k <= 3, 1, 0))
            j = jnp.where(edge, jnp.where(dz == 0, 7, 6), (3 - k) * 2 + dc)
            slot = dx * 16 + j * 2 + (b & 1)
            out[base + n] = i | (slot << 8) | ((dest[i] + 2 * side) << 16)
            return n + held

        n = lax.fori_loop(0, 64, step, 0, unroll=8)
        for u in range(4):
            out[base + n + u] = (32 << 8) | (4 << 16)
        out[side] = (n + 3) >> 2


def plan_tiles(ids, c0, d0, c1, d1):
    return pl.pallas_call(
        plan_body,
        out_shape=jax.ShapeDtypeStruct((160,), jnp.int32),
        in_specs=[SM] * 5,
        out_specs=SM,
        compiler_params=params(4),
        cost_estimate=cost(10000, 4096),
        name="plan_tiles",
    )(ids, c0, d0, c1, d1)


def each_tile(plan, tiles, more, use):
    for side, ref in enumerate((tiles, more)):
        def step(g, carry, side=side, ref=ref):
            for u in range(4):
                e = plan[8 + 72 * side + g * 4 + u]
                use(ref[e & 255], (e >> 8) & 255, e >> 16)
            return carry

        lax.fori_loop(0, plan[side], step, 0)


def agg_body(plan, tiles, more, *refs):
    mine, theirs, src, acc, sem = refs[10:]
    both, x0, o14, o2, o3, p14, p2, p3 = refs[0:8]
    copies = []

    def put(dx, j, v):
        n = v.shape[0]
        at = dx * 16 + j * 2
        copies.append(pltpu.make_async_copy(v, src.at[at : at + n], sem.at[len(copies)]))
        copies[-1].start()

    for dx, (v3, v2, v14, v0) in enumerate(((o3, o2, o14, both.at[0:2]), (p3, p2, p14, x0))):
        for j, v in ((0, v3), (2, v2), (4, v14), (7, v0)):
            put(dx, j, v)
    acc[...] = jnp.zeros_like(acc)
    src[32] = jnp.zeros((B, B), bf16)
    for c in copies:
        c.wait()

    def use(tile, slot, dest):
        acc[dest] += jnp.dot(tile, src[slot], preferred_element_type=f32)

    each_tile(plan, tiles, more, use)
    mine[...] = acc[0:2]
    theirs[...] = acc[2:4]


def aggregate(plan, tiles, more, pieces, *ready):
    parts = [v.reshape(-1, B, B) for v in pieces]
    return pl.pallas_call(
        agg_body,
        out_shape=(jax.ShapeDtypeStruct((2, B, B), f32), jax.ShapeDtypeStruct((2, B, B), f32)),
        in_specs=[SM, VM, VM] + [HB] * 8 + [ANY] * 2,
        out_specs=(VM, VM),
        scratch_shapes=[
            pltpu.VMEM((33, B, B), bf16),
            pltpu.VMEM((5, B, B), f32),
            pltpu.SemaphoreType.DMA((8,)),
        ],
        compiler_params=params(12),
        cost_estimate=cost(2 * 64 * B**3, 4 << 20),
        name="aggregate",
    )(plan, tiles, more, *parts, *ready)


def lay_body(ids, *refs):
    own = refs[0:5]
    w_out, og_out, bias_out, rows, sem = refs[6:11]
    yy, xx = ids[1] & 3, ids[1] >> 2
    copies, cols = [], []

    def put(src, dst):
        copies.append(pltpu.make_async_copy(src, dst, sem.at[len(copies)]))
        copies[-1].start()

    for j, off in enumerate((0, -1, 1, 2)):
        for i in range(2):
            k = j * 2 + i
            n, base = (j, i * 784) if j < 3 else (3 + i, 0)
            col = pl.multiple_of((((xx ^ i) << 2) | ((yy + off) & 3)) * B, B)
            cols.append(col)
            for m in range(4):
                put(own[n].at[pl.ds(base + m * B, B), :], w_out.at[pl.ds(k * B, B), pl.ds(m * B, B)])
            put(own[n].at[pl.ds(base + 512, 256), :], og_out.at[:, pl.ds(col, B)])
            put(own[n].at[pl.ds(base + 768, 16), :], rows.at[k])
    for c in copies:
        c.wait()
    for k in range(8):
        bias_out[:, pl.ds(cols[k], B)] = rows[k].astype(f32)[0:8]


def lay_out(ids, own, ready):
    return pl.pallas_call(
        lay_body,
        out_shape=(
            jax.ShapeDtypeStruct((1024, 512), bf16),
            jax.ShapeDtypeStruct((256, 1024), bf16),
            jax.ShapeDtypeStruct((8, 1024), f32),
        ),
        in_specs=[SM] + [HB] * 5 + [ANY],
        out_specs=(VM, VM, VM),
        scratch_shapes=[pltpu.VMEM((8, 16, B), bf16), pltpu.SemaphoreType.DMA((48,))],
        compiler_params=params(8),
        cost_estimate=cost(0, 3 << 20),
        name="lay_out",
    )(ids, *own, ready)


def mid_body(ids, p0, p1, p2, p3, w0, w1, og, bias, w_own, hidden, prop, keep, give, agg, pre, gp, wp):
    x, core = ids[0] >> 4, ids[0] & 1
    for j, p in enumerate((p0, p1, p2, p3)):
        for i in range(2):
            agg[:, (j * 2 + i) * B : (j * 2 + i + 1) * B] = p[i * 256 : (i + 1) * 256, :]
    for w, c in ((w0, core), (w1, 1 - core)):
        for m in range(2):
            cols = pl.ds(pl.multiple_of(c * 512 + m * 256, 256), 256)
            v = jnp.dot(agg[...], w[:, m * 256 : (m + 1) * 256], preferred_element_type=f32)
            v = v + bias[0:1, cols]
            pre[:, cols] = v
            s = jax.nn.sigmoid(v)
            gp[:, cols] = (og[:, cols].astype(f32) * s * (1.0 + v * (1.0 - s))).astype(bf16)
    mine = pl.ds(pl.multiple_of(ids[1] * B, B), B)
    v = pre[:, mine]
    hidden[...] = v * jax.nn.sigmoid(v)
    prop[...] = lax.dot_general(
        gp[...], w_own[...], (((1,), (1,)), ((), ())), preferred_element_type=f32
    ).astype(bf16)
    wp[:, 0:1024] = lax.dot_general(
        agg[:, 0:B], gp[...], (((0,), (0,)), ((), ())), preferred_element_type=f32
    )
    total = jnp.sum(gp[:, mine].astype(f32), axis=0, keepdims=True)
    wp[:, 1024:1152] = jnp.broadcast_to(total, (B, B))
    for ref, c in ((keep, core), (give, 1 - core)):
        for i in range(2):
            ref[i * 32 : (i + 1) * 32, :] = wp[pl.ds(pl.multiple_of(c * 64 + (x ^ i) * 32, 32), 32), :]


def middle(ids, pieces, w0, w1, og, bias, w_own):
    return pl.pallas_call(
        mid_body,
        out_shape=(
            jax.ShapeDtypeStruct((256, B), f32),
            jax.ShapeDtypeStruct((256, B), bf16),
            jax.ShapeDtypeStruct((64, 1152), f32),
            jax.ShapeDtypeStruct((64, 1152), f32),
        ),
        in_specs=[SM] + [VM] * 9,
        out_specs=(VM, VM, VM, VM),
        scratch_shapes=[
            pltpu.VMEM((256, 1024), bf16),
            pltpu.VMEM((256, 1024), f32),
            pltpu.VMEM((256, 1024), bf16),
            pltpu.VMEM((B, 1152), f32),
        ],
        compiler_params=params(),
        cost_estimate=cost(2 * 256 * 1024 * 1280, 5 << 20),
        name="middle",
    )(ids, *pieces, w0, w1, og, bias, w_own)


def spread_body(plan, tiles, more, prop, peer, send, near, far, acc, both):
    acc[...] = jnp.zeros_like(acc)
    both[0:2] = prop[...]
    both[2:4] = peer[...]
    both[4] = jnp.zeros((B, B), bf16)

    def use(tile, slot, dest):
        acc[slot] += lax.dot_general(
            tile, both[dest], (((0,), (0,)), ((), ())), preferred_element_type=f32
        )

    each_tile(plan, tiles, more, use)
    near[...] = acc[0:16]
    far[...] = acc[16:32].astype(bf16)


def spread(plan, tiles, more, prop, peer, send):
    return pl.pallas_call(
        spread_body,
        out_shape=(
            jax.ShapeDtypeStruct((16, B, B), f32),
            jax.ShapeDtypeStruct((16, B, B), bf16),
        ),
        in_specs=[SM] + [VM] * 4 + [ANY],
        out_specs=(VM, VM),
        scratch_shapes=[pltpu.VMEM((33, B, B), f32), pltpu.VMEM((5, B, B), bf16)],
        compiler_params=params(12),
        cost_estimate=cost(2 * 64 * B**3, 6 << 20),
        name="spread",
    )(plan, tiles, more, prop, peer, send)


def quarter_body(keep, got, came, far, out):
    out[...] = (keep[0:32, :] + got[0:32, :] + came[...].astype(f32)).astype(bf16)


def quarter_up(keep, got, came, far):
    return pl.pallas_call(
        quarter_body,
        out_shape=jax.ShapeDtypeStruct((32, 1152), bf16),
        in_specs=[VM] * 3 + [ANY],
        out_specs=VM,
        compiler_params=params(4),
        cost_estimate=cost(0, 1 << 18),
        name="quarter_up",
    )(keep, got, came, far)


def join_body(near, came, ready, t14, t2, t3, t0):
    t3[...] = near[0:4] + came[0:4].astype(f32)
    t2[...] = (near[4:8] + came[4:8].astype(f32)).astype(bf16)
    t14[...] = (near[8:14] + came[8:14].astype(f32)).astype(bf16)
    t0[...] = near[14:16] + came[14:16].astype(f32)


def join(near, came, ready):
    return pl.pallas_call(
        join_body,
        out_shape=(
            jax.ShapeDtypeStruct((6, B, B), bf16),
            jax.ShapeDtypeStruct((4, B, B), bf16),
            jax.ShapeDtypeStruct((4, B, B), f32),
            jax.ShapeDtypeStruct((2, B, B), f32),
        ),
        in_specs=[VM, VM, ANY],
        out_specs=(VM, VM, VM, VM),
        compiler_params=params(8),
        cost_estimate=cost(0, 2 << 20),
        name="join",
    )(near, came, ready)


def ride_body(t3, r14, out):
    out[0:2] = (t3[0:2] + r14[4:6].astype(f32)).astype(bf16)
    out[2:4] = t3[2:4].astype(bf16)


def ride(t3, r14):
    return pl.pallas_call(
        ride_body,
        out_shape=jax.ShapeDtypeStruct((4, B, B), bf16),
        in_specs=[VM, VM],
        out_specs=VM,
        compiler_params=params(4),
        cost_estimate=cost(0, 1 << 18),
        name="ride",
    )(t3, r14)


def rows_body(d1, d2, d3, t, out):
    for n, d in enumerate((d1, d2, d3)):
        out[32 * n : 32 * n + 32, :] = d[32:64, :]


def peer_rows(d1, d2, d3, t):
    return pl.pallas_call(
        rows_body,
        out_shape=jax.ShapeDtypeStruct((96, 1152), bf16),
        in_specs=[VM] * 3 + [ANY],
        out_specs=VM,
        compiler_params=params(4),
        cost_estimate=cost(0, 1 << 18),
        name="peer_rows",
    )(d1, d2, d3, t)


def sum_body(scale, ids, own, d1, d2, d3, e, t, out, buf):
    core, z = ids[0] & 1, (ids[0] >> 1) & 7
    buf[0] = own[...]
    buf[4] = d1[64:96, :]
    for k, d in ((1, d1), (2, d2), (3, d3)):
        mine = jnp.where(core == 0, k, NZ - k)
        buf[mine] = d[0:32, :]
        buf[NZ - mine] = e[(k - 1) * 32 : k * 32, :]
    acc = buf[(NZ - z) & 7].astype(f32)
    for n in range(1, NZ):
        acc = acc + buf[(n - z) & 7].astype(f32)
    out[...] = (acc * scale).astype(bf16)


def sum_z(scale, ids, *parts):
    return pl.pallas_call(
        functools.partial(sum_body, scale),
        out_shape=jax.ShapeDtypeStruct((32, 1152), bf16),
        in_specs=[SM] + [VM] * 5 + [ANY],
        out_specs=VM,
        scratch_shapes=[pltpu.VMEM((NZ, 32, 1152), bf16)],
        compiler_params=params(8),
        cost_estimate=cost(32 * 1152 * 8, 1 << 20),
        name="sum_z",
    )(ids, *parts)


def wout_body(ids, mine, theirs, w_out, b_out, buf):
    x, core = ids[0] >> 4, ids[0] & 1
    for ref, c in ((mine, core), (theirs, 1 - core)):
        for i in range(2):
            at = pl.multiple_of(c * 64 + (x ^ i) * 32, 32)
            buf[pl.ds(at, 32), :] = ref[i * 32 : (i + 1) * 32, :].astype(f32)
    w_out[...] = buf[:, 0:1024]
    b_out[...] = buf[0:8, 1024:1152]


def weight_out(ids, mine, theirs):
    return pl.pallas_call(
        wout_body,
        out_shape=(jax.ShapeDtypeStruct((B, 1024), f32), jax.ShapeDtypeStruct((8, B), f32)),
        in_specs=[SM, VM, VM],
        out_specs=(VM, VM),
        scratch_shapes=[pltpu.VMEM((B, 1152), f32)],
        compiler_params=params(8),
        cost_estimate=cost(0, 1 << 20),
        name="weight_out",
    )(ids, mine, theirs)


def body(features, weight, bias_vector, adj_tiles, col_blocks, dest_blocks, out_grad):
    ids = jnp.stack([lax.axis_index("row"), lax.axis_index("feat")]).astype(jnp.int32)

    both = jnp.concatenate([features, row_send(features, dc=1)], axis=0)
    x0 = row_send(features, dx=1)
    lists = row_send(jnp.stack([col_blocks, dest_blocks]), dc=1)
    swap, both_a = tie(adj_tiles, both)
    more = row_send(swap, dc=1)
    o3, o2 = spin_send(both, 3, -1), spin_send(both, 2, -1)
    plan = plan_tiles(ids, col_blocks, dest_blocks, lists[0], lists[1])

    pack = pack_up(ids, weight, out_grad, bias_vector[None, :])
    pack_x = feat_send(pack, dx=1)

    pair = append(1568, pack, pack_x, o3, o2, x0)
    o14 = spin_send(append(768, both, o3, lists), 1, -1)
    p3, p2 = row_send(o3, dx=1), row_send(o2, dx=1)
    p14 = row_send(hold(o14, p3, p2), dx=1)
    wu, wd = feat_send(pair, dy=1), feat_send(pair, dy=-1)

    wa, wb = turn(wu, wd, p14, plan)
    mine, theirs = aggregate(plan, adj_tiles, more, (both_a, x0, o14, o2, o3, p14, p2, p3), wa, wb)
    wa, wb = feat_send(wa, dy=1), feat_send(wb, dy=-1)
    aggregated = settle(mine, row_send(theirs, dc=1), wa, wb).reshape(256, B)

    q = jnp.concatenate([aggregated, feat_send(aggregated, dx=1)], axis=0)
    w0, og, bias = lay_out(ids, (pair, wu, wd, wa, wb), q)
    pieces = (q, feat_send(q, dy=1), feat_send(q, dy=-1), feat_send(q, dy=2))
    hidden, prop, keep, give = middle(ids, pieces, w0, row_send(w0, dc=1), og, bias, weight)
    prop = prop.reshape(2, B, B)

    peer = row_send(prop, dc=1)
    got = row_send(give, dc=1)
    send = (keep[32:] + got[32:]).astype(bf16)
    got_x = row_send(send, dx=1)
    near, far = spread(plan, adj_tiles, more, prop, peer, send)
    came = row_send(far, dx=1)
    quarter = quarter_up(keep, got, got_x, far)
    halves = jnp.concatenate([quarter, row_send(quarter, dc=1)], axis=0)
    d3, d2 = spin_send(halves, 3, -1), spin_send(halves, 2, -1)
    last = append(96, halves, d3, d2)
    d1 = spin_send(last, 1, -1)

    t14, t2, t3, t0 = join(near, came, halves)
    r14, r2 = spin_send(t14, 1), spin_send(t2, 2)
    t3 = ride(t3, r14)
    r3 = spin_send(t3, 3)

    e = row_send(peer_rows(d1, d2, d3, r2), dc=1)
    scale = float(256 * lax.axis_size("row")) ** (-0.5)
    total = sum_z(scale, ids, quarter, d1, d2, d3, e, t3)
    two = jnp.concatenate([total, row_send(total, dx=1)], axis=0)
    weight_grad, bias_grad = weight_out(ids, two, row_send(two, dc=1))

    r = r14[:4].astype(f32) + r2.astype(f32) + r3.astype(f32)
    out = t0 + r[:2] + row_send(r[2:], dc=1)
    return hidden, out.reshape(256, B), weight_grad, bias_grad[0]


def solution(mesh):
    in_specs = (
        P("row", "feat"),
        P("feat", None),
        P("feat"),
        P("row", None, None),
        P("row"),
        P("row"),
        P("row", "feat"),
    )
    out_specs = (P("row", "feat"), P("row", "feat"), P("feat", None), P("feat"))
    return jax.shard_map(body, mesh=mesh, in_specs=in_specs, out_specs=out_specs, check_vma=False)
```

```python
import functools

import jax
import jax.numpy as jnp
from jax import lax
from jax.experimental import pallas as pl
from jax.experimental.pallas import tpu as pltpu
from jax.sharding import PartitionSpec as P

bf16 = jnp.bfloat16
f32 = jnp.float32
B = 128
NZ = 8
VM = pl.BlockSpec(memory_space=pltpu.VMEM)
SM = pl.BlockSpec(memory_space=pltpu.SMEM)
HB = pl.BlockSpec(memory_space=pltpu.HBM)
ANY = pl.BlockSpec(memory_space=pl.ANY)


def row_send(v, dx=0, dz=0, dc=0):
    perm = []
    for i in range(32):
        x, z, c = i >> 4, (i >> 1) & 7, i & 1
        perm.append((i, ((x ^ dx) << 4) | (((z + dz) % NZ) << 1) | (c ^ dc)))
    return lax.ppermute(v, "row", perm)


def feat_send(v, dx=0, dy=0):
    return lax.ppermute(v, "feat", [(i, (((i >> 2) ^ dx) << 2) | ((i + dy) & 3)) for i in range(8)])


def params(mib=20):
    return pltpu.CompilerParams(vmem_limit_bytes=mib << 20)


def spin_send(v, k, way=1):
    perm = []
    for i in range(32):
        x, z, c = i >> 4, (i >> 1) & 7, i & 1
        perm.append((i, (x << 4) | (((z + way * (k if c == 0 else -k)) % NZ) << 1) | c))
    return lax.ppermute(v, "row", perm)


def tie(a, b):
    return lax.optimization_barrier((a, b))


def cost(flops, nbytes):
    return pl.CostEstimate(flops=flops, bytes_accessed=nbytes, transcendentals=0)


def pack_body(ids, w, og, bias, *refs):
    out, sem = refs[-2:]
    core = ids[0] & 1
    copies = []
    for m in range(4):
        at = pl.multiple_of(core * 512 + m * B, B)
        copies.append(
            pltpu.make_async_copy(w.at[:, pl.ds(at, B)], out.at[m * B : (m + 1) * B, :], sem.at[m])
        )
    copies.append(pltpu.make_async_copy(og, out.at[512:768, :], sem.at[4]))
    for c in copies:
        c.start()
    out[768:784, :] = jnp.broadcast_to(bias[...], (16, B))
    for c in copies:
        c.wait()


def pack_up(ids, w, og, bias, *ready):
    return pl.pallas_call(
        pack_body,
        out_shape=jax.ShapeDtypeStruct((784, B), bf16),
        in_specs=[SM, HB, HB, VM] + [ANY] * len(ready),
        out_specs=VM,
        scratch_shapes=[pltpu.SemaphoreType.DMA((5,))],
        compiler_params=params(60),
        cost_estimate=cost(0, 1 << 19),
        name="pack_up",
    )(ids, w, og, bias, *ready)


def append_body(a, b, *refs):
    out = refs[-1]
    rows = a.shape[0]
    out[0:rows, :] = a[...]
    out[rows:, :] = b[0 : out.shape[0] - rows, :]


def append(n, a, b, *ready):
    return pl.pallas_call(
        append_body,
        out_shape=jax.ShapeDtypeStruct((n, a.shape[1]), a.dtype),
        in_specs=[VM, VM] + [ANY] * len(ready),
        out_specs=VM,
        compiler_params=params(4),
        cost_estimate=cost(0, 1 << 18),
        name="append",
    )(a, b, *ready)


def turn_body(u, d, *refs):
    a, b = refs[-2:]
    a[...] = u[0:784, :]
    b[...] = d[784:1568, :]


def turn(u, d, *ready):
    half = jax.ShapeDtypeStruct((784, B), bf16)
    return pl.pallas_call(
        turn_body,
        out_shape=(half, half),
        in_specs=[VM, VM] + [ANY] * len(ready),
        out_specs=(VM, VM),
        compiler_params=params(4),
        cost_estimate=cost(0, 1 << 18),
        name="turn",
    )(u, d, *ready)


def hold_body(v, r0, r1, r2, out):
    out[...] = v[...]


def hold(v, *ready):
    return pl.pallas_call(
        hold_body,
        out_shape=jax.ShapeDtypeStruct(v.shape, v.dtype),
        in_specs=[VM, ANY, ANY, ANY],
        out_specs=VM,
        compiler_params=params(4),
        cost_estimate=cost(0, 1 << 18),
        name="hold",
    )(v, *ready)


def settle_body(mine, came, a, b, agg):
    agg[...] = (mine[...] + came[...]).astype(bf16)


def settle(mine, came, a, b):
    return pl.pallas_call(
        settle_body,
        out_shape=jax.ShapeDtypeStruct((2, B, B), bf16),
        in_specs=[VM, VM, ANY, ANY],
        out_specs=VM,
        compiler_params=params(4),
        cost_estimate=cost(0, 1 << 18),
        name="settle",
    )(mine, came, a, b)


def plan_body(ids, mine, theirs, out):
    me = ids[0]
    mx, mz, mc = me >> 4, (me >> 1) & 7, me & 1
    for side, ref in enumerate((mine, theirs)):
        base = 8 + 72 * side

        def step(i, n, ref=ref, base=base, side=side):
            b = ref[0, i]
            o = b >> 1
            dx, dz, dc = (o >> 4) ^ mx, ((o >> 1) - mz) & 7, (o & 1) ^ mc
            k = jnp.where(mc == 0, dz, NZ - dz)
            edge = (dz & 3) == 0
            held = jnp.where(edge, 1 - dc, jnp.where(k <= 3, 1, 0))
            j = jnp.where(edge, jnp.where(dz == 0, 7, 6), (3 - k) * 2 + dc)
            slot = dx * 16 + j * 2 + (b & 1)
            out[base + n] = i | (slot << 8) | ((ref[1, i] + 2 * side) << 16)
            return n + held

        n = lax.fori_loop(0, 64, step, 0, unroll=8)
        for u in range(4):
            out[base + n + u] = (32 << 8) | (4 << 16)
        out[side] = (n + 3) >> 2


def plan_tiles(ids, mine, theirs):
    return pl.pallas_call(
        plan_body,
        out_shape=jax.ShapeDtypeStruct((160,), jnp.int32),
        in_specs=[SM] * 3,
        out_specs=SM,
        compiler_params=params(4),
        cost_estimate=cost(10000, 4096),
        name="plan_tiles",
    )(ids, mine, theirs)


def each_tile(plan, tiles, more, use):
    for side, ref in enumerate((tiles, more)):
        def step(g, carry, side=side, ref=ref):
            for u in range(4):
                e = plan[8 + 72 * side + g * 4 + u]
                use(ref[e & 255], (e >> 8) & 255, e >> 16)
            return carry

        lax.fori_loop(0, plan[side], step, 0)


def agg_body(plan, tiles, more, *refs):
    mine, theirs, src, acc, sem = refs[10:]
    both, x0, o14, o2, o3, p14, p2, p3 = refs[0:8]
    copies = []

    def put(dx, j, v):
        n = v.shape[0]
        at = dx * 16 + j * 2
        copies.append(pltpu.make_async_copy(v, src.at[at : at + n], sem.at[len(copies)]))
        copies[-1].start()

    for dx, (v3, v2, v14, v0) in enumerate(((o3, o2, o14, both.at[0:2]), (p3, p2, p14, x0))):
        for j, v in ((0, v3), (2, v2), (4, v14), (7, v0)):
            put(dx, j, v)
    acc[...] = jnp.zeros_like(acc)
    src[32] = jnp.zeros((B, B), bf16)
    for c in copies:
        c.wait()

    def use(tile, slot, dest):
        acc[dest] += jnp.dot(tile, src[slot], preferred_element_type=f32)

    each_tile(plan, tiles, more, use)
    mine[...] = acc[0:2]
    theirs[...] = acc[2:4]


def aggregate(plan, tiles, more, pieces, *ready):
    parts = [v.reshape(-1, B, B) for v in pieces]
    return pl.pallas_call(
        agg_body,
        out_shape=(jax.ShapeDtypeStruct((2, B, B), f32), jax.ShapeDtypeStruct((2, B, B), f32)),
        in_specs=[SM, VM, VM] + [HB] * 8 + [ANY] * 2,
        out_specs=(VM, VM),
        scratch_shapes=[
            pltpu.VMEM((33, B, B), bf16),
            pltpu.VMEM((5, B, B), f32),
            pltpu.SemaphoreType.DMA((8,)),
        ],
        compiler_params=params(12),
        cost_estimate=cost(2 * 64 * B**3, 4 << 20),
        name="aggregate",
    )(plan, tiles, more, *parts, *ready)


def lay_body(ids, *refs):
    own = refs[0:5]
    w_out, og_out, bias_out, rows, sem = refs[6:11]
    yy, xx = ids[1] & 3, ids[1] >> 2
    copies, cols = [], []

    def put(src, dst):
        copies.append(pltpu.make_async_copy(src, dst, sem.at[len(copies)]))
        copies[-1].start()

    for j, off in enumerate((0, -1, 1, 2)):
        for i in range(2):
            k = j * 2 + i
            n, base = (j, i * 784) if j < 3 else (3 + i, 0)
            col = pl.multiple_of((((xx ^ i) << 2) | ((yy + off) & 3)) * B, B)
            cols.append(col)
            for m in range(4):
                put(own[n].at[pl.ds(base + m * B, B), :], w_out.at[pl.ds(k * B, B), pl.ds(m * B, B)])
            put(own[n].at[pl.ds(base + 512, 256), :], og_out.at[:, pl.ds(col, B)])
            put(own[n].at[pl.ds(base + 768, 16), :], rows.at[k])
    for c in copies:
        c.wait()
    for k in range(8):
        bias_out[:, pl.ds(cols[k], B)] = rows[k].astype(f32)[0:8]


def lay_out(ids, own, ready):
    return pl.pallas_call(
        lay_body,
        out_shape=(
            jax.ShapeDtypeStruct((1024, 512), bf16),
            jax.ShapeDtypeStruct((256, 1024), bf16),
            jax.ShapeDtypeStruct((8, 1024), f32),
        ),
        in_specs=[SM] + [HB] * 5 + [ANY],
        out_specs=(VM, VM, VM),
        scratch_shapes=[pltpu.VMEM((8, 16, B), bf16), pltpu.SemaphoreType.DMA((48,))],
        compiler_params=params(8),
        cost_estimate=cost(0, 3 << 20),
        name="lay_out",
    )(ids, *own, ready)


def mid_body(ids, p0, p1, p2, p3, w0, w1, og, bias, w_own, hidden, prop, keep, give, agg, pre, gp, wp):
    x, core = ids[0] >> 4, ids[0] & 1
    for j, p in enumerate((p0, p1, p2, p3)):
        for i in range(2):
            agg[:, (j * 2 + i) * B : (j * 2 + i + 1) * B] = p[i * 256 : (i + 1) * 256, :]
    for w, c in ((w0, core), (w1, 1 - core)):
        for m in range(2):
            cols = pl.ds(pl.multiple_of(c * 512 + m * 256, 256), 256)
            v = jnp.dot(agg[...], w[:, m * 256 : (m + 1) * 256], preferred_element_type=f32)
            v = v + bias[0:1, cols]
            pre[:, cols] = v
            s = jax.nn.sigmoid(v)
            gp[:, cols] = (og[:, cols].astype(f32) * s * (1.0 + v * (1.0 - s))).astype(bf16)
    mine = pl.ds(pl.multiple_of(ids[1] * B, B), B)
    v = pre[:, mine]
    hidden[...] = v * jax.nn.sigmoid(v)
    prop[...] = lax.dot_general(
        gp[...], w_own[...], (((1,), (1,)), ((), ())), preferred_element_type=f32
    ).astype(bf16)
    wp[:, 0:1024] = lax.dot_general(
        agg[:, 0:B], gp[...], (((0,), (0,)), ((), ())), preferred_element_type=f32
    )
    total = jnp.sum(gp[:, mine].astype(f32), axis=0, keepdims=True)
    wp[:, 1024:1152] = jnp.broadcast_to(total, (B, B))
    for ref, c in ((keep, core), (give, 1 - core)):
        for i in range(2):
            ref[i * 32 : (i + 1) * 32, :] = wp[pl.ds(pl.multiple_of(c * 64 + (x ^ i) * 32, 32), 32), :]


def middle(ids, pieces, w0, w1, og, bias, w_own):
    return pl.pallas_call(
        mid_body,
        out_shape=(
            jax.ShapeDtypeStruct((256, B), f32),
            jax.ShapeDtypeStruct((256, B), bf16),
            jax.ShapeDtypeStruct((64, 1152), f32),
            jax.ShapeDtypeStruct((64, 1152), f32),
        ),
        in_specs=[SM] + [VM] * 9,
        out_specs=(VM, VM, VM, VM),
        scratch_shapes=[
            pltpu.VMEM((256, 1024), bf16),
            pltpu.VMEM((256, 1024), f32),
            pltpu.VMEM((256, 1024), bf16),
            pltpu.VMEM((B, 1152), f32),
        ],
        compiler_params=params(),
        cost_estimate=cost(2 * 256 * 1024 * 1280, 5 << 20),
        name="middle",
    )(ids, *pieces, w0, w1, og, bias, w_own)


def spread_body(plan, tiles, more, prop, peer, send, near, far, acc, both):
    acc[...] = jnp.zeros_like(acc)
    both[0:2] = prop[...]
    both[2:4] = peer[...]
    both[4] = jnp.zeros((B, B), bf16)

    def use(tile, slot, dest):
        acc[slot] += lax.dot_general(
            tile, both[dest], (((0,), (0,)), ((), ())), preferred_element_type=f32
        )

    each_tile(plan, tiles, more, use)
    near[...] = acc[0:16]
    far[...] = acc[16:32].astype(bf16)


def spread(plan, tiles, more, prop, peer, send):
    return pl.pallas_call(
        spread_body,
        out_shape=(
            jax.ShapeDtypeStruct((16, B, B), f32),
            jax.ShapeDtypeStruct((16, B, B), bf16),
        ),
        in_specs=[SM] + [VM] * 4 + [ANY],
        out_specs=(VM, VM),
        scratch_shapes=[pltpu.VMEM((33, B, B), f32), pltpu.VMEM((5, B, B), bf16)],
        compiler_params=params(12),
        cost_estimate=cost(2 * 64 * B**3, 6 << 20),
        name="spread",
    )(plan, tiles, more, prop, peer, send)


def quarter_body(keep, got, came, far, out):
    out[...] = (keep[0:32, :] + got[0:32, :] + came[...].astype(f32)).astype(bf16)


def quarter_up(keep, got, came, far):
    return pl.pallas_call(
        quarter_body,
        out_shape=jax.ShapeDtypeStruct((32, 1152), bf16),
        in_specs=[VM] * 3 + [ANY],
        out_specs=VM,
        compiler_params=params(4),
        cost_estimate=cost(0, 1 << 18),
        name="quarter_up",
    )(keep, got, came, far)


def join_body(near, came, ready, t14, t2, t3, t0):
    t3[...] = near[0:4] + came[0:4].astype(f32)
    t2[...] = (near[4:8] + came[4:8].astype(f32)).astype(bf16)
    t14[...] = (near[8:14] + came[8:14].astype(f32)).astype(bf16)
    t0[...] = near[14:16] + came[14:16].astype(f32)


def join(near, came, ready):
    return pl.pallas_call(
        join_body,
        out_shape=(
            jax.ShapeDtypeStruct((6, B, B), bf16),
            jax.ShapeDtypeStruct((4, B, B), bf16),
            jax.ShapeDtypeStruct((4, B, B), f32),
            jax.ShapeDtypeStruct((2, B, B), f32),
        ),
        in_specs=[VM, VM, ANY],
        out_specs=(VM, VM, VM, VM),
        compiler_params=params(8),
        cost_estimate=cost(0, 2 << 20),
        name="join",
    )(near, came, ready)


def ride_body(t3, r14, out):
    out[0:2] = (t3[0:2] + r14[4:6].astype(f32)).astype(bf16)
    out[2:4] = t3[2:4].astype(bf16)


def ride(t3, r14):
    return pl.pallas_call(
        ride_body,
        out_shape=jax.ShapeDtypeStruct((4, B, B), bf16),
        in_specs=[VM, VM],
        out_specs=VM,
        compiler_params=params(4),
        cost_estimate=cost(0, 1 << 18),
        name="ride",
    )(t3, r14)


def rows_body(d1, d2, d3, t, out):
    for n, d in enumerate((d1, d2, d3)):
        out[32 * n : 32 * n + 32, :] = d[32:64, :]


def peer_rows(d1, d2, d3, t):
    return pl.pallas_call(
        rows_body,
        out_shape=jax.ShapeDtypeStruct((96, 1152), bf16),
        in_specs=[VM] * 3 + [ANY],
        out_specs=VM,
        compiler_params=params(4),
        cost_estimate=cost(0, 1 << 18),
        name="peer_rows",
    )(d1, d2, d3, t)


def sum_body(scale, ids, own, d1, d2, d3, e, t, out, buf):
    core, z = ids[0] & 1, (ids[0] >> 1) & 7
    buf[0] = own[...]
    buf[4] = d1[64:96, :]
    for k, d in ((1, d1), (2, d2), (3, d3)):
        mine = jnp.where(core == 0, k, NZ - k)
        buf[mine] = d[0:32, :]
        buf[NZ - mine] = e[(k - 1) * 32 : k * 32, :]
    acc = buf[(NZ - z) & 7].astype(f32)
    for n in range(1, NZ):
        acc = acc + buf[(n - z) & 7].astype(f32)
    out[...] = (acc * scale).astype(bf16)


def sum_z(scale, ids, *parts):
    return pl.pallas_call(
        functools.partial(sum_body, scale),
        out_shape=jax.ShapeDtypeStruct((32, 1152), bf16),
        in_specs=[SM] + [VM] * 5 + [ANY],
        out_specs=VM,
        scratch_shapes=[pltpu.VMEM((NZ, 32, 1152), bf16)],
        compiler_params=params(8),
        cost_estimate=cost(32 * 1152 * 8, 1 << 20),
        name="sum_z",
    )(ids, *parts)


def wout_body(ids, mine, theirs, w_out, b_out, buf):
    x, core = ids[0] >> 4, ids[0] & 1
    for ref, c in ((mine, core), (theirs, 1 - core)):
        for i in range(2):
            at = pl.multiple_of(c * 64 + (x ^ i) * 32, 32)
            buf[pl.ds(at, 32), :] = ref[i * 32 : (i + 1) * 32, :].astype(f32)
    w_out[...] = buf[:, 0:1024]
    b_out[...] = buf[0, 1024:1152]


def weight_out(ids, mine, theirs):
    return pl.pallas_call(
        wout_body,
        out_shape=(jax.ShapeDtypeStruct((B, 1024), f32), jax.ShapeDtypeStruct((B,), f32)),
        in_specs=[SM, VM, VM],
        out_specs=(VM, VM),
        scratch_shapes=[pltpu.VMEM((B, 1152), f32)],
        compiler_params=params(8),
        cost_estimate=cost(0, 1 << 20),
        name="weight_out",
    )(ids, mine, theirs)


def body(features, weight, bias_vector, adj_tiles, col_blocks, dest_blocks, out_grad):
    ids = jnp.stack([lax.axis_index("row"), lax.axis_index("feat")]).astype(jnp.int32)

    both = jnp.concatenate([features, row_send(features, dc=1)], axis=0)
    x0 = row_send(features, dx=1)
    listed = jnp.stack([col_blocks, dest_blocks])
    lists = row_send(listed, dc=1)
    swap, both_a = tie(adj_tiles, both)
    more = row_send(swap, dc=1)
    o3, o2 = spin_send(both, 3, -1), spin_send(both, 2, -1)
    plan = plan_tiles(ids, listed, lists)

    pack = pack_up(ids, weight, out_grad, bias_vector[None, :])
    pack_x = feat_send(pack, dx=1)

    ext = append(768, both, o3, lists)
    o14 = spin_send(ext, 1, -1)
    pair = append(1568, pack, pack_x, ext, o2, x0)
    p3, p2 = row_send(o3, dx=1), row_send(o2, dx=1)
    p14 = row_send(hold(o14, p3, p2, plan), dx=1)
    wu, wd = feat_send(pair, dy=1), feat_send(pair, dy=-1)

    wa, wb = turn(wu, wd, plan)
    mine, theirs = aggregate(plan, adj_tiles, more, (both_a, x0, o14, o2, o3, p14, p2, p3), wa, wb)
    wa, wb = feat_send(wa, dy=1), feat_send(wb, dy=-1)
    aggregated = settle(mine, row_send(theirs, dc=1), wa, wb).reshape(256, B)

    q = jnp.concatenate([aggregated, feat_send(aggregated, dx=1)], axis=0)
    w0, og, bias = lay_out(ids, (pair, wu, wd, wa, wb), q)
    pieces = (q, feat_send(q, dy=1), feat_send(q, dy=-1), feat_send(q, dy=2))
    hidden, prop, keep, give = middle(ids, pieces, w0, row_send(w0, dc=1), og, bias, weight)
    prop = prop.reshape(2, B, B)

    peer = row_send(prop, dc=1)
    got = row_send(give, dc=1)
    send = (keep[32:] + got[32:]).astype(bf16)
    got_x = row_send(send, dx=1)
    near, far = spread(plan, adj_tiles, more, prop, peer, send)
    came = row_send(far, dx=1)
    quarter = quarter_up(keep, got, got_x, far)
    halves = jnp.concatenate([quarter, row_send(quarter, dc=1)], axis=0)
    d3, d2 = spin_send(halves, 3, -1), spin_send(halves, 2, -1)
    d1 = spin_send(append(96, halves, d3, d2), 1, -1)

    t14, t2, t3, t0 = join(near, came, halves)
    r14, r2 = spin_send(t14, 1), spin_send(t2, 2)
    t3 = ride(t3, r14)
    r3 = spin_send(t3, 3)

    e = row_send(peer_rows(d1, d2, d3, r2), dc=1)
    scale = float(256 * lax.axis_size("row")) ** (-0.5)
    total = sum_z(scale, ids, quarter, d1, d2, d3, e, t3)
    two = jnp.concatenate([total, row_send(total, dx=1)], axis=0)
    weight_grad, bias_grad = weight_out(ids, two, row_send(two, dc=1))

    r = r14[:4].astype(f32) + r2.astype(f32) + r3.astype(f32)
    out = t0 + r[:2] + row_send(r[2:], dc=1)
    return hidden, out.reshape(256, B), weight_grad, bias_grad


def solution(mesh):
    in_specs = (
        P("row", "feat"),
        P("feat", None),
        P("feat"),
        P("row", None, None),
        P("row"),
        P("row"),
        P("row", "feat"),
    )
    out_specs = (P("row", "feat"), P("row", "feat"), P("feat", None), P("feat"))
    return jax.shard_map(body, mesh=mesh, in_specs=in_specs, out_specs=out_specs, check_vma=False)
```

```python
import functools

import jax
import jax.numpy as jnp
from jax import lax
from jax.experimental import pallas as pl
from jax.experimental.pallas import tpu as pltpu
from jax.sharding import PartitionSpec as P

bf16 = jnp.bfloat16
f32 = jnp.float32
B = 128
NZ = 8
VM = pl.BlockSpec(memory_space=pltpu.VMEM)
SM = pl.BlockSpec(memory_space=pltpu.SMEM)
HB = pl.BlockSpec(memory_space=pltpu.HBM)
ANY = pl.BlockSpec(memory_space=pl.ANY)


def row_send(v, dx=0, dz=0, dc=0):
    perm = []
    for i in range(32):
        x, z, c = i >> 4, (i >> 1) & 7, i & 1
        perm.append((i, ((x ^ dx) << 4) | (((z + dz) % NZ) << 1) | (c ^ dc)))
    return lax.ppermute(v, "row", perm)


def feat_send(v, dx=0, dy=0):
    return lax.ppermute(v, "feat", [(i, (((i >> 2) ^ dx) << 2) | ((i + dy) & 3)) for i in range(8)])


def params(mib=20):
    return pltpu.CompilerParams(vmem_limit_bytes=mib << 20)


def spin_send(v, k, way=1):
    perm = []
    for i in range(32):
        x, z, c = i >> 4, (i >> 1) & 7, i & 1
        perm.append((i, (x << 4) | (((z + way * (k if c == 0 else -k)) % NZ) << 1) | c))
    return lax.ppermute(v, "row", perm)


def tie(a, b):
    return lax.optimization_barrier((a, b))


def cost(flops, nbytes):
    return pl.CostEstimate(flops=flops, bytes_accessed=nbytes, transcendentals=0)


def pack_body(ids, w, og, bias, *refs):
    out, sem = refs[-2:]
    core = ids[0] & 1
    copies = []
    for m in range(4):
        at = pl.multiple_of(core * 512 + m * B, B)
        copies.append(
            pltpu.make_async_copy(w.at[:, pl.ds(at, B)], out.at[m * B : (m + 1) * B, :], sem.at[m])
        )
    copies.append(pltpu.make_async_copy(og, out.at[512:768, :], sem.at[4]))
    for c in copies:
        c.start()
    out[768:784, :] = jnp.broadcast_to(bias[...], (16, B))
    for c in copies:
        c.wait()


def pack_up(ids, w, og, bias, *ready):
    return pl.pallas_call(
        pack_body,
        out_shape=jax.ShapeDtypeStruct((784, B), bf16),
        in_specs=[SM, HB, HB, VM] + [ANY] * len(ready),
        out_specs=VM,
        scratch_shapes=[pltpu.SemaphoreType.DMA((5,))],
        compiler_params=params(60),
        cost_estimate=cost(0, 1 << 19),
        name="pack_up",
    )(ids, w, og, bias, *ready)


def append_body(a, b, *refs):
    out = refs[-1]
    rows = a.shape[0]
    out[0:rows, :] = a[...]
    out[rows:, :] = b[0 : out.shape[0] - rows, :]


def append(n, a, b, *ready):
    return pl.pallas_call(
        append_body,
        out_shape=jax.ShapeDtypeStruct((n, a.shape[1]), a.dtype),
        in_specs=[VM, VM] + [ANY] * len(ready),
        out_specs=VM,
        compiler_params=params(4),
        cost_estimate=cost(0, 1 << 18),
        name="append",
    )(a, b, *ready)


def turn_body(u, d, *refs):
    a, b = refs[-2:]
    a[...] = u[0:784, :]
    b[...] = d[784:1568, :]


def turn(u, d, *ready):
    half = jax.ShapeDtypeStruct((784, B), bf16)
    return pl.pallas_call(
        turn_body,
        out_shape=(half, half),
        in_specs=[VM, VM] + [ANY] * len(ready),
        out_specs=(VM, VM),
        compiler_params=params(4),
        cost_estimate=cost(0, 1 << 18),
        name="turn",
    )(u, d, *ready)


def hold_body(v, r0, r1, r2, out):
    out[...] = v[...]


def hold(v, *ready):
    return pl.pallas_call(
        hold_body,
        out_shape=jax.ShapeDtypeStruct(v.shape, v.dtype),
        in_specs=[VM, ANY, ANY, ANY],
        out_specs=VM,
        compiler_params=params(4),
        cost_estimate=cost(0, 1 << 18),
        name="hold",
    )(v, *ready)


def settle_body(mine, came, a, b, agg):
    agg[...] = (mine[...] + came[...]).astype(bf16)


def settle(mine, came, a, b):
    return pl.pallas_call(
        settle_body,
        out_shape=jax.ShapeDtypeStruct((2, B, B), bf16),
        in_specs=[VM, VM, ANY, ANY],
        out_specs=VM,
        compiler_params=params(4),
        cost_estimate=cost(0, 1 << 18),
        name="settle",
    )(mine, came, a, b)


def plan_body(ids, mine, theirs, out):
    me = ids[0]
    mx, mz, mc = me >> 4, (me >> 1) & 7, me & 1
    for side, ref in enumerate((mine, theirs)):
        base = 8 + 72 * side

        def step(i, n, ref=ref, base=base, side=side):
            b = ref[0, i]
            o = b >> 1
            dx, dz, dc = (o >> 4) ^ mx, ((o >> 1) - mz) & 7, (o & 1) ^ mc
            k = jnp.where(mc == 0, dz, NZ - dz)
            edge = (dz & 3) == 0
            held = jnp.where(edge, 1 - dc, jnp.where(k <= 3, 1, 0))
            j = jnp.where(edge, jnp.where(dz == 0, 7, 6), (3 - k) * 2 + dc)
            slot = dx * 16 + j * 2 + (b & 1)
            out[base + n] = i | (slot << 8) | ((ref[1, i] + 2 * side) << 16)
            return n + held

        n = lax.fori_loop(0, 64, step, 0, unroll=8)
        for u in range(4):
            out[base + n + u] = (32 << 8) | (4 << 16)
        out[side] = (n + 3) >> 2


def plan_tiles(ids, mine, theirs):
    return pl.pallas_call(
        plan_body,
        out_shape=jax.ShapeDtypeStruct((160,), jnp.int32),
        in_specs=[SM] * 3,
        out_specs=SM,
        compiler_params=params(4),
        cost_estimate=cost(10000, 4096),
        name="plan_tiles",
    )(ids, mine, theirs)


def each_tile(plan, tiles, more, use):
    for side, ref in enumerate((tiles, more)):
        def step(g, carry, side=side, ref=ref):
            for u in range(4):
                e = plan[8 + 72 * side + g * 4 + u]
                use(u, ref[e & 255], (e >> 8) & 255, e >> 16)
            return carry

        lax.fori_loop(0, plan[side], step, 0)


def agg_body(plan, tiles, more, *refs):
    mine, theirs, src, acc0, acc1, acc2, acc3, sem = refs[10:]
    accs = (acc0, acc1, acc2, acc3)
    both, x0, o14, o2, o3, p14, p2, p3 = refs[0:8]
    copies = []

    def put(dx, j, v):
        n = v.shape[0]
        at = dx * 16 + j * 2
        copies.append(pltpu.make_async_copy(v, src.at[at : at + n], sem.at[len(copies)]))
        copies[-1].start()

    for dx, (v3, v2, v14, v0) in enumerate(((o3, o2, o14, both.at[0:2]), (p3, p2, p14, x0))):
        for j, v in ((0, v3), (2, v2), (4, v14), (7, v0)):
            put(dx, j, v)
    for acc in accs:
        acc[...] = jnp.zeros_like(acc)
    src[32] = jnp.zeros((B, B), bf16)
    for c in copies:
        c.wait()

    def use(u, tile, slot, dest):
        accs[u][dest] += jnp.dot(tile, src[slot], preferred_element_type=f32)

    each_tile(plan, tiles, more, use)
    mine[...] = (acc0[0:2] + acc1[0:2]) + (acc2[0:2] + acc3[0:2])
    theirs[...] = (acc0[2:4] + acc1[2:4]) + (acc2[2:4] + acc3[2:4])


def aggregate(plan, tiles, more, pieces, *ready):
    parts = [v.reshape(-1, B, B) for v in pieces]
    return pl.pallas_call(
        agg_body,
        out_shape=(jax.ShapeDtypeStruct((2, B, B), f32), jax.ShapeDtypeStruct((2, B, B), f32)),
        in_specs=[SM, VM, VM] + [HB] * 8 + [ANY] * 2,
        out_specs=(VM, VM),
        scratch_shapes=[
            pltpu.VMEM((33, B, B), bf16),
            *[pltpu.VMEM((5, B, B), f32)] * 4,
            pltpu.SemaphoreType.DMA((8,)),
        ],
        compiler_params=params(12),
        cost_estimate=cost(2 * 64 * B**3, 4 << 20),
        name="aggregate",
    )(plan, tiles, more, *parts, *ready)


def lay_body(ids, *refs):
    own = refs[0:5]
    w_out, og_out, bias_out, rows, sem = refs[6:11]
    yy, xx = ids[1] & 3, ids[1] >> 2
    copies, cols = [], []

    def put(src, dst):
        copies.append(pltpu.make_async_copy(src, dst, sem.at[len(copies)]))
        copies[-1].start()

    for j, off in enumerate((0, -1, 1, 2)):
        for i in range(2):
            k = j * 2 + i
            n, base = (j, i * 784) if j < 3 else (3 + i, 0)
            col = pl.multiple_of((((xx ^ i) << 2) | ((yy + off) & 3)) * B, B)
            cols.append(col)
            for m in range(4):
                put(own[n].at[pl.ds(base + m * B, B), :], w_out.at[pl.ds(k * B, B), pl.ds(m * B, B)])
            put(own[n].at[pl.ds(base + 512, 256), :], og_out.at[:, pl.ds(col, B)])
            put(own[n].at[pl.ds(base + 768, 16), :], rows.at[k])
    for c in copies:
        c.wait()
    for k in range(8):
        bias_out[:, pl.ds(cols[k], B)] = rows[k].astype(f32)[0:8]


def lay_out(ids, own, ready):
    return pl.pallas_call(
        lay_body,
        out_shape=(
            jax.ShapeDtypeStruct((1024, 512), bf16),
            jax.ShapeDtypeStruct((256, 1024), bf16),
            jax.ShapeDtypeStruct((8, 1024), f32),
        ),
        in_specs=[SM] + [HB] * 5 + [ANY],
        out_specs=(VM, VM, VM),
        scratch_shapes=[pltpu.VMEM((8, 16, B), bf16), pltpu.SemaphoreType.DMA((48,))],
        compiler_params=params(8),
        cost_estimate=cost(0, 3 << 20),
        name="lay_out",
    )(ids, *own, ready)


def mid_body(ids, p0, p1, p2, p3, w0, w1, og, bias, w_own, hidden, prop, keep, give, agg, pre, gp, wp):
    x, core = ids[0] >> 4, ids[0] & 1
    for j, p in enumerate((p0, p1, p2, p3)):
        for i in range(2):
            agg[:, (j * 2 + i) * B : (j * 2 + i + 1) * B] = p[i * 256 : (i + 1) * 256, :]
    for w, c in ((w0, core), (w1, 1 - core)):
        for m in range(2):
            cols = pl.ds(pl.multiple_of(c * 512 + m * 256, 256), 256)
            v = jnp.dot(agg[...], w[:, m * 256 : (m + 1) * 256], preferred_element_type=f32)
            v = v + bias[0:1, cols]
            pre[:, cols] = v
            s = jax.nn.sigmoid(v)
            gp[:, cols] = (og[:, cols].astype(f32) * s * (1.0 + v * (1.0 - s))).astype(bf16)
    mine = pl.ds(pl.multiple_of(ids[1] * B, B), B)
    v = pre[:, mine]
    hidden[...] = v * jax.nn.sigmoid(v)
    prop[...] = lax.dot_general(
        gp[...], w_own[...], (((1,), (1,)), ((), ())), preferred_element_type=f32
    ).astype(bf16)
    wp[:, 0:1024] = lax.dot_general(
        agg[:, 0:B], gp[...], (((0,), (0,)), ((), ())), preferred_element_type=f32
    )
    total = jnp.sum(gp[:, mine].astype(f32), axis=0, keepdims=True)
    wp[:, 1024:1152] = jnp.broadcast_to(total, (B, B))
    for ref, c in ((keep, core), (give, 1 - core)):
        for i in range(2):
            ref[i * 32 : (i + 1) * 32, :] = wp[pl.ds(pl.multiple_of(c * 64 + (x ^ i) * 32, 32), 32), :]


def middle(ids, pieces, w0, w1, og, bias, w_own):
    return pl.pallas_call(
        mid_body,
        out_shape=(
            jax.ShapeDtypeStruct((256, B), f32),
            jax.ShapeDtypeStruct((256, B), bf16),
            jax.ShapeDtypeStruct((64, 1152), f32),
            jax.ShapeDtypeStruct((64, 1152), f32),
        ),
        in_specs=[SM] + [VM] * 9,
        out_specs=(VM, VM, VM, VM),
        scratch_shapes=[
            pltpu.VMEM((256, 1024), bf16),
            pltpu.VMEM((256, 1024), f32),
            pltpu.VMEM((256, 1024), bf16),
            pltpu.VMEM((B, 1152), f32),
        ],
        compiler_params=params(),
        cost_estimate=cost(2 * 256 * 1024 * 1280, 5 << 20),
        name="middle",
    )(ids, *pieces, w0, w1, og, bias, w_own)


def spread_body(plan, tiles, more, prop, peer, send, near, far, acc0, acc1, both):
    accs = (acc0, acc1)
    for acc in accs:
        acc[...] = jnp.zeros_like(acc)
    both[0:2] = prop[...]
    both[2:4] = peer[...]
    both[4] = jnp.zeros((B, B), bf16)

    def use(u, tile, slot, dest):
        accs[u & 1][slot] += lax.dot_general(
            tile, both[dest], (((0,), (0,)), ((), ())), preferred_element_type=f32
        )

    each_tile(plan, tiles, more, use)
    near[...] = acc0[0:16] + acc1[0:16]
    far[...] = (acc0[16:32] + acc1[16:32]).astype(bf16)


def spread(plan, tiles, more, prop, peer, send):
    return pl.pallas_call(
        spread_body,
        out_shape=(
            jax.ShapeDtypeStruct((16, B, B), f32),
            jax.ShapeDtypeStruct((16, B, B), bf16),
        ),
        in_specs=[SM] + [VM] * 4 + [ANY],
        out_specs=(VM, VM),
        scratch_shapes=[pltpu.VMEM((33, B, B), f32), pltpu.VMEM((33, B, B), f32), pltpu.VMEM((5, B, B), bf16)],
        compiler_params=params(14),
        cost_estimate=cost(2 * 64 * B**3, 6 << 20),
        name="spread",
    )(plan, tiles, more, prop, peer, send)


def quarter_body(keep, got, came, far, out):
    out[...] = (keep[0:32, :] + got[0:32, :] + came[...].astype(f32)).astype(bf16)


def quarter_up(keep, got, came, far):
    return pl.pallas_call(
        quarter_body,
        out_shape=jax.ShapeDtypeStruct((32, 1152), bf16),
        in_specs=[VM] * 3 + [ANY],
        out_specs=VM,
        compiler_params=params(4),
        cost_estimate=cost(0, 1 << 18),
        name="quarter_up",
    )(keep, got, came, far)


def join_body(near, came, ready, t14, t2, t3, t0):
    t3[...] = near[0:4] + came[0:4].astype(f32)
    t2[...] = (near[4:8] + came[4:8].astype(f32)).astype(bf16)
    t14[...] = (near[8:14] + came[8:14].astype(f32)).astype(bf16)
    t0[...] = near[14:16] + came[14:16].astype(f32)


def join(near, came, ready):
    return pl.pallas_call(
        join_body,
        out_shape=(
            jax.ShapeDtypeStruct((6, B, B), bf16),
            jax.ShapeDtypeStruct((4, B, B), bf16),
            jax.ShapeDtypeStruct((4, B, B), f32),
            jax.ShapeDtypeStruct((2, B, B), f32),
        ),
        in_specs=[VM, VM, ANY],
        out_specs=(VM, VM, VM, VM),
        compiler_params=params(8),
        cost_estimate=cost(0, 2 << 20),
        name="join",
    )(near, came, ready)


def ride_body(t3, r14, out):
    out[0:2] = (t3[0:2] + r14[4:6].astype(f32)).astype(bf16)
    out[2:4] = t3[2:4].astype(bf16)


def ride(t3, r14):
    return pl.pallas_call(
        ride_body,
        out_shape=jax.ShapeDtypeStruct((4, B, B), bf16),
        in_specs=[VM, VM],
        out_specs=VM,
        compiler_params=params(4),
        cost_estimate=cost(0, 1 << 18),
        name="ride",
    )(t3, r14)


def rows_body(d1, d2, d3, t, out):
    for n, d in enumerate((d1, d2, d3)):
        out[32 * n : 32 * n + 32, :] = d[32:64, :]


def peer_rows(d1, d2, d3, t):
    return pl.pallas_call(
        rows_body,
        out_shape=jax.ShapeDtypeStruct((96, 1152), bf16),
        in_specs=[VM] * 3 + [ANY],
        out_specs=VM,
        compiler_params=params(4),
        cost_estimate=cost(0, 1 << 18),
        name="peer_rows",
    )(d1, d2, d3, t)


def sum_body(scale, ids, own, d1, d2, d3, e, t, out, buf):
    core, z = ids[0] & 1, (ids[0] >> 1) & 7
    buf[0] = own[...]
    buf[4] = d1[64:96, :]
    for k, d in ((1, d1), (2, d2), (3, d3)):
        mine = jnp.where(core == 0, k, NZ - k)
        buf[mine] = d[0:32, :]
        buf[NZ - mine] = e[(k - 1) * 32 : k * 32, :]
    acc = buf[(NZ - z) & 7].astype(f32)
    for n in range(1, NZ):
        acc = acc + buf[(n - z) & 7].astype(f32)
    out[...] = (acc * scale).astype(bf16)


def sum_z(scale, ids, *parts):
    return pl.pallas_call(
        functools.partial(sum_body, scale),
        out_shape=jax.ShapeDtypeStruct((32, 1152), bf16),
        in_specs=[SM] + [VM] * 5 + [ANY],
        out_specs=VM,
        scratch_shapes=[pltpu.VMEM((NZ, 32, 1152), bf16)],
        compiler_params=params(8),
        cost_estimate=cost(32 * 1152 * 8, 1 << 20),
        name="sum_z",
    )(ids, *parts)


def wout_body(ids, mine, theirs, w_out, b_out, buf):
    x, core = ids[0] >> 4, ids[0] & 1
    for ref, c in ((mine, core), (theirs, 1 - core)):
        for i in range(2):
            at = pl.multiple_of(c * 64 + (x ^ i) * 32, 32)
            buf[pl.ds(at, 32), :] = ref[i * 32 : (i + 1) * 32, :].astype(f32)
    w_out[...] = buf[:, 0:1024]
    b_out[...] = buf[0, 1024:1152]


def weight_out(ids, mine, theirs):
    return pl.pallas_call(
        wout_body,
        out_shape=(jax.ShapeDtypeStruct((B, 1024), f32), jax.ShapeDtypeStruct((B,), f32)),
        in_specs=[SM, VM, VM],
        out_specs=(VM, VM),
        scratch_shapes=[pltpu.VMEM((B, 1152), f32)],
        compiler_params=params(8),
        cost_estimate=cost(0, 1 << 20),
        name="weight_out",
    )(ids, mine, theirs)


def body(features, weight, bias_vector, adj_tiles, col_blocks, dest_blocks, out_grad):
    ids = jnp.stack([lax.axis_index("row"), lax.axis_index("feat")]).astype(jnp.int32)

    both = jnp.concatenate([features, row_send(features, dc=1)], axis=0)
    x0 = row_send(features, dx=1)
    listed = jnp.stack([col_blocks, dest_blocks])
    lists = row_send(listed, dc=1)
    swap, both_a = tie(adj_tiles, both)
    more = row_send(swap, dc=1)
    o3, o2 = spin_send(both, 3, -1), spin_send(both, 2, -1)
    plan = plan_tiles(ids, listed, lists)

    pack = pack_up(ids, weight, out_grad, bias_vector[None, :])
    pack_x = feat_send(pack, dx=1)

    ext = append(768, both, o3, lists)
    o14 = spin_send(ext, 1, -1)
    pair = append(1568, pack, pack_x, ext, o2, x0)
    p3, p2 = row_send(o3, dx=1), row_send(o2, dx=1)
    p14 = row_send(hold(o14, p3, p2, plan), dx=1)
    wu, wd = feat_send(pair, dy=1), feat_send(pair, dy=-1)

    wa, wb = turn(wu, wd, plan)
    mine, theirs = aggregate(plan, adj_tiles, more, (both_a, x0, o14, o2, o3, p14, p2, p3), wa, wb)
    wa, wb = feat_send(wa, dy=1), feat_send(wb, dy=-1)
    aggregated = settle(mine, row_send(theirs, dc=1), wa, wb).reshape(256, B)

    q = jnp.concatenate([aggregated, feat_send(aggregated, dx=1)], axis=0)
    w0, og, bias = lay_out(ids, (pair, wu, wd, wa, wb), q)
    pieces = (q, feat_send(q, dy=1), feat_send(q, dy=-1), feat_send(q, dy=2))
    hidden, prop, keep, give = middle(ids, pieces, w0, row_send(w0, dc=1), og, bias, weight)
    prop = prop.reshape(2, B, B)

    peer = row_send(prop, dc=1)
    got = row_send(give, dc=1)
    send = (keep[32:] + got[32:]).astype(bf16)
    got_x = row_send(send, dx=1)
    near, far = spread(plan, adj_tiles, more, prop, peer, send)
    came = row_send(far, dx=1)
    quarter = quarter_up(keep, got, got_x, far)
    halves = jnp.concatenate([quarter, row_send(quarter, dc=1)], axis=0)
    d3, d2 = spin_send(halves, 3, -1), spin_send(halves, 2, -1)
    d1 = spin_send(append(96, halves, d3, d2), 1, -1)

    t14, t2, t3, t0 = join(near, came, halves)
    r14, r2 = spin_send(t14, 1), spin_send(t2, 2)
    t3 = ride(t3, r14)
    r3 = spin_send(t3, 3)

    e = row_send(peer_rows(d1, d2, d3, r2), dc=1)
    scale = float(256 * lax.axis_size("row")) ** (-0.5)
    total = sum_z(scale, ids, quarter, d1, d2, d3, e, t3)
    two = jnp.concatenate([total, row_send(total, dx=1)], axis=0)
    weight_grad, bias_grad = weight_out(ids, two, row_send(two, dc=1))

    r = r14[:4].astype(f32) + r2.astype(f32) + r3.astype(f32)
    out = t0 + r[:2] + row_send(r[2:], dc=1)
    return hidden, out.reshape(256, B), weight_grad, bias_grad


def solution(mesh):
    in_specs = (
        P("row", "feat"),
        P("feat", None),
        P("feat"),
        P("row", None, None),
        P("row"),
        P("row"),
        P("row", "feat"),
    )
    out_specs = (P("row", "feat"), P("row", "feat"), P("feat", None), P("feat"))
    return jax.shard_map(body, mesh=mesh, in_specs=in_specs, out_specs=out_specs, check_vma=False)
```

```python
import functools

import jax
import jax.numpy as jnp
from jax import lax
from jax.experimental import pallas as pl
from jax.experimental.pallas import tpu as pltpu
from jax.sharding import PartitionSpec as P

bf16 = jnp.bfloat16
f32 = jnp.float32
B = 128
NZ = 8
VM = pl.BlockSpec(memory_space=pltpu.VMEM)
SM = pl.BlockSpec(memory_space=pltpu.SMEM)
HB = pl.BlockSpec(memory_space=pltpu.HBM)
ANY = pl.BlockSpec(memory_space=pl.ANY)


def row_send(v, dx=0, dz=0, dc=0):
    perm = []
    for i in range(32):
        x, z, c = i >> 4, (i >> 1) & 7, i & 1
        perm.append((i, ((x ^ dx) << 4) | (((z + dz) % NZ) << 1) | (c ^ dc)))
    return lax.ppermute(v, "row", perm)


def feat_send(v, dx=0, dy=0):
    return lax.ppermute(v, "feat", [(i, (((i >> 2) ^ dx) << 2) | ((i + dy) & 3)) for i in range(8)])


def params(mib=20):
    return pltpu.CompilerParams(vmem_limit_bytes=mib << 20)


def spin_send(v, k, way=1):
    perm = []
    for i in range(32):
        x, z, c = i >> 4, (i >> 1) & 7, i & 1
        perm.append((i, (x << 4) | (((z + way * (k if c == 0 else -k)) % NZ) << 1) | c))
    return lax.ppermute(v, "row", perm)


def tie(a, b):
    return lax.optimization_barrier((a, b))


def cost(flops, nbytes):
    return pl.CostEstimate(flops=flops, bytes_accessed=nbytes, transcendentals=0)


def pack_body(ids, w, og, bias, *refs):
    out, sem = refs[-2:]
    core = ids[0] & 1
    copies = []
    for m in range(4):
        at = pl.multiple_of(core * 512 + m * B, B)
        copies.append(
            pltpu.make_async_copy(w.at[:, pl.ds(at, B)], out.at[m * B : (m + 1) * B, :], sem.at[m])
        )
    copies.append(pltpu.make_async_copy(og, out.at[512:768, :], sem.at[4]))
    for c in copies:
        c.start()
    out[768:784, :] = jnp.broadcast_to(bias[...], (16, B))
    for c in copies:
        c.wait()


def pack_up(ids, w, og, bias, *ready):
    return pl.pallas_call(
        pack_body,
        out_shape=jax.ShapeDtypeStruct((784, B), bf16),
        in_specs=[SM, HB, HB, VM] + [ANY] * len(ready),
        out_specs=VM,
        scratch_shapes=[pltpu.SemaphoreType.DMA((5,))],
        compiler_params=params(60),
        cost_estimate=cost(0, 1 << 19),
        name="pack_up",
    )(ids, w, og, bias, *ready)


def append_body(a, b, *refs):
    out = refs[-1]
    rows = a.shape[0]
    out[0:rows, :] = a[...]
    out[rows:, :] = b[0 : out.shape[0] - rows, :]


def append(n, a, b, *ready):
    return pl.pallas_call(
        append_body,
        out_shape=jax.ShapeDtypeStruct((n, a.shape[1]), a.dtype),
        in_specs=[VM, VM] + [ANY] * len(ready),
        out_specs=VM,
        compiler_params=params(4),
        cost_estimate=cost(0, 1 << 18),
        name="append",
    )(a, b, *ready)


def turn_body(u, d, *refs):
    a, b = refs[-2:]
    a[...] = u[0:784, :]
    b[...] = d[784:1568, :]


def turn(u, d, *ready):
    half = jax.ShapeDtypeStruct((784, B), bf16)
    return pl.pallas_call(
        turn_body,
        out_shape=(half, half),
        in_specs=[VM, VM] + [ANY] * len(ready),
        out_specs=(VM, VM),
        compiler_params=params(4),
        cost_estimate=cost(0, 1 << 18),
        name="turn",
    )(u, d, *ready)


def hold_body(v, r0, r1, r2, out):
    out[...] = v[...]


def hold(v, *ready):
    return pl.pallas_call(
        hold_body,
        out_shape=jax.ShapeDtypeStruct(v.shape, v.dtype),
        in_specs=[VM, ANY, ANY, ANY],
        out_specs=VM,
        compiler_params=params(4),
        cost_estimate=cost(0, 1 << 18),
        name="hold",
    )(v, *ready)


def settle_body(mine, came, a, b, agg):
    agg[...] = (mine[...] + came[...]).astype(bf16)


def settle(mine, came, a, b):
    return pl.pallas_call(
        settle_body,
        out_shape=jax.ShapeDtypeStruct((2, B, B), bf16),
        in_specs=[VM, VM, ANY, ANY],
        out_specs=VM,
        compiler_params=params(4),
        cost_estimate=cost(0, 1 << 18),
        name="settle",
    )(mine, came, a, b)


def plan_body(ids, mine, theirs, out):
    me = ids[0]
    mx, mz, mc = me >> 4, (me >> 1) & 7, me & 1
    for side, ref in enumerate((mine, theirs)):
        base = 8 + 72 * side

        def step(i, n, ref=ref, base=base, side=side):
            b = ref[0, i]
            o = b >> 1
            dx, dz, dc = (o >> 4) ^ mx, ((o >> 1) - mz) & 7, (o & 1) ^ mc
            k = jnp.where(mc == 0, dz, NZ - dz)
            edge = (dz & 3) == 0
            held = jnp.where(edge, 1 - dc, jnp.where(k <= 3, 1, 0))
            j = jnp.where(edge, jnp.where(dz == 0, 7, 6), (3 - k) * 2 + dc)
            slot = dx * 16 + j * 2 + (b & 1)
            out[base + n] = i | (slot << 8) | ((ref[1, i] + 2 * side) << 16)
            return n + held

        n = lax.fori_loop(0, 64, step, 0, unroll=8)
        for u in range(4):
            out[base + n + u] = (32 << 8) | (4 << 16)
        out[side] = (n + 3) >> 2


def plan_tiles(ids, mine, theirs):
    return pl.pallas_call(
        plan_body,
        out_shape=jax.ShapeDtypeStruct((160,), jnp.int32),
        in_specs=[SM] * 3,
        out_specs=SM,
        compiler_params=params(4),
        cost_estimate=cost(10000, 4096),
        name="plan_tiles",
    )(ids, mine, theirs)


def each_tile(plan, tiles, more, use):
    for side, ref in enumerate((tiles, more)):
        def step(g, carry, side=side, ref=ref):
            for u in range(4):
                e = plan[8 + 72 * side + g * 4 + u]
                use(u, ref[e & 255], (e >> 8) & 255, e >> 16)
            return carry

        lax.fori_loop(0, plan[side], step, 0)


def agg_body(plan, tiles, more, *refs):
    mine, theirs, src, acc0, acc1, acc2, acc3, sem = refs[10:]
    accs = (acc0, acc1, acc2, acc3)
    both, x0, o14, o2, o3, p14, p2, p3 = refs[0:8]
    copies = []

    def put(dx, j, v):
        n = v.shape[0]
        at = dx * 16 + j * 2
        copies.append(pltpu.make_async_copy(v, src.at[at : at + n], sem.at[len(copies)]))
        copies[-1].start()

    for dx, (v3, v2, v14, v0) in enumerate(((o3, o2, o14, both.at[0:2]), (p3, p2, p14, x0))):
        for j, v in ((0, v3), (2, v2), (4, v14), (7, v0)):
            put(dx, j, v)
    for acc in accs:
        acc[...] = jnp.zeros_like(acc)
    src[32] = jnp.zeros((B, B), bf16)
    for c in copies:
        c.wait()

    def use(u, tile, slot, dest):
        accs[u][dest] += jnp.dot(tile, src[slot], preferred_element_type=f32)

    each_tile(plan, tiles, more, use)
    mine[...] = (acc0[0:2] + acc1[0:2]) + (acc2[0:2] + acc3[0:2])
    theirs[...] = (acc0[2:4] + acc1[2:4]) + (acc2[2:4] + acc3[2:4])


def aggregate(plan, tiles, more, pieces, *ready):
    parts = [v.reshape(-1, B, B) for v in pieces]
    return pl.pallas_call(
        agg_body,
        out_shape=(jax.ShapeDtypeStruct((2, B, B), f32), jax.ShapeDtypeStruct((2, B, B), f32)),
        in_specs=[SM, VM, VM] + [HB] * 8 + [ANY] * 2,
        out_specs=(VM, VM),
        scratch_shapes=[
            pltpu.VMEM((33, B, B), bf16),
            *[pltpu.VMEM((5, B, B), f32)] * 4,
            pltpu.SemaphoreType.DMA((8,)),
        ],
        compiler_params=params(12),
        cost_estimate=cost(2 * 64 * B**3, 4 << 20),
        name="aggregate",
    )(plan, tiles, more, *parts, *ready)


def lay_body(ids, *refs):
    own = refs[0:5]
    w_out, og_out, bias_out, rows, sem = refs[6:11]
    yy, xx = ids[1] & 3, ids[1] >> 2
    copies, cols = [], []

    def put(src, dst):
        copies.append(pltpu.make_async_copy(src, dst, sem.at[len(copies)]))
        copies[-1].start()

    for j, off in enumerate((0, -1, 1, 2)):
        for i in range(2):
            k = j * 2 + i
            n, base = (j, i * 784) if j < 3 else (3 + i, 0)
            col = pl.multiple_of((((xx ^ i) << 2) | ((yy + off) & 3)) * B, B)
            cols.append(col)
            for m in range(4):
                put(own[n].at[pl.ds(base + m * B, B), :], w_out.at[pl.ds(k * B, B), pl.ds(m * B, B)])
            put(own[n].at[pl.ds(base + 512, 256), :], og_out.at[:, pl.ds(col, B)])
            put(own[n].at[pl.ds(base + 768, 16), :], rows.at[k])
    for c in copies:
        c.wait()
    for k in range(8):
        bias_out[:, pl.ds(cols[k], B)] = rows[k].astype(f32)[0:8]


def lay_out(ids, own, ready):
    return pl.pallas_call(
        lay_body,
        out_shape=(
            jax.ShapeDtypeStruct((1024, 512), bf16),
            jax.ShapeDtypeStruct((256, 1024), bf16),
            jax.ShapeDtypeStruct((8, 1024), f32),
        ),
        in_specs=[SM] + [HB] * 5 + [ANY],
        out_specs=(VM, VM, VM),
        scratch_shapes=[pltpu.VMEM((8, 16, B), bf16), pltpu.SemaphoreType.DMA((48,))],
        compiler_params=params(8),
        cost_estimate=cost(0, 3 << 20),
        name="lay_out",
    )(ids, *own, ready)


def mid_body(ids, p0, p1, p2, p3, w0, w1, og, bias, w_own, hidden, prop, keep, give, agg, pre, gp, wp):
    x, core = ids[0] >> 4, ids[0] & 1
    for j, p in enumerate((p0, p1, p2, p3)):
        for i in range(2):
            agg[:, (j * 2 + i) * B : (j * 2 + i + 1) * B] = p[i * 256 : (i + 1) * 256, :]
    for w, c in ((w0, core), (w1, 1 - core)):
        for m in range(2):
            cols = pl.ds(pl.multiple_of(c * 512 + m * 256, 256), 256)
            v = jnp.dot(agg[...], w[:, m * 256 : (m + 1) * 256], preferred_element_type=f32)
            v = v + bias[0:1, cols]
            pre[:, cols] = v
            s = jax.nn.sigmoid(v)
            gp[:, cols] = (og[:, cols].astype(f32) * s * (1.0 + v * (1.0 - s))).astype(bf16)
    mine = pl.ds(pl.multiple_of(ids[1] * B, B), B)
    v = pre[:, mine]
    hidden[...] = v * jax.nn.sigmoid(v)
    prop[...] = lax.dot_general(
        gp[...], w_own[...], (((1,), (1,)), ((), ())), preferred_element_type=f32
    ).astype(bf16)
    wp[:, 0:1024] = lax.dot_general(
        agg[:, 0:B], gp[...], (((0,), (0,)), ((), ())), preferred_element_type=f32
    )
    total = jnp.sum(gp[:, mine].astype(f32), axis=0, keepdims=True)
    wp[:, 1024:1152] = jnp.broadcast_to(total, (B, B))
    for ref, c in ((keep, core), (give, 1 - core)):
        for i in range(2):
            ref[i * 32 : (i + 1) * 32, :] = wp[pl.ds(pl.multiple_of(c * 64 + (x ^ i) * 32, 32), 32), :]


def middle(ids, pieces, w0, w1, og, bias, w_own):
    return pl.pallas_call(
        mid_body,
        out_shape=(
            jax.ShapeDtypeStruct((256, B), f32),
            jax.ShapeDtypeStruct((256, B), bf16),
            jax.ShapeDtypeStruct((64, 1152), f32),
            jax.ShapeDtypeStruct((64, 1152), f32),
        ),
        in_specs=[SM] + [VM] * 9,
        out_specs=(VM, VM, VM, VM),
        scratch_shapes=[
            pltpu.VMEM((256, 1024), bf16),
            pltpu.VMEM((256, 1024), f32),
            pltpu.VMEM((256, 1024), bf16),
            pltpu.VMEM((B, 1152), f32),
        ],
        compiler_params=params(),
        cost_estimate=cost(2 * 256 * 1024 * 1280, 5 << 20),
        name="middle",
    )(ids, *pieces, w0, w1, og, bias, w_own)


def spread_body(plan, tiles, more, prop, peer, send, near, far, acc0, acc1, both):
    accs = (acc0, acc1)
    for acc in accs:
        acc[...] = jnp.zeros_like(acc)
    both[0:2] = prop[...]
    both[2:4] = peer[...]
    both[4] = jnp.zeros((B, B), bf16)

    def use(u, tile, slot, dest):
        accs[u & 1][slot] += lax.dot_general(
            tile, both[dest], (((0,), (0,)), ((), ())), preferred_element_type=f32
        )

    each_tile(plan, tiles, more, use)
    near[...] = acc0[0:16] + acc1[0:16]
    far[...] = (acc0[16:32] + acc1[16:32]).astype(bf16)


def spread(plan, tiles, more, prop, peer, send):
    return pl.pallas_call(
        spread_body,
        out_shape=(
            jax.ShapeDtypeStruct((16, B, B), f32),
            jax.ShapeDtypeStruct((16, B, B), bf16),
        ),
        in_specs=[SM] + [VM] * 4 + [ANY],
        out_specs=(VM, VM),
        scratch_shapes=[pltpu.VMEM((33, B, B), f32), pltpu.VMEM((33, B, B), f32), pltpu.VMEM((5, B, B), bf16)],
        compiler_params=params(14),
        cost_estimate=cost(2 * 64 * B**3, 6 << 20),
        name="spread",
    )(plan, tiles, more, prop, peer, send)


def quarter_body(keep, got, came, far, out):
    out[...] = (keep[0:32, :] + got[0:32, :] + came[...].astype(f32)).astype(bf16)


def quarter_up(keep, got, came, far):
    return pl.pallas_call(
        quarter_body,
        out_shape=jax.ShapeDtypeStruct((32, 1152), bf16),
        in_specs=[VM] * 3 + [ANY],
        out_specs=VM,
        compiler_params=params(4),
        cost_estimate=cost(0, 1 << 18),
        name="quarter_up",
    )(keep, got, came, far)


def join_body(near, came, ready, t14, t2, t3, t0):
    t3[...] = near[0:4] + came[0:4].astype(f32)
    t2[...] = (near[4:8] + came[4:8].astype(f32)).astype(bf16)
    t14[...] = (near[8:14] + came[8:14].astype(f32)).astype(bf16)
    t0[...] = near[14:16] + came[14:16].astype(f32)


def join(near, came, ready):
    return pl.pallas_call(
        join_body,
        out_shape=(
            jax.ShapeDtypeStruct((6, B, B), bf16),
            jax.ShapeDtypeStruct((4, B, B), bf16),
            jax.ShapeDtypeStruct((4, B, B), f32),
            jax.ShapeDtypeStruct((2, B, B), f32),
        ),
        in_specs=[VM, VM, ANY],
        out_specs=(VM, VM, VM, VM),
        compiler_params=params(8),
        cost_estimate=cost(0, 2 << 20),
        name="join",
    )(near, came, ready)


def ride_body(t3, r14, t2, out, on):
    out[0:2] = (t3[0:2] + r14[4:6].astype(f32)).astype(bf16)
    out[2:4] = t3[2:4].astype(bf16)
    on[...] = t2[...]


def ride(t3, r14, t2):
    return pl.pallas_call(
        ride_body,
        out_shape=(jax.ShapeDtypeStruct((4, B, B), bf16),) * 2,
        in_specs=[VM, VM, VM],
        out_specs=(VM, VM),
        compiler_params=params(4),
        cost_estimate=cost(0, 1 << 18),
        name="ride",
    )(t3, r14, t2)


def rows_body(d1, d2, d3, t, out):
    for n, d in enumerate((d1, d2, d3)):
        out[32 * n : 32 * n + 32, :] = d[32:64, :]


def peer_rows(d1, d2, d3, t):
    return pl.pallas_call(
        rows_body,
        out_shape=jax.ShapeDtypeStruct((96, 1152), bf16),
        in_specs=[VM] * 3 + [ANY],
        out_specs=VM,
        compiler_params=params(4),
        cost_estimate=cost(0, 1 << 18),
        name="peer_rows",
    )(d1, d2, d3, t)


def sum_body(scale, ids, own, d1, d2, d3, e, t, out, buf):
    core, z = ids[0] & 1, (ids[0] >> 1) & 7
    buf[0] = own[...]
    buf[4] = d1[64:96, :]
    for k, d in ((1, d1), (2, d2), (3, d3)):
        mine = jnp.where(core == 0, k, NZ - k)
        buf[mine] = d[0:32, :]
        buf[NZ - mine] = e[(k - 1) * 32 : k * 32, :]
    acc = buf[(NZ - z) & 7].astype(f32)
    for n in range(1, NZ):
        acc = acc + buf[(n - z) & 7].astype(f32)
    out[...] = (acc * scale).astype(bf16)


def sum_z(scale, ids, *parts):
    return pl.pallas_call(
        functools.partial(sum_body, scale),
        out_shape=jax.ShapeDtypeStruct((32, 1152), bf16),
        in_specs=[SM] + [VM] * 5 + [ANY],
        out_specs=VM,
        scratch_shapes=[pltpu.VMEM((NZ, 32, 1152), bf16)],
        compiler_params=params(8),
        cost_estimate=cost(32 * 1152 * 8, 1 << 20),
        name="sum_z",
    )(ids, *parts)


def wout_body(ids, mine, theirs, w_out, b_out, buf):
    x, core = ids[0] >> 4, ids[0] & 1
    for ref, c in ((mine, core), (theirs, 1 - core)):
        for i in range(2):
            at = pl.multiple_of(c * 64 + (x ^ i) * 32, 32)
            buf[pl.ds(at, 32), :] = ref[i * 32 : (i + 1) * 32, :].astype(f32)
    w_out[...] = buf[:, 0:1024]
    b_out[...] = buf[0, 1024:1152]


def weight_out(ids, mine, theirs):
    return pl.pallas_call(
        wout_body,
        out_shape=(jax.ShapeDtypeStruct((B, 1024), f32), jax.ShapeDtypeStruct((B,), f32)),
        in_specs=[SM, VM, VM],
        out_specs=(VM, VM),
        scratch_shapes=[pltpu.VMEM((B, 1152), f32)],
        compiler_params=params(8),
        cost_estimate=cost(0, 1 << 20),
        name="weight_out",
    )(ids, mine, theirs)


def body(features, weight, bias_vector, adj_tiles, col_blocks, dest_blocks, out_grad):
    ids = jnp.stack([lax.axis_index("row"), lax.axis_index("feat")]).astype(jnp.int32)

    both = jnp.concatenate([features, row_send(features, dc=1)], axis=0)
    x0 = row_send(features, dx=1)
    listed = jnp.stack([col_blocks, dest_blocks])
    lists = row_send(listed, dc=1)
    swap, both_a = tie(adj_tiles, both)
    more = row_send(swap, dc=1)
    o3, o2 = spin_send(both, 3, -1), spin_send(both, 2, -1)
    plan = plan_tiles(ids, listed, lists)

    pack = pack_up(ids, weight, out_grad, bias_vector[None, :])
    pack_x = feat_send(pack, dx=1)

    ext = append(768, both, o3, lists)
    o14 = spin_send(ext, 1, -1)
    pair = append(1568, pack, pack_x, ext, o2, x0)
    p3, p2 = row_send(o3, dx=1), row_send(o2, dx=1)
    p14 = row_send(hold(o14, p3, p2, plan), dx=1)
    wu, wd = feat_send(pair, dy=1), feat_send(pair, dy=-1)

    wa, wb = turn(wu, wd, plan)
    mine, theirs = aggregate(plan, adj_tiles, more, (both_a, x0, o14, o2, o3, p14, p2, p3), wa, wb)
    wa, wb = feat_send(wa, dy=1), feat_send(wb, dy=-1)
    aggregated = settle(mine, row_send(theirs, dc=1), wa, wb).reshape(256, B)

    q = jnp.concatenate([aggregated, feat_send(aggregated, dx=1)], axis=0)
    w0, og, bias = lay_out(ids, (pair, wu, wd, wa, wb), q)
    pieces = (q, feat_send(q, dy=1), feat_send(q, dy=-1), feat_send(q, dy=2))
    hidden, prop, keep, give = middle(ids, pieces, w0, row_send(w0, dc=1), og, bias, weight)
    prop = prop.reshape(2, B, B)

    peer = row_send(prop, dc=1)
    got = row_send(give, dc=1)
    send = (keep[32:] + got[32:]).astype(bf16)
    got_x = row_send(send, dx=1)
    near, far = spread(plan, adj_tiles, more, prop, peer, send)
    came = row_send(far, dx=1)
    quarter = quarter_up(keep, got, got_x, far)
    halves = jnp.concatenate([quarter, row_send(quarter, dc=1)], axis=0)
    d3, d2 = spin_send(halves, 3, -1), spin_send(halves, 2, -1)
    d1 = spin_send(append(96, halves, d3, d2), 1, -1)

    t14, t2, t3, t0 = join(near, came, halves)
    r14 = spin_send(t14, 1)
    t3, t2 = ride(t3, r14, t2)
    r2, r3 = spin_send(t2, 2), spin_send(t3, 3)

    e = row_send(peer_rows(d1, d2, d3, r14), dc=1)
    scale = float(256 * lax.axis_size("row")) ** (-0.5)
    total = sum_z(scale, ids, quarter, d1, d2, d3, e, t3)
    two = jnp.concatenate([total, row_send(total, dx=1)], axis=0)
    weight_grad, bias_grad = weight_out(ids, two, row_send(two, dc=1))

    r = r14[:4].astype(f32) + r2.astype(f32) + r3.astype(f32)
    out = t0 + r[:2] + row_send(r[2:], dc=1)
    return hidden, out.reshape(256, B), weight_grad, bias_grad


def solution(mesh):
    in_specs = (
        P("row", "feat"),
        P("feat", None),
        P("feat"),
        P("row", None, None),
        P("row"),
        P("row"),
        P("row", "feat"),
    )
    out_specs = (P("row", "feat"), P("row", "feat"), P("feat", None), P("feat"))
    return jax.shard_map(body, mesh=mesh, in_specs=in_specs, out_specs=out_specs, check_vma=False)
```
